32 devices in a mesh: land: 4 (over z), rows: 8 (over y, x, core).
Axes of the slice: x: 2, y: 2, z: 4, core: 2. Of those that a mesh axis runs over, the one named last changes fastest.
Arguments:
- embeddings: bfloat16 [32768, 768], P(('land', 'rows')), may hold values from -8 to 8
- landmarks: bfloat16 [1024, 768], P('land'), may hold values from -8 to 8
Outputs:
- factor: float32 [1024, 1024], replicated
The draws below stay inside these ranges and needn't reach their ends.
All inputs are finite; a program needn't handle non-finite values.
Results may differ from the reference program's by a relative error of at most 0.0003.
Values may be sent and summed in bfloat16 or wider, within the bound.
No kernel may reach another device: no remote copies, remote signals or barrier semaphores. Data moves between devices by JAX's collectives and lax.ppermute only.
A program may use at most 64 MiB of HBM per device.

```python
import math
import jax
import jax.numpy as jnp
from jax import lax

E = 768
LANDMARKS = 1024
LAYERS = 6
ROWS_DEV = 1024
TOTAL_ROWS = 32768


def shared_parts(key):
    shared_key = jax.random.fold_in(key, 7001)
    mean_dir = jnp.clip(jax.random.normal(jax.random.fold_in(shared_key, 1), (E,), jnp.float32), -3.0, 3.0)
    flip_bits = jax.random.randint(jax.random.fold_in(shared_key, 2), (E,), 0, 2)
    sign_flip = flip_bits.astype(jnp.float32) * 2.0 - 1.0
    centers = jax.random.normal(jax.random.fold_in(shared_key, 3), (64, 16), jnp.float32)
    return (mean_dir, sign_flip, centers)


def draw_points(key, number, tag_value, low_scale, high_scale):
    mean_dir, sign_flip, centers = shared_parts(key)
    own_key = jax.random.fold_in(key, tag_value)
    groups = 16
    levels = jnp.arange(groups, dtype=jnp.float32)
    spectrum = 1.0 / jnp.sqrt(1.0 + levels / 2.0)
    labels = jax.random.randint(jax.random.fold_in(own_key, 1), (number,), 0, 64)
    chosen = jnp.take(centers, labels, axis=0)
    private = jax.random.normal(jax.random.fold_in(own_key, 2), (number, groups), jnp.float32)
    coefficients = 0.8 * chosen + 0.6 * private
    factor_part = jnp.tile(coefficients * spectrum, (1, E // groups)) * sign_flip
    log_scale = jax.random.uniform(jax.random.fold_in(own_key, 4), (number, 1), jnp.float32, math.log(low_scale), math.log(high_scale))
    row_scale = jnp.exp(log_scale)
    jitter = jax.random.normal(jax.random.fold_in(own_key, 3), (number, E), jnp.float32)
    strength = 0.3
    points = row_scale * (strength * mean_dir + 1.2 * factor_part + 0.35 * jitter)
    return jnp.clip(points, -8.0, 8.0)


def draw_embeddings(key, part):
    return draw_points(key, TOTAL_ROWS, 101, 0.15, 3.0).astype(jnp.bfloat16)


def draw_landmarks(key, part):
    return draw_points(key, LANDMARKS, 202, 0.6, 1.8).astype(jnp.bfloat16)


def setup_inputs(seed: int = 0) -> dict:
    streams_of = jax.random.split(jax.random.key(seed), 3)
    embeddings = draw_embeddings(jax.random.fold_in(streams_of[2], 71), 0)
    landmarks = draw_landmarks(jax.random.fold_in(streams_of[2], 71), 0)
    return {"embeddings": embeddings, "landmarks": landmarks}


SCALE_SQ = 1.0 / 32.0
RIDGE = 0.1

def squares_mean(points):
    wide = points.astype(jnp.float32)
    return lax.optimization_barrier(jnp.sum(wide * wide, axis=1, keepdims=True)) / points.shape[1] + 1e-06

def nngp_kernel(left, left_q, right, right_q):
    kernel = jnp.dot(left.astype(jnp.float32), right.T.astype(jnp.float32), preferred_element_type=jnp.float32) / left.shape[1]
    q_left = left_q
    q_right = right_q
    for layer in range(LAYERS):
        scale = jnp.sqrt(q_left * q_right)
        cosine = jnp.clip(kernel / scale, -1.0, 1.0)
        branch = scale / math.pi * (jnp.sqrt(jnp.maximum(1.0 - cosine * cosine, 0.0)) + (math.pi - jnp.arccos(cosine)) * cosine)
        kernel = kernel + SCALE_SQ * branch
        q_left = q_left * (1.0 + SCALE_SQ)
        q_right = q_right * (1.0 + SCALE_SQ)
    return kernel

def reference(embeddings, landmarks):
    land_q = squares_mean(landmarks)
    blocks = embeddings.reshape(TOTAL_ROWS // ROWS_DEV, ROWS_DEV, embeddings.shape[1])

    def add_block(total, block):
        cross = nngp_kernel(block, squares_mean(block), landmarks, land_q.T).astype(jnp.bfloat16)
        term = jnp.dot(cross.T.astype(jnp.float32), cross.astype(jnp.float32), preferred_element_type=jnp.float32) / TOTAL_ROWS
        return (total + term, None)
    start = jnp.zeros((LANDMARKS, LANDMARKS), jnp.float32)
    data_gram, unused = lax.scan(add_block, start, blocks)
    landmark_kernel = nngp_kernel(landmarks, land_q, landmarks, land_q.T)
    normal = data_gram + RIDGE * landmark_kernel
    return jnp.linalg.cholesky(normal).T
```

```python
import functools
import math

import jax
import jax.numpy as jnp
from jax import lax
from jax.experimental import pallas as pl
from jax.experimental.pallas import tpu as pltpu
from jax.sharding import PartitionSpec as P

LAYERS = 6
SCALE_SQ = 1.0 / 32.0
RIDGE = 0.1
EPS = 1e-06
HI = lax.Precision.HIGHEST
B = 128
W = 16
TINY = 1e-30

ARC = (0.9428362797873839, 0.04684592969277604, 0.008663018923508323, 1.324670644556325e-05, 0.0016412996811995852)
KEEP = 1.0 / (1.0 + SCALE_SQ)
ARC = tuple(c * SCALE_SQ * KEEP / math.pi for c in ARC)
GROWTH = (1.0 + SCALE_SQ) ** LAYERS


def recursion(c):
    for _ in range(LAYERS):
        w = jnp.maximum(1.0 - jnp.abs(c), TINY)
        t = (w * w) * lax.rsqrt(w)
        poly = ARC[4]
        for a in ARC[3::-1]:
            poly = poly * w + a
        c = jnp.maximum(c, KEEP * c) + t * poly
    return c


def squares(x):
    wide = x.astype(jnp.float32)
    wide = wide * wide
    hi = wide.astype(jnp.bfloat16)
    return hi, (wide - hi.astype(jnp.float32)).astype(jnp.bfloat16)


def nt(a, b):
    return lax.dot_general(a, b, (((1,), (1,)), ((), ())), preferred_element_type=jnp.float32)


def squares_mean_column(x):
    ones = jnp.ones((B, x.shape[1]), jnp.bfloat16)
    hi, lo = squares(x)
    return (nt(hi, ones) + nt(lo, ones)) / x.shape[1] + EPS


def squares_mean_row(x):
    ones = jnp.ones((8, x.shape[1]), jnp.bfloat16)
    hi, lo = squares(x)
    return (nt(ones, hi) + nt(ones, lo)) / x.shape[1] + EPS


def spread(column, lanes):
    return jnp.concatenate([column] * (lanes // B), axis=1)


def gram_kernel(all_points, chunk, pos_ref, emb_ref, marks_ref, own_ref, out_ref, k_ref, x_ref, vq_ref, ridge_ref):
    n, e = marks_ref.shape
    m = emb_ref.shape[0]
    share = own_ref.shape[0]
    uq = squares_mean_row(emb_ref[...])
    u_inv = lax.rsqrt(uq)
    u_root = uq * u_inv
    vq_ref[...] = squares_mean_column(marks_ref[...])

    def block(j, _):
        row = pl.multiple_of(j * B, B)
        k_ref[...] = nt(marks_ref[pl.ds(row, B), :], emb_ref[...])

        def part(i, _):
            r = pl.multiple_of(i * chunk, chunk)
            vq = vq_ref[pl.ds(row + r, chunk), :]
            v_inv = lax.rsqrt(vq)
            v_root = vq * v_inv
            up = jnp.concatenate([u_inv] * (chunk // 8), axis=0)
            ur = jnp.concatenate([u_root] * (chunk // 8), axis=0)
            c = k_ref[pl.ds(r, chunk), :] * up * spread(v_inv * (1.0 / e), m)
            c = recursion(c)
            x_ref[pl.ds(row + r, chunk), :] = (c * ur * spread(v_root * GROWTH, m)).astype(jnp.bfloat16)
            return 0

        lax.fori_loop(0, B // chunk, part, 0)
        return 0

    lax.fori_loop(0, n // B, block, 0)

    oq = squares_mean_column(own_ref[...])
    vr = squares_mean_row(marks_ref[...])
    o_inv, v_inv = lax.rsqrt(oq), lax.rsqrt(vr)
    k_own = nt(own_ref[...], marks_ref[...])
    for i in range(share // 8):
        oi = o_inv[8 * i : 8 * i + 8]
        c = recursion(k_own[8 * i : 8 * i + 8] * v_inv * spread(oi * (1.0 / e), n))
        root = oq[8 * i : 8 * i + 8] * oi
        ridge_ref[8 * i : 8 * i + 8, :] = c * (vr * v_inv) * spread(root * (RIDGE * GROWTH), n)

    pos = pos_ref[0]
    row_block = pos // B
    offset = pos % B
    for j in range(n // B):
        start = j * (j + 1) // 2 * B
        out_ref[start : start + (j + 1) * B, :] = nt(
            x_ref[: (j + 1) * B, :], x_ref[j * B : (j + 1) * B, :]
        ) * (1.0 / all_points)

        @pl.when(row_block <= j)
        def _():
            at = pl.ds(pl.multiple_of(start + row_block * B + offset, share), share)
            out_ref[at, :] = out_ref[at, :] + ridge_ref[:, j * B : (j + 1) * B]


def local_normal(position, embeddings, gathered, own, all_points):
    n = gathered.shape[0]
    nb = n // B
    vmem = pl.BlockSpec(memory_space=pltpu.VMEM)
    return pl.pallas_call(
        functools.partial(gram_kernel, all_points, 16),
        out_shape=jax.ShapeDtypeStruct((nb * (nb + 1) // 2 * B, B), jnp.float32),
        in_specs=[pl.BlockSpec(memory_space=pltpu.SMEM), vmem, vmem, vmem],
        out_specs=vmem,
        scratch_shapes=[
            pltpu.VMEM((B, embeddings.shape[0]), jnp.float32),
            pltpu.VMEM((n, embeddings.shape[0]), jnp.bfloat16),
            pltpu.VMEM((n, B), jnp.float32),
            pltpu.VMEM((own.shape[0], n), jnp.float32),
        ],
        compiler_params=pltpu.CompilerParams(vmem_limit_bytes=40 << 20),
        name="gram",
    )(position.reshape(1), embeddings, gathered, own)


def factor_block(d):
    rows8 = lax.broadcasted_iota(jnp.int32, (8, 128), 0)
    eye = (lax.broadcasted_iota(jnp.int32, (B, B), 0) == lax.broadcasted_iota(jnp.int32, (B, B), 1)).astype(jnp.float32)
    n = B // W
    g = W // 8
    left = [d[8 * i:8 * i + 8] for i in range(B // 8)]
    right = [eye[8 * i:8 * i + 8] for i in range(B // 8)]
    for p in range(n):
        base = p * g
        last = p == n - 1
        groups = list(range(base, base + (g if last else 2 * g)))
        col = [[None] * len(groups) for _ in range(W)]
        for i in range(W):
            for t, r in enumerate(groups):
                if t < g and t < i // 8:
                    continue
                lane = p * W + i
                col[i][t] = jnp.broadcast_to(left[r][:, lane:lane + 1], (8, 128))
        diag = [jnp.ones((8, 128), jnp.float32) for _ in range(g)]
        for j in range(W):
            tj, sj = j // 8, j % 8
            pivot = jnp.broadcast_to(col[j][tj][sj:sj + 1], (8, 128))
            diag[tj] = jnp.where(rows8 == sj, pivot, diag[tj])
            inv = 1.0 / pivot
            coefs = {}
            for i in range(j + 1, W):
                coefs[i] = jnp.broadcast_to(col[j][i // 8][i % 8:i % 8 + 1], (8, 128))
            scaled = [None] * len(groups)
            for t in range(len(groups)):
                if col[j][t] is None:
                    continue
                scaled[t] = col[j][t] * inv
            for i in range(j + 1, W):
                for t in range(len(groups)):
                    if col[i][t] is None:
                        continue
                    if i == j + 1:
                        col[i][t] = col[i][t] - (col[j][t] * coefs[i]) * inv
                    else:
                        col[i][t] = col[i][t] - scaled[t] * coefs[i]
            rl = jnp.broadcast_to(left[base + tj][sj:sj + 1], (8, 128))
            rr = jnp.broadcast_to(right[base + tj][sj:sj + 1], (8, 128))
            for t, r in enumerate(groups):
                if scaled[t] is None:
                    continue
                c = scaled[t]
                if t == tj:
                    if sj == 7:
                        continue
                    c = jnp.where(rows8 > sj, c, 0.0)
                left[r] = left[r] - c * rl
                right[r] = right[r] - c * rr
        for t in range(g):
            s = lax.rsqrt(diag[t])
            left[base + t] = left[base + t] * s
            right[base + t] = right[base + t] * s
        rest = (n - p - 2) * W
        if rest > 0:
            ul = jnp.concatenate(left[base:base + g], 0)
            ur = jnp.concatenate(right[base:base + g], 0)
            u = jnp.concatenate([ul, ur], 1)
            lo_row = (p + 2) * W
            upd = lax.dot_general(ul, u, (((0,), (0,)), ((), ())), preferred_element_type=jnp.float32, precision=HI)
            for r in range(lo_row // 8, B // 8):
                left[r] = left[r] - upd[8 * r:8 * r + 8, :128]
                right[r] = right[r] - upd[8 * r:8 * r + 8, 128:]
    u = jnp.concatenate(left, 0)
    w = jnp.concatenate(right, 0)
    tri = lax.broadcasted_iota(jnp.int32, (B, B), 0) <= lax.broadcasted_iota(jnp.int32, (B, B), 1)
    return jnp.where(tri, u, 0.0), w

def chol_kernel(a_ref, o_ref, s_ref, w_ref):
    n = o_ref.shape[0] // B
    o_ref[...] = jnp.zeros_like(o_ref)
    def step(k, _):
        for i in range(n):
            @pl.when(k == i)
            def _():
                blk = jnp.concatenate([a_ref[(j * (j + 1) // 2 + i) * B:(j * (j + 1) // 2 + i + 1) * B, :] for j in range(i, n)], 1)
                if i:
                    l = o_ref[:i * B, i * B:(i + 1) * B]
                    r = o_ref[:i * B, i * B:]
                    blk = blk - lax.dot_general(l, r, (((0,), (0,)), ((), ())), preferred_element_type=jnp.float32, precision=HI)
                s_ref[:, :(n - i) * B] = blk
        u, w = factor_block(s_ref[:, :B])
        s_ref[:, :B] = u
        w_ref[...] = w
        for i in range(n):
            @pl.when(k == i)
            def _():
                o_ref[i * B:(i + 1) * B, i * B:(i + 1) * B] = s_ref[:, :B]
                if i < n - 1:
                    o_ref[i * B:(i + 1) * B, (i + 1) * B:] = lax.dot_general(w_ref[...], s_ref[:, B:(n - i) * B], (((1,), (0,)), ((), ())), preferred_element_type=jnp.float32, precision=HI)
        return 0
    lax.fori_loop(0, n, step, 0)


def cholesky_upper(packed, n):
    vmem = pl.BlockSpec(memory_space=pltpu.VMEM)
    return pl.pallas_call(
        chol_kernel,
        out_shape=jax.ShapeDtypeStruct((n, n), jnp.float32),
        in_specs=[vmem],
        out_specs=vmem,
        scratch_shapes=[pltpu.VMEM((B, n), jnp.float32), pltpu.VMEM((B, B), jnp.float32)],
        compiler_params=pltpu.CompilerParams(vmem_limit_bytes=40 << 20),
        name="chol",
    )(packed)


def bits_of(axis):
    return range(lax.axis_size(axis).bit_length() - 1)


def swap(x, axis, bit):
    return lax.ppermute(x, axis, [(i, i ^ (1 << bit)) for i in range(lax.axis_size(axis))])


def my_bit(axis, bit):
    return (lax.axis_index(axis) >> bit) & 1


def all_reduce(x):
    stages = [(axis, bit) for axis in ("rows", "land") for bit in bits_of(axis)]
    for axis, bit in stages:
        half = x.shape[0] // 2
        mine = my_bit(axis, bit)
        send = lax.dynamic_slice_in_dim(x, (1 - mine) * half, half, 0)
        keep = lax.dynamic_slice_in_dim(x, mine * half, half, 0)
        x = keep + swap(send, axis, bit)
    for axis, bit in stages[::-1]:
        other = swap(x, axis, bit)
        first = my_bit(axis, bit) == 0
        x = jnp.concatenate([jnp.where(first, x, other), jnp.where(first, other, x)], 0)
    return x


def gather_marks(landmarks):
    rows = lax.axis_size("rows")
    share = landmarks.shape[0] // rows
    x = lax.dynamic_slice_in_dim(landmarks, lax.axis_index("rows") * share, share, 0)
    x = x.reshape(1, 1, share, landmarks.shape[1])
    for dim, axis in ((0, "land"), (1, "rows")):
        for bit in bits_of(axis) if axis == "land" else list(bits_of(axis)):
            other = swap(x, axis, bit)
            first = my_bit(axis, bit) == 0
            x = jnp.concatenate([jnp.where(first, x, other), jnp.where(first, other, x)], dim)
    return x.reshape(-1, landmarks.shape[1])


def shards(embeddings, landmarks):
    land, rows = lax.axis_size("land"), lax.axis_size("rows")
    n = landmarks.shape[0] * land
    share = n // (land * rows)
    position = (lax.axis_index("land") * rows + lax.axis_index("rows")) * share
    own = lax.dynamic_slice_in_dim(landmarks, lax.axis_index("rows") * share, share, 0)
    gathered = gather_marks(landmarks)
    packed = local_normal(position, embeddings, gathered, own, embeddings.shape[0] * land * rows)
    return cholesky_upper(all_reduce(packed), n)


def solution(mesh):
    in_specs = (P(("land", "rows"), None), P("land", None))
    return jax.shard_map(shards, mesh=mesh, in_specs=in_specs, out_specs=P(), check_vma=False)
```

```python
import functools
import math

import jax
import jax.numpy as jnp
from jax import lax
from jax.experimental import pallas as pl
from jax.experimental.pallas import tpu as pltpu
from jax.sharding import Mesh
from jax.sharding import PartitionSpec as P

LAYERS = 6
SCALE_SQ = 1.0 / 32.0
RIDGE = 0.1
EPS = 1e-06
HI = lax.Precision.HIGHEST
B = 128
W = 16
TINY = 1e-30

ARC = (0.9428362797873839, 0.04684592969277604, 0.008663018923508323, 1.324670644556325e-05, 0.0016412996811995852)
KEEP = 1.0 / (1.0 + SCALE_SQ)
ARC = tuple(c * SCALE_SQ * KEEP / math.pi for c in ARC)
GROWTH = (1.0 + SCALE_SQ) ** LAYERS


def recursion(c):
    for _ in range(LAYERS):
        w = jnp.maximum(1.0 - jnp.abs(c), TINY)
        t = (w * w) * lax.rsqrt(w)
        poly = ARC[4]
        for a in ARC[3::-1]:
            poly = poly * w + a
        c = jnp.maximum(c, KEEP * c) + t * poly
    return c


def squares(x):
    wide = x.astype(jnp.float32)
    wide = wide * wide
    hi = wide.astype(jnp.bfloat16)
    return hi, (wide - hi.astype(jnp.float32)).astype(jnp.bfloat16)


def nt(a, b):
    return lax.dot_general(a, b, (((1,), (1,)), ((), ())), preferred_element_type=jnp.float32)


def squares_mean_column(x):
    ones = jnp.ones((B, x.shape[1]), jnp.bfloat16)
    hi, lo = squares(x)
    return (nt(hi, ones) + nt(lo, ones)) / x.shape[1] + EPS


def squares_mean_row(x):
    ones = jnp.ones((8, x.shape[1]), jnp.bfloat16)
    hi, lo = squares(x)
    return (nt(ones, hi) + nt(ones, lo)) / x.shape[1] + EPS


def spread(column, lanes):
    return jnp.concatenate([column] * (lanes // B), axis=1)


def fill_cross(marks_ref, marks_row, rows, emb_ref, u_ref, k_ref, vq_ref, x_ref, x_row, chunk):
    e = emb_ref.shape[1]
    m = emb_ref.shape[0]

    def block(j, _):
        row = pl.multiple_of(marks_row + j * B, B)
        out = pl.multiple_of(x_row + j * B, B)
        tile = marks_ref[pl.ds(row, B), :]
        k_ref[...] = nt(tile, emb_ref[...])
        vq_ref[...] = squares_mean_column(tile)

        def part(i, _):
            r = pl.multiple_of(i * chunk, chunk)
            vq = vq_ref[pl.ds(r, chunk), :]
            v_inv = lax.rsqrt(vq)
            v_root = vq * v_inv
            up = jnp.concatenate([u_ref[:8, :]] * (chunk // 8), axis=0)
            ur = jnp.concatenate([u_ref[8:, :]] * (chunk // 8), axis=0)
            c = recursion(k_ref[pl.ds(r, chunk), :] * up * spread(v_inv * (1.0 / e), m))
            x_ref[pl.ds(out + r, chunk), :] = (c * ur * spread(v_root * GROWTH, m)).astype(jnp.bfloat16)
            return 0

        lax.fori_loop(0, B // chunk, part, 0)
        return 0

    lax.fori_loop(0, rows // B, block, 0)


def fill_u(emb_ref, u_ref):
    uq = squares_mean_row(emb_ref[...])
    inv = lax.rsqrt(uq)
    u_ref[:8, :] = inv
    u_ref[8:, :] = uq * inv


def own_kernel(marks_ref, emb_ref, x_ref, u_ref, k_ref, vq_ref):
    fill_u(emb_ref, u_ref)
    fill_cross(marks_ref, 0, marks_ref.shape[0], emb_ref, u_ref, k_ref, vq_ref, x_ref, 0, 16)


def own_cross(landmarks, embeddings):
    m = embeddings.shape[0]
    vmem = pl.BlockSpec(memory_space=pltpu.VMEM)
    return pl.pallas_call(
        own_kernel,
        out_shape=(
            jax.ShapeDtypeStruct((landmarks.shape[0], m), jnp.bfloat16),
            jax.ShapeDtypeStruct((16, m), jnp.float32),
        ),
        in_specs=[vmem, vmem],
        out_specs=(vmem, vmem),
        scratch_shapes=[pltpu.VMEM((B, m), jnp.float32), pltpu.VMEM((B, B), jnp.float32)],
        compiler_params=pltpu.CompilerParams(vmem_limit_bytes=24 << 20),
        cost_estimate=pl.CostEstimate(flops=10**10, transcendentals=10**7, bytes_accessed=10**7),
        name="own_cross",
    )(landmarks, embeddings)


def gram_kernel(plan, at_ref, emb_ref, mine_ref, own_ref, u_ref, x_mine_ref, *refs):
    lands, chips, cores, split, all_points, total_rows = plan
    count = (chips - 1 + 1) * (cores if split else 1)
    far = refs[:count]
    keep_ref, send_ref, marks_ref, x_ref, k_ref, vq_ref, ridge_ref, out_ref = refs[count:]
    shard, e = mine_ref.shape
    n = shard * lands
    m = emb_ref.shape[0]
    land, chip, core = at_ref[0], at_ref[1], at_ref[2]
    here = pl.multiple_of(land * shard, shard)
    marks_ref[pl.ds(here, shard), :] = mine_ref[...]
    x_ref[pl.ds(here, shard), :] = x_mine_ref[...]
    piece = far[0].shape[0] // (lands - 1)
    for a in range(cores if split else 1):
        for t in range(chips):
            slot = ((chip ^ t) * cores + (core ^ a)) if split else (chip ^ t)
            for s in range(1, lands):
                to = pl.multiple_of((land ^ s) * shard + slot * piece, piece)
                marks_ref[pl.ds(to, piece), :] = far[a * chips + t][(s - 1) * piece : s * piece, :]
    for s in range(1, lands):
        there = pl.multiple_of((land ^ s) * shard, shard)
        fill_cross(marks_ref, there, shard, emb_ref, u_ref, k_ref, vq_ref, x_ref, there, 16)

    share = own_ref.shape[0]
    oq = squares_mean_column(own_ref[...])
    vr = squares_mean_row(marks_ref[...])
    o_inv, v_inv = lax.rsqrt(oq), lax.rsqrt(vr)
    k_own = nt(own_ref[...], marks_ref[...])
    for i in range(share // 8):
        oi = o_inv[8 * i : 8 * i + 8]
        c = recursion(k_own[8 * i : 8 * i + 8] * v_inv * spread(oi * (1.0 / e), n))
        root = oq[8 * i : 8 * i + 8] * oi
        ridge_ref[8 * i : 8 * i + 8, :] = c * (vr * v_inv) * spread(root * (RIDGE * GROWTH), n)

    position = land * shard + (chip * cores + core) * share
    row_block = position // B
    offset = position % B
    for j in range(n // B):
        start = j * (j + 1) // 2 * B
        out_ref[start : start + (j + 1) * B, :] = nt(
            x_ref[: (j + 1) * B, :], x_ref[j * B : (j + 1) * B, :]
        ) * (1.0 / all_points)

        @pl.when(row_block <= j)
        def _():
            at = pl.ds(pl.multiple_of(start + row_block * B + offset, share), share)
            out_ref[at, :] = out_ref[at, :] + ridge_ref[:, j * B : (j + 1) * B]

    half = total_rows // cores
    keep_ref[...] = out_ref[pl.ds(pl.multiple_of(core * half, half), half), :]
    send_ref[...] = out_ref[pl.ds(pl.multiple_of((1 - core) * half, half), half), :]


def local_normal(at, plan, embeddings, landmarks, own, u, x_mine, far):
    lands, chips, cores, split, all_points, total_rows = plan
    n, m = landmarks.shape[0] * lands, embeddings.shape[0]
    half = jax.ShapeDtypeStruct((total_rows // cores, B), jnp.float32)
    vmem = pl.BlockSpec(memory_space=pltpu.VMEM)
    return pl.pallas_call(
        functools.partial(gram_kernel, plan),
        out_shape=(half, half),
        in_specs=[pl.BlockSpec(memory_space=pltpu.SMEM)] + [vmem] * (5 + len(far)),
        out_specs=(vmem, vmem),
        scratch_shapes=[
            pltpu.VMEM((n, landmarks.shape[1]), jnp.bfloat16),
            pltpu.VMEM((n, m), jnp.bfloat16),
            pltpu.VMEM((B, m), jnp.float32),
            pltpu.VMEM((B, B), jnp.float32),
            pltpu.VMEM((own.shape[0], n), jnp.float32),
            pltpu.VMEM((total_rows, B), jnp.float32),
        ],
        compiler_params=pltpu.CompilerParams(vmem_limit_bytes=40 << 20),
        name="gram",
    )(at, embeddings, landmarks, own, u, x_mine, *far)


def add_cut_kernel(ways, axis, at_ref, *refs):
    ins, outs = refs[: len(refs) - ways], refs[len(refs) - ways :]
    h = outs[0].shape[0]
    for s in range(ways):
        rows = pl.ds(pl.multiple_of((at_ref[axis] ^ s) * h, h), h) if ways > 1 else slice(None)
        total = ins[0][rows, :]
        for r in ins[1:]:
            total = total + r[rows, :]
        outs[s][...] = total


def add_cut(at, axis, ways, parts):
    h = parts[0].shape[0] // ways
    vmem = pl.BlockSpec(memory_space=pltpu.VMEM)
    return pl.pallas_call(
        functools.partial(add_cut_kernel, ways, axis),
        out_shape=tuple([jax.ShapeDtypeStruct((h, B), jnp.float32)] * ways),
        in_specs=[pl.BlockSpec(memory_space=pltpu.SMEM)] + [vmem] * len(parts),
        out_specs=tuple([vmem] * ways),
        name="add_cut",
    )(at, *parts)


def place_kernel(axis, at_ref, *refs):
    out = refs[-1]
    h = refs[0].shape[0]
    for s in range(len(refs) - 1):
        out[pl.ds(pl.multiple_of((at_ref[axis] ^ s) * h, h), h), :] = refs[s][...]


def place(at, axis, parts):
    vmem = pl.BlockSpec(memory_space=pltpu.VMEM)
    return pl.pallas_call(
        functools.partial(place_kernel, axis),
        out_shape=jax.ShapeDtypeStruct((parts[0].shape[0] * len(parts), B), jnp.float32),
        in_specs=[pl.BlockSpec(memory_space=pltpu.SMEM)] + [vmem] * len(parts),
        out_specs=vmem,
        name="place",
    )(at, *parts)


def factor_block(d):
    rows8 = lax.broadcasted_iota(jnp.int32, (8, 128), 0)
    eye = (lax.broadcasted_iota(jnp.int32, (B, B), 0) == lax.broadcasted_iota(jnp.int32, (B, B), 1)).astype(jnp.float32)
    n = B // W
    g = W // 8
    left = [d[8 * i:8 * i + 8] for i in range(B // 8)]
    right = [eye[8 * i:8 * i + 8] for i in range(B // 8)]
    for p in range(n):
        base = p * g
        last = p == n - 1
        groups = list(range(base, base + (g if last else 2 * g)))
        col = [[None] * len(groups) for _ in range(W)]
        for i in range(W):
            for t, r in enumerate(groups):
                if t < g and t < i // 8:
                    continue
                lane = p * W + i
                col[i][t] = jnp.broadcast_to(left[r][:, lane:lane + 1], (8, 128))
        diag = [jnp.ones((8, 128), jnp.float32) for _ in range(g)]
        for j in range(W):
            tj, sj = j // 8, j % 8
            pivot = jnp.broadcast_to(col[j][tj][sj:sj + 1], (8, 128))
            diag[tj] = jnp.where(rows8 == sj, pivot, diag[tj])
            inv = 1.0 / pivot
            coefs = {}
            for i in range(j + 1, W):
                coefs[i] = jnp.broadcast_to(col[j][i // 8][i % 8:i % 8 + 1], (8, 128))
            scaled = [None] * len(groups)
            for t in range(len(groups)):
                if col[j][t] is None:
                    continue
                scaled[t] = col[j][t] * inv
            for i in range(j + 1, W):
                for t in range(len(groups)):
                    if col[i][t] is None:
                        continue
                    if i == j + 1:
                        col[i][t] = col[i][t] - (col[j][t] * coefs[i]) * inv
                    else:
                        col[i][t] = col[i][t] - scaled[t] * coefs[i]
            rl = jnp.broadcast_to(left[base + tj][sj:sj + 1], (8, 128))
            rr = jnp.broadcast_to(right[base + tj][sj:sj + 1], (8, 128))
            for t, r in enumerate(groups):
                if scaled[t] is None:
                    continue
                c = scaled[t]
                if t == tj:
                    if sj == 7:
                        continue
                    c = jnp.where(rows8 > sj, c, 0.0)
                left[r] = left[r] - c * rl
                right[r] = right[r] - c * rr
        for t in range(g):
            s = lax.rsqrt(diag[t])
            left[base + t] = left[base + t] * s
            right[base + t] = right[base + t] * s
        rest = (n - p - 2) * W
        if rest > 0:
            ul = jnp.concatenate(left[base:base + g], 0)
            ur = jnp.concatenate(right[base:base + g], 0)
            u = jnp.concatenate([ul, ur], 1)
            lo_row = (p + 2) * W
            upd = lax.dot_general(ul, u, (((0,), (0,)), ((), ())), preferred_element_type=jnp.float32, precision=HI)
            for r in range(lo_row // 8, B // 8):
                left[r] = left[r] - upd[8 * r:8 * r + 8, :128]
                right[r] = right[r] - upd[8 * r:8 * r + 8, 128:]
    u = jnp.concatenate(left, 0)
    w = jnp.concatenate(right, 0)
    tri = lax.broadcasted_iota(jnp.int32, (B, B), 0) <= lax.broadcasted_iota(jnp.int32, (B, B), 1)
    return jnp.where(tri, u, 0.0), w

def chol_kernel(chips, cores, at_ref, *refs):
    parts = refs[: chips * cores]
    o_ref, a_ref, s_ref, w_ref = refs[chips * cores :]
    n = o_ref.shape[0] // B
    h = parts[0].shape[0]
    for a in range(cores):
        for t in range(chips):
            slot = (at_ref[2] ^ a) * chips + (at_ref[1] ^ t)
            a_ref[pl.ds(pl.multiple_of(slot * h, h), h), :] = parts[a * chips + t][...]
    o_ref[...] = jnp.zeros_like(o_ref)

    def step(k, _):
        for i in range(n):

            @pl.when(k == i)
            def _():
                starts = [(j * (j + 1) // 2 + i) * B for j in range(i, n)]
                blk = jnp.concatenate([a_ref[r : r + B, :] for r in starts], 1)
                if i:
                    left = o_ref[: i * B, i * B : (i + 1) * B]
                    right = o_ref[: i * B, i * B :]
                    blk = blk - lax.dot_general(
                        left, right, (((0,), (0,)), ((), ())), preferred_element_type=jnp.float32, precision=HI
                    )
                s_ref[:, : (n - i) * B] = blk

        u, w = factor_block(s_ref[:, :B])
        s_ref[:, :B] = u
        w_ref[...] = w
        for i in range(n):

            @pl.when(k == i)
            def _():
                o_ref[i * B : (i + 1) * B, i * B : (i + 1) * B] = s_ref[:, :B]
                if i < n - 1:
                    o_ref[i * B : (i + 1) * B, (i + 1) * B :] = lax.dot_general(
                        w_ref[...],
                        s_ref[:, B : (n - i) * B],
                        (((1,), (0,)), ((), ())),
                        preferred_element_type=jnp.float32,
                        precision=HI,
                    )

        return 0

    lax.fori_loop(0, n, step, 0)


def cholesky_upper(at, chips, cores, parts, n):
    vmem = pl.BlockSpec(memory_space=pltpu.VMEM)
    return pl.pallas_call(
        functools.partial(chol_kernel, chips, cores),
        out_shape=jax.ShapeDtypeStruct((n, n), jnp.float32),
        in_specs=[pl.BlockSpec(memory_space=pltpu.SMEM)] + [vmem] * len(parts),
        out_specs=vmem,
        scratch_shapes=[
            pltpu.VMEM((parts[0].shape[0] * len(parts), B), jnp.float32),
            pltpu.VMEM((B, n), jnp.float32),
            pltpu.VMEM((B, B), jnp.float32),
        ],
        compiler_params=pltpu.CompilerParams(vmem_limit_bytes=40 << 20),
        name="chol",
    )(at, *parts)


def swap(x, axis, s):
    return lax.ppermute(x, axis, [(i, i ^ s) for i in range(lax.axis_size(axis))])


def scatter(pieces, axis):
    return [pieces[0]] + [swap(p, axis, s) for s, p in enumerate(pieces) if s]


def spread_out(x, axis):
    return [x] + [swap(x, axis, s) for s in range(1, lax.axis_size(axis))]


def shards(embeddings, landmarks):
    lands, chips, cores = (lax.axis_size(a) for a in ("land", "chip", "core"))
    land, chip, core = (lax.axis_index(a) for a in ("land", "chip", "core"))
    at = jnp.stack([land, chip, core]).astype(jnp.int32)
    shard = landmarks.shape[0]
    n = shard * lands
    devices = lands * chips * cores
    blocks = n // B * (n // B + 1) // 2
    unit = 8 * devices
    total_rows = -(-blocks * B // unit) * unit
    split = shard // (chips * cores) % 16 == 0

    share = shard // (chips * cores)
    own = lax.dynamic_slice_in_dim(landmarks, (chip * cores + core) * share, share, 0)
    if split:
        piece = own
    else:
        piece = lax.dynamic_slice_in_dim(landmarks, chip * (shard // chips), shard // chips, 0)
    z = jnp.concatenate(spread_out(piece, "land")[1:], 0)
    far = spread_out(z, "chip")
    if split:
        for a in range(1, cores):
            far = far + [swap(f, "core", a) for f in far[:chips]]
    x_mine, u = own_cross(landmarks, embeddings)
    plan = (lands, chips, cores, split, embeddings.shape[0] * devices, total_rows)
    keep, send = local_normal(at, plan, embeddings, landmarks, own, u, x_mine, far)

    parts = scatter(add_cut(at, 1, chips, [keep, swap(send, "core", 1)]), "chip")
    parts = scatter(add_cut(at, 0, lands, parts), "land")
    (whole,) = add_cut(at, 0, 1, parts)
    whole = place(at, 0, spread_out(whole, "land"))
    parts = spread_out(whole, "chip")
    parts = parts + [swap(p, "core", 1) for p in parts]
    return cholesky_upper(at, chips, cores, parts, n)


def solution(mesh):
    land, rows = mesh.axis_names
    cores = 2
    fine = Mesh(mesh.devices.reshape(mesh.shape[land], mesh.shape[rows] // cores, cores), ("land", "chip", "core"))
    in_specs = (P(("land", "chip", "core"), None), P("land", None))
    return jax.shard_map(shards, mesh=fine, in_specs=in_specs, out_specs=P(), check_vma=False)
```

```python
import functools
import math

import jax
import jax.numpy as jnp
from jax import lax
from jax.experimental import pallas as pl
from jax.experimental.pallas import tpu as pltpu
from jax.sharding import Mesh
from jax.sharding import PartitionSpec as P

LAYERS = 6
SCALE_SQ = 1.0 / 32.0
RIDGE = 0.1
EPS = 1e-06
HI = lax.Precision.HIGHEST
B = 128
W = 16
TINY = 1e-30

ARC = (0.9428362797873839, 0.04684592969277604, 0.008663018923508323, 1.324670644556325e-05, 0.0016412996811995852)
KEEP = 1.0 / (1.0 + SCALE_SQ)
ARC = tuple(c * SCALE_SQ * KEEP / math.pi for c in ARC)
GROWTH = (1.0 + SCALE_SQ) ** LAYERS


def recursion(c):
    for _ in range(LAYERS):
        w = jnp.maximum(1.0 - jnp.abs(c), TINY)
        t = (w * w) * lax.rsqrt(w)
        poly = ARC[4]
        for a in ARC[3::-1]:
            poly = poly * w + a
        c = jnp.maximum(c, KEEP * c) + t * poly
    return c


def nt(a, b):
    return lax.dot_general(a, b, (((1,), (1,)), ((), ())), preferred_element_type=jnp.float32)


def lane_tiles_of_squares(x):
    total = None
    for l in range(0, x.shape[1], B):
        wide = x[:, l : l + B].astype(jnp.float32)
        total = wide * wide if total is None else total + wide * wide
    return total


def squares_mean_column(x):
    total = jnp.sum(lane_tiles_of_squares(x), axis=1, keepdims=True)
    return jnp.broadcast_to(total * (1.0 / x.shape[1]) + EPS, (x.shape[0], B))


def squares_mean_row(x):
    total = lane_tiles_of_squares(x)
    rows = [jnp.sum(total[i : i + B].T, axis=0, keepdims=True) for i in range(0, x.shape[0], B)]
    row = jnp.concatenate(rows, axis=1) * (1.0 / x.shape[1]) + EPS
    return jnp.broadcast_to(row, (8, x.shape[0]))


def spread(column, lanes):
    return jnp.concatenate([column] * (lanes // B), axis=1)


CHUNK = 16


def fill_cross(marks_ref, emb_ref, u_ref, k_ref, vq_ref, x_ref, x_row):
    m, e = emb_ref.shape
    k_ref[...] = nt(marks_ref[...], emb_ref[...])
    vq_ref[...] = squares_mean_column(marks_ref[...])

    def part(i, _):
        r = pl.multiple_of(i * CHUNK, CHUNK)
        vq = vq_ref[pl.ds(r, CHUNK), :]
        v_inv = lax.rsqrt(vq)
        v_root = vq * v_inv
        up = jnp.concatenate([u_ref[:8, :]] * (CHUNK // 8), axis=0)
        ur = jnp.concatenate([u_ref[8:, :]] * (CHUNK // 8), axis=0)
        c = recursion(k_ref[pl.ds(r, CHUNK), :] * up * spread(v_inv * (1.0 / e), m))
        x_ref[pl.ds(x_row(r), CHUNK), :] = (c * ur * spread(v_root * GROWTH, m)).astype(jnp.bfloat16)
        return 0

    lax.fori_loop(0, marks_ref.shape[0] // CHUNK, part, 0)


def own_kernel(marks_ref, emb_ref, x_ref, u_ref, k_ref, vq_ref):
    uq = squares_mean_row(emb_ref[...])
    inv = lax.rsqrt(uq)
    u_ref[:8, :] = inv
    u_ref[8:, :] = uq * inv
    fill_cross(marks_ref, emb_ref, u_ref, k_ref, vq_ref, x_ref, lambda r: r)


def own_cross(landmarks, embeddings):
    m = embeddings.shape[0]
    shard = landmarks.shape[0]
    vmem = pl.BlockSpec(memory_space=pltpu.VMEM)
    return pl.pallas_call(
        own_kernel,
        out_shape=(
            jax.ShapeDtypeStruct((shard, m), jnp.bfloat16),
            jax.ShapeDtypeStruct((16, m), jnp.float32),
        ),
        in_specs=[vmem, vmem],
        out_specs=(vmem, vmem),
        scratch_shapes=[pltpu.VMEM((shard, m), jnp.float32), pltpu.VMEM((shard, B), jnp.float32)],
        compiler_params=pltpu.CompilerParams(vmem_limit_bytes=12 << 20),
        name="own_cross",
    )(landmarks, embeddings)


def gram_kernel(plan, at_ref, emb_ref, mine_ref, own_ref, u_ref, x_mine_ref, *refs):
    lands, chips, cores, split, all_points, total_rows = plan
    count = chips * (cores if split else 1)
    far = refs[:count]
    keep_ref, send_ref, marks_ref, x_ref, k_ref, vq_ref, ridge_ref, out_ref = refs[count:]
    shard, e = mine_ref.shape
    n = shard * lands
    land, chip, core = at_ref[0], at_ref[1], at_ref[2]
    here = pl.multiple_of(land * shard, shard)
    x_ref[pl.ds(here, shard), :] = x_mine_ref[...]
    piece = far[0].shape[0] // (lands - 1)
    for a in range(cores if split else 1):
        for t in range(chips):
            slot = ((chip ^ t) * cores + (core ^ a)) if split else (chip ^ t)
            for s in range(1, lands):
                to = pl.multiple_of((s - 1) * shard + slot * piece, piece)
                marks_ref[pl.ds(to, piece), :] = far[a * chips + t][(s - 1) * piece : s * piece, :]

    def x_row(r):
        s = r // shard + 1
        return pl.multiple_of((land ^ s) * shard + r % shard, CHUNK)

    fill_cross(marks_ref, emb_ref, u_ref, k_ref, vq_ref, x_ref, x_row)

    share = own_ref.shape[0]
    oq = squares_mean_column(own_ref[...])
    o_inv = lax.rsqrt(oq)

    def ridge(marks, marks_q, to):
        k_own = nt(own_ref[...], marks)
        for l in range(0, shard, B):
            vq = marks_q[l : l + B].T[:8]
            v_inv = lax.rsqrt(vq)
            for i in range(share // 8):
                oi = o_inv[8 * i : 8 * i + 8]
                c = recursion(k_own[8 * i : 8 * i + 8, l : l + B] * v_inv * (oi * (1.0 / e)))
                root = oq[8 * i : 8 * i + 8] * oi
                ridge_ref[8 * i : 8 * i + 8, pl.ds(to + l, B)] = c * (vq * v_inv) * (root * (RIDGE * GROWTH))

    ridge(mine_ref[...], squares_mean_column(mine_ref[...]), here)
    for s in range(1, lands):
        rows = slice((s - 1) * shard, s * shard)
        ridge(marks_ref[rows, :], vq_ref[rows, :], pl.multiple_of((land ^ s) * shard, shard))

    position = land * shard + (chip * cores + core) * share
    row_block = position // B
    offset = position % B
    wide = 2 * B
    for w in range(n // wide):
        both = nt(x_ref[: (w + 1) * wide, :], x_ref[w * wide : (w + 1) * wide, :]) * (1.0 / all_points)
        for j in (2 * w, 2 * w + 1):
            start = j * (j + 1) // 2 * B
            out_ref[start : start + (j + 1) * B, :] = both[: (j + 1) * B, (j % 2) * B : (j % 2 + 1) * B]
    for j in range(n // B):
        start = j * (j + 1) // 2 * B

        @pl.when(row_block <= j)
        def _():
            at = pl.ds(pl.multiple_of(start + row_block * B + offset, share), share)
            out_ref[at, :] = out_ref[at, :] + ridge_ref[:, j * B : (j + 1) * B]

    half = total_rows // cores
    keep_ref[...] = out_ref[pl.ds(pl.multiple_of(core * half, half), half), :]
    send_ref[...] = out_ref[pl.ds(pl.multiple_of((1 - core) * half, half), half), :]


def local_normal(at, plan, embeddings, landmarks, own, u, x_mine, far):
    lands, chips, cores, split, all_points, total_rows = plan
    n, m = landmarks.shape[0] * lands, embeddings.shape[0]
    away = n - landmarks.shape[0]
    half = jax.ShapeDtypeStruct((total_rows // cores, B), jnp.float32)
    vmem = pl.BlockSpec(memory_space=pltpu.VMEM)
    return pl.pallas_call(
        functools.partial(gram_kernel, plan),
        out_shape=(half, half),
        in_specs=[pl.BlockSpec(memory_space=pltpu.SMEM)] + [vmem] * (5 + len(far)),
        out_specs=(vmem, vmem),
        scratch_shapes=[
            pltpu.VMEM((away, landmarks.shape[1]), jnp.bfloat16),
            pltpu.VMEM((n, m), jnp.bfloat16),
            pltpu.VMEM((away, m), jnp.float32),
            pltpu.VMEM((away, B), jnp.float32),
            pltpu.VMEM((own.shape[0], n), jnp.float32),
            pltpu.VMEM((total_rows, B), jnp.float32),
        ],
        compiler_params=pltpu.CompilerParams(vmem_limit_bytes=24 << 20),
        name="gram",
    )(at, embeddings, landmarks, own, u, x_mine, *far)


def add_cut_kernel(ways, axis, at_ref, *refs):
    ins, outs = refs[: len(refs) - ways], refs[len(refs) - ways :]
    h = outs[0].shape[0]
    for s in range(ways):
        rows = pl.ds(pl.multiple_of((at_ref[axis] ^ s) * h, h), h) if ways > 1 else slice(None)
        total = ins[0][rows, :]
        for r in ins[1:]:
            total = total + r[rows, :]
        outs[s][...] = total


def add_cut(at, axis, ways, parts):
    h = parts[0].shape[0] // ways
    vmem = pl.BlockSpec(memory_space=pltpu.VMEM)
    return pl.pallas_call(
        functools.partial(add_cut_kernel, ways, axis),
        out_shape=tuple([jax.ShapeDtypeStruct((h, B), jnp.float32)] * ways),
        in_specs=[pl.BlockSpec(memory_space=pltpu.SMEM)] + [vmem] * len(parts),
        out_specs=tuple([vmem] * ways),
        compiler_params=pltpu.CompilerParams(vmem_limit_bytes=8 << 20),
        name="add_cut",
    )(at, *parts)


def place_kernel(axis, at_ref, *refs):
    out = refs[-1]
    h = refs[0].shape[0]
    for s in range(len(refs) - 1):
        out[pl.ds(pl.multiple_of((at_ref[axis] ^ s) * h, h), h), :] = refs[s][...]


def place(at, axis, parts):
    vmem = pl.BlockSpec(memory_space=pltpu.VMEM)
    return pl.pallas_call(
        functools.partial(place_kernel, axis),
        out_shape=jax.ShapeDtypeStruct((parts[0].shape[0] * len(parts), B), jnp.float32),
        in_specs=[pl.BlockSpec(memory_space=pltpu.SMEM)] + [vmem] * len(parts),
        out_specs=vmem,
        compiler_params=pltpu.CompilerParams(vmem_limit_bytes=8 << 20),
        name="place",
    )(at, *parts)


def factor_block(d):
    rows8 = lax.broadcasted_iota(jnp.int32, (8, 128), 0)
    eye = (lax.broadcasted_iota(jnp.int32, (B, B), 0) == lax.broadcasted_iota(jnp.int32, (B, B), 1)).astype(jnp.float32)
    n = B // W
    g = W // 8
    left = [d[8 * i:8 * i + 8] for i in range(B // 8)]
    right = [eye[8 * i:8 * i + 8] for i in range(B // 8)]
    for p in range(n):
        base = p * g
        last = p == n - 1
        groups = list(range(base, base + (g if last else 2 * g)))
        col = [[None] * len(groups) for _ in range(W)]
        for i in range(W):
            for t, r in enumerate(groups):
                if t < g and t < i // 8:
                    continue
                lane = p * W + i
                col[i][t] = jnp.broadcast_to(left[r][:, lane:lane + 1], (8, 128))
        diag = [jnp.ones((8, 128), jnp.float32) for _ in range(g)]
        for j in range(W):
            tj, sj = j // 8, j % 8
            pivot = jnp.broadcast_to(col[j][tj][sj:sj + 1], (8, 128))
            diag[tj] = jnp.where(rows8 == sj, pivot, diag[tj])
            inv = 1.0 / pivot
            coefs = {}
            for i in range(j + 1, W):
                coefs[i] = jnp.broadcast_to(col[j][i // 8][i % 8:i % 8 + 1], (8, 128))
            scaled = [None] * len(groups)
            for t in range(len(groups)):
                if col[j][t] is None:
                    continue
                scaled[t] = col[j][t] * inv
            for i in range(j + 1, W):
                for t in range(len(groups)):
                    if col[i][t] is None:
                        continue
                    if i == j + 1:
                        col[i][t] = col[i][t] - (col[j][t] * coefs[i]) * inv
                    else:
                        col[i][t] = col[i][t] - scaled[t] * coefs[i]
            rl = jnp.broadcast_to(left[base + tj][sj:sj + 1], (8, 128))
            rr = jnp.broadcast_to(right[base + tj][sj:sj + 1], (8, 128))
            for t, r in enumerate(groups):
                if scaled[t] is None:
                    continue
                c = scaled[t]
                if t == tj:
                    if sj == 7:
                        continue
                    c = jnp.where(rows8 > sj, c, 0.0)
                left[r] = left[r] - c * rl
                right[r] = right[r] - c * rr
        for t in range(g):
            s = lax.rsqrt(diag[t])
            left[base + t] = left[base + t] * s
            right[base + t] = right[base + t] * s
        rest = (n - p - 2) * W
        if rest > 0:
            ul = jnp.concatenate(left[base:base + g], 0)
            ur = jnp.concatenate(right[base:base + g], 0)
            u = jnp.concatenate([ul, ur], 1)
            lo_row = (p + 2) * W
            upd = lax.dot_general(ul, u, (((0,), (0,)), ((), ())), preferred_element_type=jnp.float32, precision=HI)
            for r in range(lo_row // 8, B // 8):
                left[r] = left[r] - upd[8 * r:8 * r + 8, :128]
                right[r] = right[r] - upd[8 * r:8 * r + 8, 128:]
    u = jnp.concatenate(left, 0)
    w = jnp.concatenate(right, 0)
    tri = lax.broadcasted_iota(jnp.int32, (B, B), 0) <= lax.broadcasted_iota(jnp.int32, (B, B), 1)
    return jnp.where(tri, u, 0.0), w

def chol_kernel(chips, cores, at_ref, *refs):
    parts = refs[: chips * cores]
    o_ref, a_ref, s_ref, w_ref = refs[chips * cores :]
    n = o_ref.shape[0] // B
    h = parts[0].shape[0]
    for a in range(cores):
        for t in range(chips):
            slot = (at_ref[2] ^ a) * chips + (at_ref[1] ^ t)
            a_ref[pl.ds(pl.multiple_of(slot * h, h), h), :] = parts[a * chips + t][...]
    o_ref[...] = jnp.zeros_like(o_ref)

    def step(k, _):
        for i in range(n):

            @pl.when(k == i)
            def _():
                starts = [(j * (j + 1) // 2 + i) * B for j in range(i, n)]
                blk = jnp.concatenate([a_ref[r : r + B, :] for r in starts], 1)
                if i:
                    left = o_ref[: i * B, i * B : (i + 1) * B]
                    right = o_ref[: i * B, i * B :]
                    blk = blk - lax.dot_general(
                        left, right, (((0,), (0,)), ((), ())), preferred_element_type=jnp.float32, precision=HI
                    )
                s_ref[:, : (n - i) * B] = blk

        u, w = factor_block(s_ref[:, :B])
        s_ref[:, :B] = u
        w_ref[...] = w
        for i in range(n):

            @pl.when(k == i)
            def _():
                o_ref[i * B : (i + 1) * B, i * B : (i + 1) * B] = s_ref[:, :B]
                if i < n - 1:
                    o_ref[i * B : (i + 1) * B, (i + 1) * B :] = lax.dot_general(
                        w_ref[...],
                        s_ref[:, B : (n - i) * B],
                        (((1,), (0,)), ((), ())),
                        preferred_element_type=jnp.float32,
                        precision=HI,
                    )

        return 0

    lax.fori_loop(0, n, step, 0)


def cholesky_upper(at, chips, cores, parts, n):
    vmem = pl.BlockSpec(memory_space=pltpu.VMEM)
    return pl.pallas_call(
        functools.partial(chol_kernel, chips, cores),
        out_shape=jax.ShapeDtypeStruct((n, n), jnp.float32),
        in_specs=[pl.BlockSpec(memory_space=pltpu.SMEM)] + [vmem] * len(parts),
        out_specs=vmem,
        scratch_shapes=[
            pltpu.VMEM((parts[0].shape[0] * len(parts), B), jnp.float32),
            pltpu.VMEM((B, n), jnp.float32),
            pltpu.VMEM((B, B), jnp.float32),
        ],
        compiler_params=pltpu.CompilerParams(vmem_limit_bytes=24 << 20),
        name="chol",
    )(at, *parts)


def swap(x, axis, s):
    return lax.ppermute(x, axis, [(i, i ^ s) for i in range(lax.axis_size(axis))])


def scatter(pieces, axis):
    return [pieces[0]] + [swap(p, axis, s) for s, p in enumerate(pieces) if s]


def spread_out(x, axis):
    return [x] + [swap(x, axis, s) for s in range(1, lax.axis_size(axis))]


def shards(embeddings, landmarks):
    lands, chips, cores = (lax.axis_size(a) for a in ("land", "chip", "core"))
    land, chip, core = (lax.axis_index(a) for a in ("land", "chip", "core"))
    at = jnp.stack([land, chip, core]).astype(jnp.int32)
    shard = landmarks.shape[0]
    n = shard * lands
    devices = lands * chips * cores
    blocks = n // B * (n // B + 1) // 2
    unit = 8 * devices
    total_rows = -(-blocks * B // unit) * unit
    split = shard // (chips * cores) % 16 == 0

    share = shard // (chips * cores)
    own = lax.dynamic_slice_in_dim(landmarks, (chip * cores + core) * share, share, 0)
    if split:
        piece = own
    else:
        piece = lax.dynamic_slice_in_dim(landmarks, chip * (shard // chips), shard // chips, 0)
    z = jnp.concatenate(spread_out(piece, "land")[1:], 0)
    far = spread_out(z, "chip")
    x_mine, u = own_cross(landmarks, embeddings)
    if split:
        far, x_mine, u = lax.optimization_barrier((far, x_mine, u))
        for a in range(1, cores):
            far = far + [swap(f, "core", a) for f in far[:chips]]
    plan = (lands, chips, cores, split, embeddings.shape[0] * devices, total_rows)
    keep, send = local_normal(at, plan, embeddings, landmarks, own, u, x_mine, far)

    parts = scatter(add_cut(at, 1, chips, [keep, swap(send, "core", 1)]), "chip")
    parts = scatter(add_cut(at, 0, lands, parts), "land")
    (whole,) = add_cut(at, 0, 1, parts)
    whole = place(at, 0, spread_out(whole, "land"))
    parts = spread_out(whole, "chip")
    parts = parts + [swap(p, "core", 1) for p in parts]
    return cholesky_upper(at, chips, cores, parts, n)


def solution(mesh):
    land, rows = mesh.axis_names
    cores = 2
    fine = Mesh(mesh.devices.reshape(mesh.shape[land], mesh.shape[rows] // cores, cores), ("land", "chip", "core"))
    in_specs = (P(("land", "chip", "core"), None), P("land", None))
    return jax.shard_map(shards, mesh=fine, in_specs=in_specs, out_specs=P(), check_vma=False)
```

```python
import functools
import math
import typing

import jax
import jax.numpy as jnp
from jax import lax
from jax.experimental import pallas as pl
from jax.experimental.pallas import tpu as pltpu
from jax.sharding import Mesh
from jax.sharding import PartitionSpec as P

LAYERS = 6
SCALE_SQ = 1.0 / 32.0
RIDGE = 0.1
EPS = 1e-06
B = 128
W = 16
TINY = 1e-30

ARC = (0.9428362797873839, 0.04684592969277604, 0.008663018923508323, 1.324670644556325e-05, 0.0016412996811995852)
KEEP = 1.0 / (1.0 + SCALE_SQ)
ARC = tuple(c * SCALE_SQ * KEEP / math.pi for c in ARC)
GROWTH = (1.0 + SCALE_SQ) ** LAYERS


def recursion(c):
    for _ in range(LAYERS):
        w = jnp.maximum(1.0 - jnp.abs(c), TINY)
        t = (w * w) * lax.rsqrt(w)
        poly = ARC[4]
        for a in ARC[3::-1]:
            poly = poly * w + a
        c = jnp.maximum(c, KEEP * c) + t * poly
    return c


def nt(a, b):
    return lax.dot_general(a, b, (((1,), (1,)), ((), ())), preferred_element_type=jnp.float32)


def lane_tiles_of_squares(x):
    total = None
    for l in range(0, x.shape[1], B):
        wide = x[:, l : l + B].astype(jnp.float32)
        total = wide * wide if total is None else total + wide * wide
    return total


def squares_mean_column(x):
    total = jnp.sum(lane_tiles_of_squares(x), axis=1, keepdims=True)
    return jnp.broadcast_to(total * (1.0 / x.shape[1]) + EPS, (x.shape[0], B))


def squares_mean_row(x):
    total = lane_tiles_of_squares(x)
    rows = [jnp.sum(total[i : i + B].T, axis=0, keepdims=True) for i in range(0, x.shape[0], B)]
    row = jnp.concatenate(rows, axis=1) * (1.0 / x.shape[1]) + EPS
    return jnp.broadcast_to(row, (8, x.shape[0]))


def spread(column, lanes):
    return jnp.concatenate([column] * (lanes // B), axis=1)


CHUNK = 16


def fill_cross(marks_ref, emb_ref, u_ref, k_ref, vq_ref, x_ref, x_row):
    m, e = emb_ref.shape
    k_ref[...] = nt(marks_ref[...], emb_ref[...])
    vq_ref[...] = squares_mean_column(marks_ref[...])

    def part(i, _):
        r = pl.multiple_of(i * CHUNK, CHUNK)
        vq = vq_ref[pl.ds(r, CHUNK), :]
        v_inv = lax.rsqrt(vq)
        v_root = vq * v_inv
        up = jnp.concatenate([u_ref[:8, :]] * (CHUNK // 8), axis=0)
        ur = jnp.concatenate([u_ref[8:, :]] * (CHUNK // 8), axis=0)
        c = recursion(k_ref[pl.ds(r, CHUNK), :] * up * spread(v_inv * (1.0 / e), m))
        x_ref[pl.ds(x_row(r), CHUNK), :] = (c * ur * spread(v_root * GROWTH, m)).astype(jnp.bfloat16)
        return 0

    lax.fori_loop(0, marks_ref.shape[0] // CHUNK, part, 0)


def own_kernel(marks_ref, emb_ref, x_ref, u_ref, k_ref, vq_ref):
    uq = squares_mean_row(emb_ref[...])
    inv = lax.rsqrt(uq)
    u_ref[:8, :] = inv
    u_ref[8:, :] = uq * inv
    fill_cross(marks_ref, emb_ref, u_ref, k_ref, vq_ref, x_ref, lambda r: r)


def own_cross(landmarks, embeddings):
    m = embeddings.shape[0]
    shard = landmarks.shape[0]
    vmem = pl.BlockSpec(memory_space=pltpu.VMEM)
    return pl.pallas_call(
        own_kernel,
        out_shape=(
            jax.ShapeDtypeStruct((shard, m), jnp.bfloat16),
            jax.ShapeDtypeStruct((16, m), jnp.float32),
        ),
        in_specs=[vmem, vmem],
        out_specs=(vmem, vmem),
        scratch_shapes=[pltpu.VMEM((shard, m), jnp.float32), pltpu.VMEM((shard, B), jnp.float32)],
        compiler_params=pltpu.CompilerParams(vmem_limit_bytes=12 << 20),
        name="own_cross",
    )(landmarks, embeddings)


class Plan(typing.NamedTuple):
    lands: int
    chips: int
    cores: int
    split: bool
    all_points: int


def gram_kernel(plan, first, at_ref, emb_ref, mine_ref, own_ref, u_ref, x_mine_ref, *refs):
    lands, chips, cores, split, _ = plan
    count = chips * (cores if split else 1)
    far = refs[:count]
    keep_ref, send_ref, x_ref, ridge_ref, marks_ref, k_ref, vq_ref, out_ref = refs[count:]
    shard, e = mine_ref.shape
    n = shard * lands
    land, chip, core = at_ref[0], at_ref[1], at_ref[2]
    here = pl.multiple_of(land * shard, shard)
    x_ref[pl.ds(here, shard), :] = x_mine_ref[...]
    piece = far[0].shape[0] // (lands - 1)
    for a in range(cores if split else 1):
        for t in range(chips):
            slot = ((chip ^ t) * cores + (core ^ a)) if split else (chip ^ t)
            for s in range(1, lands):
                to = pl.multiple_of((s - 1) * shard + slot * piece, piece)
                marks_ref[pl.ds(to, piece), :] = far[a * chips + t][(s - 1) * piece : s * piece, :]

    def x_row(r):
        s = r // shard + 1
        return pl.multiple_of((land ^ s) * shard + r % shard, CHUNK)

    fill_cross(marks_ref, emb_ref, u_ref, k_ref, vq_ref, x_ref, x_row)

    share = own_ref.shape[0]
    oq = squares_mean_column(own_ref[...])
    o_inv = lax.rsqrt(oq)

    def ridge(marks, marks_q, to):
        k_own = nt(own_ref[...], marks)
        for l in range(0, shard, B):
            vq = marks_q[l : l + B].T[:8]
            v_inv = lax.rsqrt(vq)
            for i in range(share // 8):
                oi = o_inv[8 * i : 8 * i + 8]
                c = recursion(k_own[8 * i : 8 * i + 8, l : l + B] * v_inv * (oi * (1.0 / e)))
                root = oq[8 * i : 8 * i + 8] * oi
                ridge_ref[8 * i : 8 * i + 8, pl.ds(to + l, B)] = c * (vq * v_inv) * (root * (RIDGE * GROWTH))

    ridge(mine_ref[...], squares_mean_column(mine_ref[...]), here)
    for s in range(1, lands):
        rows = slice((s - 1) * shard, s * shard)
        ridge(marks_ref[rows, :], vq_ref[rows, :], pl.multiple_of((land ^ s) * shard, shard))

    gram_columns(plan, first, position_of(at_ref, plan, share, shard), x_ref, ridge_ref, out_ref, at_ref[2], keep_ref, send_ref)


def position_of(at_ref, plan, share, shard):
    return at_ref[0] * shard + (at_ref[1] * plan.cores + at_ref[2]) * share


def gram_columns(plan, span, position, x_ref, ridge_ref, out_ref, core, keep_ref, send_ref):
    share = ridge_ref.shape[0]
    row_block = position // B
    offset = position % B
    base = packed_start(span[0])
    wide = 2 * B
    for w in range(span[0] // 2, span[1] // 2):
        both = nt(x_ref[: (w + 1) * wide, :], x_ref[w * wide : (w + 1) * wide, :]) * (1.0 / plan.all_points)
        for j in (2 * w, 2 * w + 1):
            start = packed_start(j) - base
            out_ref[start : start + (j + 1) * B, :] = both[: (j + 1) * B, (j % 2) * B : (j % 2 + 1) * B]
    for j in range(*span):
        start = packed_start(j) - base

        @pl.when(row_block <= j)
        def _():
            at = pl.ds(pl.multiple_of(start + row_block * B + offset, share), share)
            out_ref[at, :] = out_ref[at, :] + ridge_ref[:, j * B : (j + 1) * B]

    half = keep_ref.shape[0]
    keep_ref[...] = out_ref[pl.ds(pl.multiple_of(core * half, half), half), :]
    send_ref[...] = out_ref[pl.ds(pl.multiple_of((1 - core) * half, half), half), :]


def last_kernel(plan, span, shard, at_ref, x_ref, ridge_ref, order_ref, keep_ref, send_ref, out_ref):
    position = position_of(at_ref, plan, ridge_ref.shape[0], shard)
    gram_columns(plan, span, position, x_ref, ridge_ref, out_ref, at_ref[2], keep_ref, send_ref)


def halves(plan, span):
    return (jax.ShapeDtypeStruct((packed_rows(plan, span) // plan.cores, B), jnp.float32),) * 2


def packed_start(j):
    return j * (j + 1) // 2 * B


def packed_rows(plan, span):
    unit = 8 * plan.lands * plan.chips * plan.cores
    return -(-(packed_start(span[1]) - packed_start(span[0])) // unit) * unit


def first_columns(at, plan, span, embeddings, landmarks, own, u, x_mine, far):
    n, m = landmarks.shape[0] * plan.lands, embeddings.shape[0]
    away = n - landmarks.shape[0]
    vmem = pl.BlockSpec(memory_space=pltpu.VMEM)
    return pl.pallas_call(
        functools.partial(gram_kernel, plan, span),
        out_shape=halves(plan, span)
        + (jax.ShapeDtypeStruct((n, m), jnp.bfloat16), jax.ShapeDtypeStruct((own.shape[0], n), jnp.float32)),
        in_specs=[pl.BlockSpec(memory_space=pltpu.SMEM)] + [vmem] * (5 + len(far)),
        out_specs=(vmem,) * 4,
        scratch_shapes=[
            pltpu.VMEM((away, landmarks.shape[1]), jnp.bfloat16),
            pltpu.VMEM((away, m), jnp.float32),
            pltpu.VMEM((away, B), jnp.float32),
            pltpu.VMEM((packed_rows(plan, span), B), jnp.float32),
        ],
        compiler_params=pltpu.CompilerParams(vmem_limit_bytes=24 << 20),
        name="gram_first",
    )(at, embeddings, landmarks, own, u, x_mine, *far)


def last_columns(at, plan, span, shard, x, ridge, order):
    vmem = pl.BlockSpec(memory_space=pltpu.VMEM)
    return pl.pallas_call(
        functools.partial(last_kernel, plan, span, shard),
        out_shape=halves(plan, span),
        in_specs=[pl.BlockSpec(memory_space=pltpu.SMEM), vmem, vmem, pl.BlockSpec(memory_space=pl.ANY)],
        out_specs=(vmem,) * 2,
        scratch_shapes=[pltpu.VMEM((packed_rows(plan, span), B), jnp.float32)],
        compiler_params=pltpu.CompilerParams(vmem_limit_bytes=16 << 20),
        name="gram_last",
    )(at, x, ridge, order)


def add_cut_kernel(ways, axis, at_ref, *refs):
    ins, outs = refs[: len(refs) - ways], refs[len(refs) - ways :]
    h = outs[0].shape[0]
    for s in range(ways):
        rows = pl.ds(pl.multiple_of((at_ref[axis] ^ s) * h, h), h) if ways > 1 else slice(None)
        total = ins[0][rows, :]
        for r in ins[1:]:
            total = total + r[rows, :]
        outs[s][...] = total


def add_cut(at, axis, ways, parts):
    h = parts[0].shape[0] // ways
    vmem = pl.BlockSpec(memory_space=pltpu.VMEM)
    return pl.pallas_call(
        functools.partial(add_cut_kernel, ways, axis),
        out_shape=tuple([jax.ShapeDtypeStruct((h, B), jnp.float32)] * ways),
        in_specs=[pl.BlockSpec(memory_space=pltpu.SMEM)] + [vmem] * len(parts),
        out_specs=tuple([vmem] * ways),
        compiler_params=pltpu.CompilerParams(vmem_limit_bytes=8 << 20),
        name="add_cut",
    )(at, *parts)


def place_kernel(axis, at_ref, *refs):
    out = refs[-1]
    h = refs[0].shape[0]
    for s in range(len(refs) - 1):
        out[pl.ds(pl.multiple_of((at_ref[axis] ^ s) * h, h), h), :] = refs[s][...]


def place(at, axis, parts):
    vmem = pl.BlockSpec(memory_space=pltpu.VMEM)
    return pl.pallas_call(
        functools.partial(place_kernel, axis),
        out_shape=jax.ShapeDtypeStruct((parts[0].shape[0] * len(parts), B), jnp.float32),
        in_specs=[pl.BlockSpec(memory_space=pltpu.SMEM)] + [vmem] * len(parts),
        out_specs=vmem,
        compiler_params=pltpu.CompilerParams(vmem_limit_bytes=8 << 20),
        name="place",
    )(at, *parts)


def thirds(x):
    h = x.astype(jnp.bfloat16)
    r = x - h.astype(jnp.float32)
    m = r.astype(jnp.bfloat16)
    return h, m, (r - m.astype(jnp.float32)).astype(jnp.bfloat16)

def left_terms(x, axis):
    h, m, l = thirds(x)
    return jnp.concatenate([h, h, h, m, m, l], axis)

def right_terms(x, axis):
    h, m, l = thirds(x)
    return jnp.concatenate([h, m, l, h, m, h], axis)

def dot32(a, b):
    return lax.dot_general(left_terms(a, 1), right_terms(b, 0), (((1,), (0,)), ((), ())), preferred_element_type=jnp.float32)

def dot32_t(a, b):
    return dot32(a.T, b)

def factor_block(d):
    rows8 = lax.broadcasted_iota(jnp.int32, (8, 128), 0)
    eye = (lax.broadcasted_iota(jnp.int32, (B, B), 0) == lax.broadcasted_iota(jnp.int32, (B, B), 1)).astype(jnp.float32)
    n = B // W
    g = W // 8
    left = [d[8 * i:8 * i + 8] for i in range(B // 8)]
    right = [eye[8 * i:8 * i + 8] for i in range(B // 8)]
    for p in range(n):
        base = p * g
        last = p == n - 1
        groups = list(range(base, base + (g if last else 2 * g)))
        col = [[None] * len(groups) for _ in range(W)]
        for i in range(W):
            for t, r in enumerate(groups):
                if t < g and t < i // 8:
                    continue
                lane = p * W + i
                col[i][t] = jnp.broadcast_to(left[r][:, lane:lane + 1], (8, 128))
        diag = [jnp.ones((8, 128), jnp.float32) for _ in range(g)]
        for j in range(W):
            tj, sj = j // 8, j % 8
            pivot = jnp.broadcast_to(col[j][tj][sj:sj + 1], (8, 128))
            diag[tj] = jnp.where(rows8 == sj, pivot, diag[tj])
            inv = 1.0 / pivot
            coefs = {}
            for i in range(j + 1, W):
                coefs[i] = jnp.broadcast_to(col[j][i // 8][i % 8:i % 8 + 1], (8, 128))
            scaled = [None] * len(groups)
            for t in range(len(groups)):
                if col[j][t] is None:
                    continue
                scaled[t] = col[j][t] * inv
            for i in range(j + 1, W):
                for t in range(len(groups)):
                    if col[i][t] is None:
                        continue
                    if i == j + 1:
                        col[i][t] = col[i][t] - (col[j][t] * coefs[i]) * inv
                    else:
                        col[i][t] = col[i][t] - scaled[t] * coefs[i]
            rl = jnp.broadcast_to(left[base + tj][sj:sj + 1], (8, 128))
            rr = jnp.broadcast_to(right[base + tj][sj:sj + 1], (8, 128))
            for t, r in enumerate(groups):
                if scaled[t] is None:
                    continue
                c = scaled[t]
                if t == tj:
                    if sj == 7:
                        continue
                    c = jnp.where(rows8 > sj, c, 0.0)
                left[r] = left[r] - c * rl
                right[r] = right[r] - c * rr
        for t in range(g):
            s = lax.rsqrt(diag[t])
            left[base + t] = left[base + t] * s
            right[base + t] = right[base + t] * s
        rest = (n - p - 2) * W
        if rest > 0:
            ul = jnp.concatenate(left[base:base + g], 0)
            ur = jnp.concatenate(right[base:base + g], 0)
            u = jnp.concatenate([ul, ur], 1)
            lo_row = (p + 2) * W
            upd = lax.dot_general(left_terms(ul, 0), right_terms(u, 0), (((0,), (0,)), ((), ())), preferred_element_type=jnp.float32)
            for r in range(lo_row // 8, B // 8):
                left[r] = left[r] - upd[8 * r:8 * r + 8, :128]
                right[r] = right[r] - upd[8 * r:8 * r + 8, 128:]
    u = jnp.concatenate(left, 0)
    w = jnp.concatenate(right, 0)
    tri = lax.broadcasted_iota(jnp.int32, (B, B), 0) <= lax.broadcasted_iota(jnp.int32, (B, B), 1)
    return jnp.where(tri, u, 0.0), w


def eliminate(nb, m_ref, d_ref, r_ref, store):
    lane_block = lax.broadcasted_iota(jnp.int32, (B, nb * B), 1) // B
    d_ref[...] = m_ref[:B, :B]
    r_ref[...] = jnp.zeros_like(r_ref)

    def step(k, _):
        u, w = factor_block(d_ref[...])
        prev = r_ref[...]
        m_ref[...] = m_ref[...] - dot32_t(prev, prev)
        row = dot32(w, m_ref[pl.ds(pl.multiple_of(k * B, B), B), :])
        row = jnp.where(lane_block > k, row, 0.0)
        r_ref[...] = row
        nxt = pl.multiple_of(jnp.minimum(k + 1, nb - 1) * B, B)
        rn = r_ref[:, pl.ds(nxt, B)]
        d_ref[...] = m_ref[pl.ds(nxt, B), pl.ds(nxt, B)] - dot32_t(rn, rn)
        store(pl.multiple_of(k * B, B), row, u, w)
        return 0

    lax.fori_loop(0, nb, step, 0)


def place_parts(plan, at_ref, parts, a_ref):
    h = parts[0].shape[0]
    for a in range(plan.cores):
        for t in range(plan.chips):
            slot = (at_ref[2] ^ a) * plan.chips + (at_ref[1] ^ t)
            a_ref[pl.ds(pl.multiple_of(slot * h, h), h), :] = parts[a * plan.chips + t][...]


def first_factor_kernel(plan, at_ref, *refs):
    count = plan.chips * plan.cores
    f_ref, w_ref, a_ref, m_ref, d_ref, r_ref = refs[count + 1 :]
    na = f_ref.shape[0] // B
    place_parts(plan, at_ref, refs[:count], a_ref)
    for j in range(na):
        m_ref[: (j + 1) * B, j * B : (j + 1) * B] = a_ref[packed_start(j) : packed_start(j) + (j + 1) * B, :]

    def store(at, row, u, w):
        f_ref[pl.ds(at, B), :] = row
        f_ref[pl.ds(at, B), pl.ds(at, B)] = u
        w_ref[pl.ds(at, B), :] = w

    eliminate(na, m_ref, d_ref, r_ref, store)


def first_factor(at, plan, na, parts, order):
    vmem = pl.BlockSpec(memory_space=pltpu.VMEM)
    return pl.pallas_call(
        functools.partial(first_factor_kernel, plan),
        out_shape=(
            jax.ShapeDtypeStruct((na * B, na * B), jnp.float32),
            jax.ShapeDtypeStruct((na * B, B), jnp.float32),
        ),
        in_specs=[pl.BlockSpec(memory_space=pltpu.SMEM)] + [vmem] * len(parts) + [pl.BlockSpec(memory_space=pl.ANY)],
        out_specs=(vmem,) * 2,
        scratch_shapes=[
            pltpu.VMEM((parts[0].shape[0] * len(parts), B), jnp.float32),
            pltpu.VMEM((na * B, na * B), jnp.float32),
            pltpu.VMEM((B, B), jnp.float32),
            pltpu.VMEM((B, na * B), jnp.float32),
        ],
        compiler_params=pltpu.CompilerParams(vmem_limit_bytes=16 << 20),
        name="chol_first",
    )(at, *parts, order)


def last_factor_kernel(plan, at_ref, f_ref, w_ref, *refs):
    count = plan.chips * plan.cores
    o_ref, a_ref, t_ref, m_ref, d_ref, r_ref = refs[count:]
    n, top = o_ref.shape[0] // B, f_ref.shape[0]
    na = top // B
    place_parts(plan, at_ref, refs[:count], a_ref)
    for j in range(na, n):
        start = packed_start(j) - packed_start(na)
        lanes = slice((j - na) * B, (j - na + 1) * B)
        t_ref[:, lanes] = a_ref[start : start + top, :]
        m_ref[: (j - na + 1) * B, lanes] = a_ref[start + top : start + (j + 1) * B, :]
    o_ref[:top, :top] = f_ref[...]
    o_ref[top:, :top] = jnp.zeros((n * B - top, top), jnp.float32)
    for k in range(na):
        rows = slice(k * B, (k + 1) * B)
        row = dot32(w_ref[rows, :], t_ref[rows, :])
        o_ref[rows, top:] = row
        if k < na - 1:
            t_ref[(k + 1) * B :, :] = t_ref[(k + 1) * B :, :] - dot32_t(f_ref[rows, (k + 1) * B :], row)
        m_ref[...] = m_ref[...] - dot32_t(row, row)

    def store(at, row, u, w):
        down = pl.multiple_of(top + at, B)
        o_ref[pl.ds(down, B), top:] = row
        o_ref[pl.ds(down, B), pl.ds(down, B)] = u

    eliminate(n - na, m_ref, d_ref, r_ref, store)


def last_factor(at, plan, n, f, w, parts):
    vmem = pl.BlockSpec(memory_space=pltpu.VMEM)
    top = f.shape[0]
    return pl.pallas_call(
        functools.partial(last_factor_kernel, plan),
        out_shape=jax.ShapeDtypeStruct((n, n), jnp.float32),
        in_specs=[pl.BlockSpec(memory_space=pltpu.SMEM)] + [vmem] * (2 + len(parts)),
        out_specs=vmem,
        scratch_shapes=[
            pltpu.VMEM((parts[0].shape[0] * len(parts), B), jnp.float32),
            pltpu.VMEM((top, n - top), jnp.float32),
            pltpu.VMEM((n - top, n - top), jnp.float32),
            pltpu.VMEM((B, B), jnp.float32),
            pltpu.VMEM((B, n - top), jnp.float32),
        ],
        compiler_params=pltpu.CompilerParams(vmem_limit_bytes=24 << 20),
        name="chol_last",
    )(at, f, w, *parts)


def swap(x, axis, s):
    return lax.ppermute(x, axis, [(i, i ^ s) for i in range(lax.axis_size(axis))])


def scatter(pieces, axis):
    return [pieces[0]] + [swap(p, axis, s) for s, p in enumerate(pieces) if s]


def spread_out(x, axis):
    return [x] + [swap(x, axis, s) for s in range(1, lax.axis_size(axis))]


def shards(embeddings, landmarks):
    lands, chips, cores = (lax.axis_size(a) for a in ("land", "chip", "core"))
    land, chip, core = (lax.axis_index(a) for a in ("land", "chip", "core"))
    at = jnp.stack([land, chip, core]).astype(jnp.int32)
    shard = landmarks.shape[0]
    n = shard * lands
    plan = Plan(lands, chips, cores, shard // (chips * cores) % 16 == 0, embeddings.shape[0] * lands * chips * cores)

    share = shard // (chips * cores)
    own = lax.dynamic_slice_in_dim(landmarks, (chip * cores + core) * share, share, 0)
    if plan.split:
        piece = own
    else:
        piece = lax.dynamic_slice_in_dim(landmarks, chip * (shard // chips), shard // chips, 0)
    z = jnp.concatenate(spread_out(piece, "land")[1:], 0)
    far = spread_out(z, "chip")
    x_mine, u = own_cross(landmarks, embeddings)
    if plan.split:
        far, x_mine, u = lax.optimization_barrier((far, x_mine, u))
        for a in range(1, cores):
            far = far + [swap(f, "core", a) for f in far[:chips]]

    na = n // B // 2
    first, last = (0, na), (na, n // B)
    keep, send, x, ridge = first_columns(at, plan, first, embeddings, landmarks, own, u, x_mine, far)
    cut_a = add_cut(at, 1, chips, [keep, swap(send, "core", 1)])
    keep, send = last_columns(at, plan, last, shard, x, ridge, cut_a[0])
    cut_b = add_cut(at, 1, chips, [keep, swap(send, "core", 1)])
    whole_a = land_reduce(at, lands, scatter(cut_a, "chip"))
    whole_b = land_reduce(at, lands, scatter(cut_b, "chip"))
    parts_a = spread_out(whole_a, "chip")
    parts_a = parts_a + [swap(p, "core", 1) for p in parts_a]
    f, w = first_factor(at, plan, na, parts_a, whole_b)
    parts_b, f, w = lax.optimization_barrier((spread_out(whole_b, "chip"), f, w))
    parts_b = parts_b + [swap(p, "core", 1) for p in parts_b]
    return last_factor(at, plan, n, f, w, parts_b)


def land_reduce(at, lands, parts):
    parts = scatter(add_cut(at, 0, lands, parts), "land")
    (whole,) = add_cut(at, 0, 1, parts)
    return place(at, 0, spread_out(whole, "land"))


def solution(mesh):
    land, rows = mesh.axis_names
    cores = 2
    fine = Mesh(mesh.devices.reshape(mesh.shape[land], mesh.shape[rows] // cores, cores), ("land", "chip", "core"))
    in_specs = (P(("land", "chip", "core"), None), P("land", None))
    return jax.shard_map(shards, mesh=fine, in_specs=in_specs, out_specs=P(), check_vma=False)
```

```python
import functools
import math
import typing

import jax
import jax.numpy as jnp
from jax import lax
from jax.experimental import pallas as pl
from jax.experimental.pallas import tpu as pltpu
from jax.sharding import Mesh
from jax.sharding import PartitionSpec as P

LAYERS = 6
SCALE_SQ = 1.0 / 32.0
RIDGE = 0.1
EPS = 1e-06
B = 128
W = 16
TINY = 1e-30

ARC = (0.9426497266634519, 0.04833294295062493, 0.004716300148249888, 0.004298816276929029)
KEEP = 1.0 / (1.0 + SCALE_SQ)
ARC = tuple(c * SCALE_SQ * KEEP / math.pi for c in ARC)
GROWTH = (1.0 + SCALE_SQ) ** LAYERS


def recursion(c):
    for _ in range(LAYERS):
        w = jnp.maximum(1.0 - jnp.abs(c), TINY)
        t = (w * w) * lax.rsqrt(w)
        poly = ARC[3]
        for a in ARC[2::-1]:
            poly = poly * w + a
        c = jnp.maximum(c, KEEP * c) + t * poly
    return c


def nt(a, b):
    return lax.dot_general(a, b, (((1,), (1,)), ((), ())), preferred_element_type=jnp.float32)


def lane_tiles_of_squares(x):
    total = None
    for l in range(0, x.shape[1], B):
        wide = x[:, l : l + B].astype(jnp.float32)
        total = wide * wide if total is None else total + wide * wide
    return total


def squares_mean_column(x):
    total = jnp.sum(lane_tiles_of_squares(x), axis=1, keepdims=True)
    return jnp.broadcast_to(total * (1.0 / x.shape[1]) + EPS, (x.shape[0], B))


def squares_mean_row(x):
    total = lane_tiles_of_squares(x)
    rows = [jnp.sum(total[i : i + B].T, axis=0, keepdims=True) for i in range(0, x.shape[0], B)]
    row = jnp.concatenate(rows, axis=1) * (1.0 / x.shape[1]) + EPS
    return jnp.broadcast_to(row, (8, x.shape[0]))


def spread(column, lanes):
    return jnp.concatenate([column] * (lanes // B), axis=1)


CHUNK = 16


def fill_cross(marks_ref, emb_ref, u_ref, k_ref, vq_ref, x_ref, x_row):
    m, e = emb_ref.shape
    k_ref[...] = nt(marks_ref[...], emb_ref[...])
    vq_ref[...] = squares_mean_column(marks_ref[...])

    def part(i, _):
        r = pl.multiple_of(i * CHUNK, CHUNK)
        vq = vq_ref[pl.ds(r, CHUNK), :]
        v_inv = lax.rsqrt(vq)
        v_root = vq * v_inv
        up = jnp.concatenate([u_ref[:8, :]] * (CHUNK // 8), axis=0)
        ur = jnp.concatenate([u_ref[8:, :]] * (CHUNK // 8), axis=0)
        c = recursion(k_ref[pl.ds(r, CHUNK), :] * up * spread(v_inv * (1.0 / e), m))
        x_ref[pl.ds(x_row(r), CHUNK), :] = (c * ur * spread(v_root * GROWTH, m)).astype(jnp.bfloat16)
        return 0

    lax.fori_loop(0, marks_ref.shape[0] // CHUNK, part, 0)


def own_kernel(marks_ref, emb_ref, x_ref, u_ref, k_ref, vq_ref):
    uq = squares_mean_row(emb_ref[...])
    inv = lax.rsqrt(uq)
    u_ref[:8, :] = inv
    u_ref[8:, :] = uq * inv
    fill_cross(marks_ref, emb_ref, u_ref, k_ref, vq_ref, x_ref, lambda r: r)


def own_cross(landmarks, embeddings):
    m = embeddings.shape[0]
    shard = landmarks.shape[0]
    vmem = pl.BlockSpec(memory_space=pltpu.VMEM)
    return pl.pallas_call(
        own_kernel,
        out_shape=(
            jax.ShapeDtypeStruct((shard, m), jnp.bfloat16),
            jax.ShapeDtypeStruct((16, m), jnp.float32),
        ),
        in_specs=[vmem, vmem],
        out_specs=(vmem, vmem),
        scratch_shapes=[pltpu.VMEM((shard, m), jnp.float32), pltpu.VMEM((shard, B), jnp.float32)],
        compiler_params=pltpu.CompilerParams(vmem_limit_bytes=12 << 20),
        name="own_cross",
    )(landmarks, embeddings)


class Plan(typing.NamedTuple):
    lands: int
    chips: int
    cores: int
    split: bool
    all_points: int


def gram_kernel(plan, na, at_ref, emb_ref, mine_ref, own_ref, u_ref, x_mine_ref, *refs):
    lands, chips, cores, split, all_points = plan
    count = chips * (cores if split else 1)
    far = refs[:count]
    keep_ref, send_ref, x_ref, ridge_ref, marks_ref, k_ref, vq_ref, out_ref = refs[count:]
    shard, e = mine_ref.shape
    n = shard * lands
    land, chip, core = at_ref[0], at_ref[1], at_ref[2]
    here = pl.multiple_of(land * shard, shard)
    x_ref[pl.ds(here, shard), :] = x_mine_ref[...]
    piece = far[0].shape[0] // (lands - 1)
    for a in range(cores if split else 1):
        for t in range(chips):
            slot = ((chip ^ t) * cores + (core ^ a)) if split else (chip ^ t)
            for s in range(1, lands):
                to = pl.multiple_of((s - 1) * shard + slot * piece, piece)
                marks_ref[pl.ds(to, piece), :] = far[a * chips + t][(s - 1) * piece : s * piece, :]

    def x_row(r):
        s = r // shard + 1
        return pl.multiple_of((land ^ s) * shard + r % shard, CHUNK)

    fill_cross(marks_ref, emb_ref, u_ref, k_ref, vq_ref, x_ref, x_row)

    share = own_ref.shape[0]
    oq = squares_mean_column(own_ref[...])
    o_inv = lax.rsqrt(oq)

    def ridge(marks, marks_q, to):
        k_own = nt(own_ref[...], marks)
        for l in range(0, shard, B):
            vq = marks_q[l : l + B].T[:8]
            v_inv = lax.rsqrt(vq)
            for i in range(share // 8):
                oi = o_inv[8 * i : 8 * i + 8]
                c = recursion(k_own[8 * i : 8 * i + 8, l : l + B] * v_inv * (oi * (1.0 / e)))
                root = oq[8 * i : 8 * i + 8] * oi
                ridge_ref[8 * i : 8 * i + 8, pl.ds(to + l, B)] = c * (vq * v_inv) * (root * (RIDGE * GROWTH))

    ridge(mine_ref[...], squares_mean_column(mine_ref[...]), here)
    for s in range(1, lands):
        rows = slice((s - 1) * shard, s * shard)
        ridge(marks_ref[rows, :], vq_ref[rows, :], pl.multiple_of((land ^ s) * shard, shard))

    position = land * shard + (chip * cores + core) * share
    row_block = position // B
    offset = position % B
    wide = 2 * B
    for w in range(n // wide):
        both = nt(x_ref[: (w + 1) * wide, :], x_ref[w * wide : (w + 1) * wide, :]) * (1.0 / all_points)
        for j in (2 * w, 2 * w + 1):
            start = column_start(plan, na, j)
            out_ref[start : start + (j + 1) * B, :] = both[: (j + 1) * B, (j % 2) * B : (j % 2 + 1) * B]
    for j in range(n // B):
        start = column_start(plan, na, j)

        @pl.when(row_block <= j)
        def _():
            at = pl.ds(pl.multiple_of(start + row_block * B + offset, share), share)
            out_ref[at, :] = out_ref[at, :] + ridge_ref[:, j * B : (j + 1) * B]

    done = base = 0
    for rows in segments(plan, na, n // B):
        half = rows // cores
        to = slice(done, done + half)
        keep_ref[to, :] = out_ref[pl.ds(pl.multiple_of(base + core * half, 8), half), :]
        send_ref[to, :] = out_ref[pl.ds(pl.multiple_of(base + (1 - core) * half, 8), half), :]
        done, base = done + half, base + rows


def packed_start(j):
    return j * (j + 1) // 2 * B


def segments(plan, na, nb):
    unit = 8 * plan.lands * plan.chips * plan.cores
    return [-(-rows // unit) * unit for rows in (packed_start(na), packed_start(nb) - packed_start(na))]


def column_start(plan, na, j):
    return packed_start(j) if j < na else packed_start(j) - packed_start(na) + segments(plan, na, j)[0]


def local_normal(at, plan, na, embeddings, landmarks, own, u, x_mine, far):
    n, m = landmarks.shape[0] * plan.lands, embeddings.shape[0]
    away = n - landmarks.shape[0]
    rows = sum(segments(plan, na, n // B))
    half = jax.ShapeDtypeStruct((rows // plan.cores, B), jnp.float32)
    vmem = pl.BlockSpec(memory_space=pltpu.VMEM)
    return pl.pallas_call(
        functools.partial(gram_kernel, plan, na),
        out_shape=(half, half),
        in_specs=[pl.BlockSpec(memory_space=pltpu.SMEM)] + [vmem] * (5 + len(far)),
        out_specs=(vmem,) * 2,
        scratch_shapes=[
            pltpu.VMEM((n, m), jnp.bfloat16),
            pltpu.VMEM((own.shape[0], n), jnp.float32),
            pltpu.VMEM((away, landmarks.shape[1]), jnp.bfloat16),
            pltpu.VMEM((away, m), jnp.float32),
            pltpu.VMEM((away, B), jnp.float32),
            pltpu.VMEM((rows, B), jnp.float32),
        ],
        compiler_params=pltpu.CompilerParams(vmem_limit_bytes=24 << 20),
        name="gram",
    )(at, embeddings, landmarks, own, u, x_mine, *far)


def add_cut_kernel(ways, axis, parts, at_ref, *refs):
    ins, outs = refs[: len(refs) - ways], refs[len(refs) - ways :]
    base = 0
    for rows in parts:
        h = rows // ways
        for s in range(ways):
            at = pl.ds(pl.multiple_of(base + (at_ref[axis] ^ s) * h, 8), h) if ways > 1 else slice(base, base + h)
            total = ins[0][at, :]
            for r in ins[1:]:
                total = total + r[at, :]
            outs[s][base // ways : base // ways + h, :] = total
        base += rows


def add_cut(at, axis, ways, parts, ins):
    h = sum(parts) // ways
    vmem = pl.BlockSpec(memory_space=pltpu.VMEM)
    return pl.pallas_call(
        functools.partial(add_cut_kernel, ways, axis, parts),
        out_shape=tuple([jax.ShapeDtypeStruct((h, B), jnp.float32)] * ways),
        in_specs=[pl.BlockSpec(memory_space=pltpu.SMEM)] + [vmem] * len(ins),
        out_specs=tuple([vmem] * ways),
        compiler_params=pltpu.CompilerParams(vmem_limit_bytes=8 << 20),
        name="add_cut",
    )(at, *ins)


def place_kernel(axis, ways, parts, at_ref, *refs):
    ins, outs = refs[:ways], refs[ways:]
    base = 0
    for out, h in zip(outs, parts):
        for s in range(ways):
            out[pl.ds(pl.multiple_of((at_ref[axis] ^ s) * h, 8), h), :] = ins[s][base : base + h, :]
        base += h


def place(at, axis, parts, ins):
    vmem = pl.BlockSpec(memory_space=pltpu.VMEM)
    return pl.pallas_call(
        functools.partial(place_kernel, axis, len(ins), parts),
        out_shape=tuple(jax.ShapeDtypeStruct((h * len(ins), B), jnp.float32) for h in parts),
        in_specs=[pl.BlockSpec(memory_space=pltpu.SMEM)] + [vmem] * len(ins),
        out_specs=(vmem,) * len(parts),
        compiler_params=pltpu.CompilerParams(vmem_limit_bytes=8 << 20),
        name="place",
    )(at, *ins)


def thirds(x):
    h = x.astype(jnp.bfloat16)
    r = x - h.astype(jnp.float32)
    m = r.astype(jnp.bfloat16)
    return h, m, (r - m.astype(jnp.float32)).astype(jnp.bfloat16)

def left_terms(x, axis):
    h, m, l = thirds(x)
    return jnp.concatenate([h, h, h, m, m, l], axis)

def right_terms(x, axis):
    h, m, l = thirds(x)
    return jnp.concatenate([h, m, l, h, m, h], axis)

def dot32(a, b):
    return lax.dot_general(left_terms(a, 1), right_terms(b, 0), (((1,), (0,)), ((), ())), preferred_element_type=jnp.float32)

def dot32_t(a, b):
    return dot32(a.T, b)

def factor_block(d):
    rows8 = lax.broadcasted_iota(jnp.int32, (8, 128), 0)
    eye = (lax.broadcasted_iota(jnp.int32, (B, B), 0) == lax.broadcasted_iota(jnp.int32, (B, B), 1)).astype(jnp.float32)
    n = B // W
    g = W // 8
    left = [d[8 * i:8 * i + 8] for i in range(B // 8)]
    right = [eye[8 * i:8 * i + 8] for i in range(B // 8)]
    for p in range(n):
        base = p * g
        last = p == n - 1
        groups = list(range(base, base + (g if last else 2 * g)))
        col = [[None] * len(groups) for _ in range(W)]
        for i in range(W):
            for t, r in enumerate(groups):
                if t < g and t < i // 8:
                    continue
                lane = p * W + i
                col[i][t] = jnp.broadcast_to(left[r][:, lane:lane + 1], (8, 128))
        diag = [jnp.ones((8, 128), jnp.float32) for _ in range(g)]
        for j in range(W):
            tj, sj = j // 8, j % 8
            pivot = jnp.broadcast_to(col[j][tj][sj:sj + 1], (8, 128))
            diag[tj] = jnp.where(rows8 == sj, pivot, diag[tj])
            inv = 1.0 / pivot
            coefs = {}
            for i in range(j + 1, W):
                coefs[i] = jnp.broadcast_to(col[j][i // 8][i % 8:i % 8 + 1], (8, 128))
            scaled = [None] * len(groups)
            for t in range(len(groups)):
                if col[j][t] is None:
                    continue
                scaled[t] = col[j][t] * inv
            for i in range(j + 1, W):
                for t in range(len(groups)):
                    if col[i][t] is None:
                        continue
                    if i == j + 1:
                        col[i][t] = col[i][t] - (col[j][t] * coefs[i]) * inv
                    else:
                        col[i][t] = col[i][t] - scaled[t] * coefs[i]
            rl = jnp.broadcast_to(left[base + tj][sj:sj + 1], (8, 128))
            rr = jnp.broadcast_to(right[base + tj][sj:sj + 1], (8, 128))
            for t, r in enumerate(groups):
                if scaled[t] is None:
                    continue
                c = scaled[t]
                if t == tj:
                    if sj == 7:
                        continue
                    c = jnp.where(rows8 > sj, c, 0.0)
                left[r] = left[r] - c * rl
                right[r] = right[r] - c * rr
        for t in range(g):
            s = lax.rsqrt(diag[t])
            left[base + t] = left[base + t] * s
            right[base + t] = right[base + t] * s
        rest = (n - p - 2) * W
        if rest > 0:
            ul = jnp.concatenate(left[base:base + g], 0)
            ur = jnp.concatenate(right[base:base + g], 0)
            u = jnp.concatenate([ul, ur], 1)
            lo_row = (p + 2) * W
            upd = lax.dot_general(left_terms(ul, 0), right_terms(u, 0), (((0,), (0,)), ((), ())), preferred_element_type=jnp.float32)
            for r in range(lo_row // 8, B // 8):
                left[r] = left[r] - upd[8 * r:8 * r + 8, :128]
                right[r] = right[r] - upd[8 * r:8 * r + 8, 128:]
    u = jnp.concatenate(left, 0)
    w = jnp.concatenate(right, 0)
    tri = lax.broadcasted_iota(jnp.int32, (B, B), 0) <= lax.broadcasted_iota(jnp.int32, (B, B), 1)
    return jnp.where(tri, u, 0.0), w


def eliminate(nb, m_ref, d_ref, r_ref, store):
    lane_block = lax.broadcasted_iota(jnp.int32, (B, nb * B), 1) // B
    d_ref[...] = m_ref[:B, :B]
    r_ref[...] = jnp.zeros_like(r_ref)

    def step(k, _):
        u, w = factor_block(d_ref[...])
        prev = r_ref[...]
        m_ref[...] = m_ref[...] - dot32_t(prev, prev)
        row = dot32(w, m_ref[pl.ds(pl.multiple_of(k * B, B), B), :])
        row = jnp.where(lane_block > k, row, 0.0)
        r_ref[...] = row
        nxt = pl.multiple_of(jnp.minimum(k + 1, nb - 1) * B, B)
        rn = r_ref[:, pl.ds(nxt, B)]
        d_ref[...] = m_ref[pl.ds(nxt, B), pl.ds(nxt, B)] - dot32_t(rn, rn)
        store(pl.multiple_of(k * B, B), row, u, w)
        return 0

    lax.fori_loop(0, nb, step, 0)


def place_parts(plan, at_ref, parts, a_ref):
    h = parts[0].shape[0]
    for a in range(plan.cores):
        for t in range(plan.chips):
            slot = (at_ref[2] ^ a) * plan.chips + (at_ref[1] ^ t)
            a_ref[pl.ds(pl.multiple_of(slot * h, h), h), :] = parts[a * plan.chips + t][...]


def first_factor_kernel(plan, at_ref, *refs):
    count = plan.chips * plan.cores
    f_ref, w_ref, a_ref, m_ref, d_ref, r_ref = refs[count:]
    na = f_ref.shape[0] // B
    place_parts(plan, at_ref, refs[:count], a_ref)
    for j in range(na):
        m_ref[: (j + 1) * B, j * B : (j + 1) * B] = a_ref[packed_start(j) : packed_start(j) + (j + 1) * B, :]

    def store(at, row, u, w):
        f_ref[pl.ds(at, B), :] = row
        f_ref[pl.ds(at, B), pl.ds(at, B)] = u
        w_ref[pl.ds(at, B), :] = w

    eliminate(na, m_ref, d_ref, r_ref, store)


def first_factor(at, plan, na, parts):
    vmem = pl.BlockSpec(memory_space=pltpu.VMEM)
    return pl.pallas_call(
        functools.partial(first_factor_kernel, plan),
        out_shape=(
            jax.ShapeDtypeStruct((na * B, na * B), jnp.float32),
            jax.ShapeDtypeStruct((na * B, B), jnp.float32),
        ),
        in_specs=[pl.BlockSpec(memory_space=pltpu.SMEM)] + [vmem] * len(parts),
        out_specs=(vmem,) * 2,
        scratch_shapes=[
            pltpu.VMEM((parts[0].shape[0] * len(parts), B), jnp.float32),
            pltpu.VMEM((na * B, na * B), jnp.float32),
            pltpu.VMEM((B, B), jnp.float32),
            pltpu.VMEM((B, na * B), jnp.float32),
        ],
        compiler_params=pltpu.CompilerParams(vmem_limit_bytes=16 << 20),
        name="chol_first",
    )(at, *parts)


def last_factor_kernel(plan, at_ref, f_ref, w_ref, *refs):
    count = plan.chips * plan.cores
    o_ref, a_ref, t_ref, m_ref, d_ref, r_ref = refs[count:]
    n, top = o_ref.shape[0] // B, f_ref.shape[0]
    na = top // B
    place_parts(plan, at_ref, refs[:count], a_ref)
    for j in range(na, n):
        start = packed_start(j) - packed_start(na)
        lanes = slice((j - na) * B, (j - na + 1) * B)
        t_ref[:, lanes] = a_ref[start : start + top, :]
        m_ref[: (j - na + 1) * B, lanes] = a_ref[start + top : start + (j + 1) * B, :]
    o_ref[:top, :top] = f_ref[...]
    o_ref[top:, :top] = jnp.zeros((n * B - top, top), jnp.float32)
    for k in range(na):
        rows = slice(k * B, (k + 1) * B)
        row = dot32(w_ref[rows, :], t_ref[rows, :])
        o_ref[rows, top:] = row
        if k < na - 1:
            t_ref[(k + 1) * B :, :] = t_ref[(k + 1) * B :, :] - dot32_t(f_ref[rows, (k + 1) * B :], row)
        m_ref[...] = m_ref[...] - dot32_t(row, row)

    def store(at, row, u, w):
        down = pl.multiple_of(top + at, B)
        o_ref[pl.ds(down, B), top:] = row
        o_ref[pl.ds(down, B), pl.ds(down, B)] = u

    eliminate(n - na, m_ref, d_ref, r_ref, store)


def last_factor(at, plan, n, f, w, parts):
    vmem = pl.BlockSpec(memory_space=pltpu.VMEM)
    top = f.shape[0]
    return pl.pallas_call(
        functools.partial(last_factor_kernel, plan),
        out_shape=jax.ShapeDtypeStruct((n, n), jnp.float32),
        in_specs=[pl.BlockSpec(memory_space=pltpu.SMEM)] + [vmem] * (2 + len(parts)),
        out_specs=vmem,
        scratch_shapes=[
            pltpu.VMEM((parts[0].shape[0] * len(parts), B), jnp.float32),
            pltpu.VMEM((top, n - top), jnp.float32),
            pltpu.VMEM((n - top, n - top), jnp.float32),
            pltpu.VMEM((B, B), jnp.float32),
            pltpu.VMEM((B, n - top), jnp.float32),
        ],
        compiler_params=pltpu.CompilerParams(vmem_limit_bytes=24 << 20),
        name="chol_last",
    )(at, f, w, *parts)


def swap(x, axis, s):
    return lax.ppermute(x, axis, [(i, i ^ s) for i in range(lax.axis_size(axis))])


def scatter(pieces, axis):
    arrived = [swap(p, axis, s) for s, p in reversed(list(enumerate(pieces))) if s]
    return [pieces[0]] + arrived[::-1]


def spread_out(x, axis):
    return [x] + [swap(x, axis, s) for s in range(1, lax.axis_size(axis))]


def shards(embeddings, landmarks):
    lands, chips, cores = (lax.axis_size(a) for a in ("land", "chip", "core"))
    land, chip, core = (lax.axis_index(a) for a in ("land", "chip", "core"))
    at = jnp.stack([land, chip, core]).astype(jnp.int32)
    shard = landmarks.shape[0]
    n = shard * lands
    plan = Plan(lands, chips, cores, shard // (chips * cores) % 16 == 0, embeddings.shape[0] * lands * chips * cores)

    share = shard // (chips * cores)
    own = lax.dynamic_slice_in_dim(landmarks, (chip * cores + core) * share, share, 0)
    if plan.split:
        piece = own
    else:
        piece = lax.dynamic_slice_in_dim(landmarks, chip * (shard // chips), shard // chips, 0)
    z = jnp.concatenate(spread_out(piece, "land")[1:], 0)
    far = spread_out(z, "chip")
    x_mine, u = own_cross(landmarks, embeddings)
    if plan.split:
        far, x_mine, u = lax.optimization_barrier((far, x_mine, u))
        for a in range(1, cores):
            far = far + [swap(f, "core", a) for f in far[:chips]]

    na = n // B // 2
    keep, send = local_normal(at, plan, na, embeddings, landmarks, own, u, x_mine, far)
    rows = [r // cores for r in segments(plan, na, n // B)]
    parts = scatter(add_cut(at, 1, chips, rows, [keep, swap(send, "core", 1)]), "chip")
    rows = [r // chips for r in rows]
    parts = scatter(add_cut(at, 0, lands, rows, parts), "land")
    rows = [r // lands for r in rows]
    (whole,) = add_cut(at, 0, 1, rows, parts)
    first, last = place(at, 0, rows, spread_out(whole, "land"))
    first = spread_out(first, "chip")
    first = first + [swap(p, "core", 1) for p in first]
    f, w = first_factor(at, plan, na, first)
    last, f, w = lax.optimization_barrier((spread_out(last, "chip"), f, w))
    last = last + [swap(p, "core", 1) for p in last]
    return last_factor(at, plan, n, f, w, last)


def solution(mesh):
    land, rows = mesh.axis_names
    cores = 2
    fine = Mesh(mesh.devices.reshape(mesh.shape[land], mesh.shape[rows] // cores, cores), ("land", "chip", "core"))
    in_specs = (P(("land", "chip", "core"), None), P("land", None))
    return jax.shard_map(shards, mesh=fine, in_specs=in_specs, out_specs=P(), check_vma=False)
```

```python
import functools
import math
import typing

import jax
import jax.numpy as jnp
from jax import lax
from jax.experimental import pallas as pl
from jax.experimental.pallas import tpu as pltpu
from jax.sharding import Mesh
from jax.sharding import PartitionSpec as P

LAYERS = 6
SCALE_SQ = 1.0 / 32.0
RIDGE = 0.1
EPS = 1e-06
B = 128
W = 16
TINY = 1e-30

ARC = (0.9426497266634519, 0.04833294295062493, 0.004716300148249888, 0.004298816276929029)
KEEP = 1.0 / (1.0 + SCALE_SQ)
ARC = tuple(c * SCALE_SQ * KEEP / math.pi for c in ARC)
GROWTH = (1.0 + SCALE_SQ) ** LAYERS


def recursion(c):
    for _ in range(LAYERS):
        w = jnp.maximum(1.0 - jnp.abs(c), TINY)
        t = (w * w) * lax.rsqrt(w)
        poly = ARC[3]
        for a in ARC[2::-1]:
            poly = poly * w + a
        c = jnp.maximum(c, KEEP * c) + t * poly
    return c


def nt(a, b):
    return lax.dot_general(a, b, (((1,), (1,)), ((), ())), preferred_element_type=jnp.float32)


def lane_tiles_of_squares(x):
    total = None
    for l in range(0, x.shape[1], B):
        wide = x[:, l : l + B].astype(jnp.float32)
        total = wide * wide if total is None else total + wide * wide
    return total


def squares_mean_column(x):
    total = jnp.sum(lane_tiles_of_squares(x), axis=1, keepdims=True)
    return jnp.broadcast_to(total * (1.0 / x.shape[1]) + EPS, (x.shape[0], B))


def squares_mean_row(x):
    total = lane_tiles_of_squares(x)
    rows = [jnp.sum(total[i : i + B].T, axis=0, keepdims=True) for i in range(0, x.shape[0], B)]
    row = jnp.concatenate(rows, axis=1) * (1.0 / x.shape[1]) + EPS
    return jnp.broadcast_to(row, (8, x.shape[0]))


def spread(column, lanes):
    return jnp.concatenate([column] * (lanes // B), axis=1)


CHUNK = 16


def fill_cross(marks_ref, emb_ref, u_ref, k_ref, vq_ref, x_ref, x_row):
    m, e = emb_ref.shape
    k_ref[...] = nt(marks_ref[...], emb_ref[...])
    vq_ref[...] = squares_mean_column(marks_ref[...])

    def part(i, _):
        r = pl.multiple_of(i * CHUNK, CHUNK)
        vq = vq_ref[pl.ds(r, CHUNK), :]
        v_inv = lax.rsqrt(vq)
        v_root = vq * v_inv
        up = jnp.concatenate([u_ref[:8, :]] * (CHUNK // 8), axis=0)
        ur = jnp.concatenate([u_ref[8:, :]] * (CHUNK // 8), axis=0)
        c = recursion(k_ref[pl.ds(r, CHUNK), :] * up * spread(v_inv * (1.0 / e), m))
        x_ref[pl.ds(x_row(r), CHUNK), :] = (c * ur * spread(v_root * GROWTH, m)).astype(jnp.bfloat16)
        return 0

    lax.fori_loop(0, marks_ref.shape[0] // CHUNK, part, 0)


def own_kernel(marks_ref, emb_ref, x_ref, u_ref, k_ref, vq_ref):
    uq = squares_mean_row(emb_ref[...])
    inv = lax.rsqrt(uq)
    u_ref[:8, :] = inv
    u_ref[8:, :] = uq * inv
    fill_cross(marks_ref, emb_ref, u_ref, k_ref, vq_ref, x_ref, lambda r: r)


def own_cross(landmarks, embeddings):
    m = embeddings.shape[0]
    shard = landmarks.shape[0]
    vmem = pl.BlockSpec(memory_space=pltpu.VMEM)
    return pl.pallas_call(
        own_kernel,
        out_shape=(
            jax.ShapeDtypeStruct((shard, m), jnp.bfloat16),
            jax.ShapeDtypeStruct((16, m), jnp.float32),
        ),
        in_specs=[vmem, vmem],
        out_specs=(vmem, vmem),
        scratch_shapes=[pltpu.VMEM((shard, m), jnp.float32), pltpu.VMEM((shard, B), jnp.float32)],
        compiler_params=pltpu.CompilerParams(vmem_limit_bytes=12 << 20),
        name="own_cross",
    )(landmarks, embeddings)


class Plan(typing.NamedTuple):
    lands: int
    chips: int
    cores: int
    split: bool
    all_points: int


def gram_kernel(plan, na, at_ref, emb_ref, mine_ref, own_ref, u_ref, x_mine_ref, *refs):
    lands, chips, cores, split, all_points = plan
    count = chips * (cores if split else 1)
    far = refs[:count]
    keep_ref, send_ref, x_ref, ridge_ref, marks_ref, k_ref, vq_ref, out_ref = refs[count:]
    shard, e = mine_ref.shape
    n = shard * lands
    land, chip, core = at_ref[0], at_ref[1], at_ref[2]
    here = pl.multiple_of(land * shard, shard)
    x_ref[pl.ds(here, shard), :] = x_mine_ref[...]
    piece = far[0].shape[0] // (lands - 1)
    for a in range(cores if split else 1):
        for t in range(chips):
            slot = ((chip ^ t) * cores + (core ^ a)) if split else (chip ^ t)
            for s in range(1, lands):
                to = pl.multiple_of((s - 1) * shard + slot * piece, piece)
                marks_ref[pl.ds(to, piece), :] = far[a * chips + t][(s - 1) * piece : s * piece, :]

    def x_row(r):
        s = r // shard + 1
        return pl.multiple_of((land ^ s) * shard + r % shard, CHUNK)

    fill_cross(marks_ref, emb_ref, u_ref, k_ref, vq_ref, x_ref, x_row)

    share = own_ref.shape[0]
    oq = squares_mean_column(own_ref[...])
    o_inv = lax.rsqrt(oq)

    def ridge(marks, marks_q, to):
        k_own = nt(own_ref[...], marks)
        for l in range(0, shard, B):
            vq = marks_q[l : l + B].T[:8]
            v_inv = lax.rsqrt(vq)
            for i in range(share // 8):
                oi = o_inv[8 * i : 8 * i + 8]
                c = recursion(k_own[8 * i : 8 * i + 8, l : l + B] * v_inv * (oi * (1.0 / e)))
                root = oq[8 * i : 8 * i + 8] * oi
                ridge_ref[8 * i : 8 * i + 8, pl.ds(to + l, B)] = c * (vq * v_inv) * (root * (RIDGE * GROWTH))

    ridge(mine_ref[...], squares_mean_column(mine_ref[...]), here)
    for s in range(1, lands):
        rows = slice((s - 1) * shard, s * shard)
        ridge(marks_ref[rows, :], vq_ref[rows, :], pl.multiple_of((land ^ s) * shard, shard))

    position = land * shard + (chip * cores + core) * share
    row_block = position // B
    offset = position % B
    wide = 2 * B
    for w in range(n // wide):
        both = nt(x_ref[: (w + 1) * wide, :], x_ref[w * wide : (w + 1) * wide, :]) * (1.0 / all_points)
        for j in (2 * w, 2 * w + 1):
            start = column_start(plan, na, j)
            out_ref[start : start + (j + 1) * B, :] = both[: (j + 1) * B, (j % 2) * B : (j % 2 + 1) * B]
    for j in range(n // B):
        start = column_start(plan, na, j)

        @pl.when(row_block <= j)
        def _():
            at = pl.ds(pl.multiple_of(start + row_block * B + offset, share), share)
            out_ref[at, :] = out_ref[at, :] + ridge_ref[:, j * B : (j + 1) * B]

    done = base = 0
    for rows in segments(plan, na, n // B):
        half = rows // cores
        to = slice(done, done + half)
        keep_ref[to, :] = out_ref[pl.ds(pl.multiple_of(base + core * half, 8), half), :]
        send_ref[to, :] = out_ref[pl.ds(pl.multiple_of(base + (1 - core) * half, 8), half), :]
        done, base = done + half, base + rows


def packed_start(j):
    return j * (j + 1) // 2 * B


def segments(plan, na, nb):
    unit = 8 * plan.lands * plan.chips * plan.cores
    return [-(-rows // unit) * unit for rows in (packed_start(na), packed_start(nb) - packed_start(na))]


def column_start(plan, na, j):
    return packed_start(j) if j < na else packed_start(j) - packed_start(na) + segments(plan, na, j)[0]


def local_normal(at, plan, na, embeddings, landmarks, own, u, x_mine, far):
    n, m = landmarks.shape[0] * plan.lands, embeddings.shape[0]
    away = n - landmarks.shape[0]
    rows = sum(segments(plan, na, n // B))
    half = jax.ShapeDtypeStruct((rows // plan.cores, B), jnp.float32)
    vmem = pl.BlockSpec(memory_space=pltpu.VMEM)
    return pl.pallas_call(
        functools.partial(gram_kernel, plan, na),
        out_shape=(half, half),
        in_specs=[pl.BlockSpec(memory_space=pltpu.SMEM)] + [vmem] * (5 + len(far)),
        out_specs=(vmem,) * 2,
        scratch_shapes=[
            pltpu.VMEM((n, m), jnp.bfloat16),
            pltpu.VMEM((own.shape[0], n), jnp.float32),
            pltpu.VMEM((away, landmarks.shape[1]), jnp.bfloat16),
            pltpu.VMEM((away, m), jnp.float32),
            pltpu.VMEM((away, B), jnp.float32),
            pltpu.VMEM((rows, B), jnp.float32),
        ],
        compiler_params=pltpu.CompilerParams(vmem_limit_bytes=24 << 20),
        name="gram",
    )(at, embeddings, landmarks, own, u, x_mine, *far)


def add_cut_kernel(ways, axis, parts, at_ref, *refs):
    ins, outs = refs[: len(refs) - ways], refs[len(refs) - ways :]
    base = 0
    for rows in parts:
        h = rows // ways
        for q in range(ways):
            s = -q % ways
            at = pl.ds(pl.multiple_of(base + (at_ref[axis] ^ s) * h, 8), h) if ways > 1 else slice(base, base + h)
            total = ins[0][at, :]
            for r in ins[1:]:
                total = total + r[at, :]
            outs[q][base // ways : base // ways + h, :] = total
        base += rows


def add_cut(at, axis, ways, parts, ins):
    h = sum(parts) // ways
    vmem = pl.BlockSpec(memory_space=pltpu.VMEM)
    return pl.pallas_call(
        functools.partial(add_cut_kernel, ways, axis, parts),
        out_shape=tuple([jax.ShapeDtypeStruct((h, B), jnp.float32)] * ways),
        in_specs=[pl.BlockSpec(memory_space=pltpu.SMEM)] + [vmem] * len(ins),
        out_specs=tuple([vmem] * ways),
        compiler_params=pltpu.CompilerParams(vmem_limit_bytes=8 << 20),
        name="add_cut",
    )(at, *ins)


def place_kernel(axis, ways, parts, at_ref, *refs):
    ins, outs = refs[:ways], refs[ways:]
    base = 0
    for out, h in zip(outs, parts):
        for s in range(ways):
            out[pl.ds(pl.multiple_of((at_ref[axis] ^ s) * h, 8), h), :] = ins[s][base : base + h, :]
        base += h


def place(at, axis, parts, ins):
    vmem = pl.BlockSpec(memory_space=pltpu.VMEM)
    return pl.pallas_call(
        functools.partial(place_kernel, axis, len(ins), parts),
        out_shape=tuple(jax.ShapeDtypeStruct((h * len(ins), B), jnp.float32) for h in parts),
        in_specs=[pl.BlockSpec(memory_space=pltpu.SMEM)] + [vmem] * len(ins),
        out_specs=(vmem,) * len(parts),
        compiler_params=pltpu.CompilerParams(vmem_limit_bytes=8 << 20),
        name="place",
    )(at, *ins)


def thirds(x):
    h = x.astype(jnp.bfloat16)
    r = x - h.astype(jnp.float32)
    m = r.astype(jnp.bfloat16)
    return h, m, (r - m.astype(jnp.float32)).astype(jnp.bfloat16)

def left_terms(x, axis):
    h, m, l = thirds(x)
    return jnp.concatenate([h, h, h, m, m, l], axis)

def right_terms(x, axis):
    h, m, l = thirds(x)
    return jnp.concatenate([h, m, l, h, m, h], axis)

def dot32(a, b):
    return lax.dot_general(left_terms(a, 1), right_terms(b, 0), (((1,), (0,)), ((), ())), preferred_element_type=jnp.float32)

def dot32_t(a, b):
    return dot32(a.T, b)

def factor_block(d):
    rows8 = lax.broadcasted_iota(jnp.int32, (8, 128), 0)
    eye = (lax.broadcasted_iota(jnp.int32, (B, B), 0) == lax.broadcasted_iota(jnp.int32, (B, B), 1)).astype(jnp.float32)
    n = B // W
    g = W // 8
    left = [d[8 * i:8 * i + 8] for i in range(B // 8)]
    right = [eye[8 * i:8 * i + 8] for i in range(B // 8)]
    for p in range(n):
        base = p * g
        last = p == n - 1
        groups = list(range(base, base + (g if last else 2 * g)))
        col = [[None] * len(groups) for _ in range(W)]
        for i in range(W):
            for t, r in enumerate(groups):
                if t < g and t < i // 8:
                    continue
                lane = p * W + i
                col[i][t] = jnp.broadcast_to(left[r][:, lane:lane + 1], (8, 128))
        diag = [jnp.ones((8, 128), jnp.float32) for _ in range(g)]
        for j in range(W):
            tj, sj = j // 8, j % 8
            pivot = jnp.broadcast_to(col[j][tj][sj:sj + 1], (8, 128))
            diag[tj] = jnp.where(rows8 == sj, pivot, diag[tj])
            inv = 1.0 / pivot
            coefs = {}
            for i in range(j + 1, W):
                coefs[i] = jnp.broadcast_to(col[j][i // 8][i % 8:i % 8 + 1], (8, 128))
            scaled = [None] * len(groups)
            for t in range(len(groups)):
                if col[j][t] is None:
                    continue
                scaled[t] = col[j][t] * inv
            for i in range(j + 1, W):
                for t in range(len(groups)):
                    if col[i][t] is None:
                        continue
                    if i == j + 1:
                        col[i][t] = col[i][t] - (col[j][t] * coefs[i]) * inv
                    else:
                        col[i][t] = col[i][t] - scaled[t] * coefs[i]
            rl = jnp.broadcast_to(left[base + tj][sj:sj + 1], (8, 128))
            rr = jnp.broadcast_to(right[base + tj][sj:sj + 1], (8, 128))
            for t, r in enumerate(groups):
                if scaled[t] is None:
                    continue
                c = scaled[t]
                if t == tj:
                    if sj == 7:
                        continue
                    c = jnp.where(rows8 > sj, c, 0.0)
                left[r] = left[r] - c * rl
                right[r] = right[r] - c * rr
        for t in range(g):
            s = lax.rsqrt(diag[t])
            left[base + t] = left[base + t] * s
            right[base + t] = right[base + t] * s
        rest = (n - p - 2) * W
        if rest > 0:
            ul = jnp.concatenate(left[base:base + g], 0)
            ur = jnp.concatenate(right[base:base + g], 0)
            u = jnp.concatenate([ul, ur], 1)
            lo_row = (p + 2) * W
            upd = lax.dot_general(left_terms(ul, 0), right_terms(u, 0), (((0,), (0,)), ((), ())), preferred_element_type=jnp.float32)
            for r in range(lo_row // 8, B // 8):
                left[r] = left[r] - upd[8 * r:8 * r + 8, :128]
                right[r] = right[r] - upd[8 * r:8 * r + 8, 128:]
    u = jnp.concatenate(left, 0)
    w = jnp.concatenate(right, 0)
    tri = lax.broadcasted_iota(jnp.int32, (B, B), 0) <= lax.broadcasted_iota(jnp.int32, (B, B), 1)
    return jnp.where(tri, u, 0.0), w


def eliminate(nb, m_ref, d_ref, r_ref, store):
    lane_block = lax.broadcasted_iota(jnp.int32, (B, nb * B), 1) // B
    d_ref[...] = m_ref[:B, :B]
    r_ref[...] = jnp.zeros_like(r_ref)

    def step(k, _):
        u, w = factor_block(d_ref[...])
        prev = r_ref[...]
        m_ref[...] = m_ref[...] - dot32_t(prev, prev)
        row = dot32(w, m_ref[pl.ds(pl.multiple_of(k * B, B), B), :])
        row = jnp.where(lane_block > k, row, 0.0)
        r_ref[...] = row
        nxt = pl.multiple_of(jnp.minimum(k + 1, nb - 1) * B, B)
        rn = r_ref[:, pl.ds(nxt, B)]
        d_ref[...] = m_ref[pl.ds(nxt, B), pl.ds(nxt, B)] - dot32_t(rn, rn)
        store(pl.multiple_of(k * B, B), row, u, w)
        return 0

    lax.fori_loop(0, nb, step, 0)


def place_parts(plan, at_ref, parts, a_ref):
    h = parts[0].shape[0]
    for a in range(plan.cores):
        for t in range(plan.chips):
            slot = (at_ref[2] ^ a) * plan.chips + (at_ref[1] ^ t)
            a_ref[pl.ds(pl.multiple_of(slot * h, h), h), :] = parts[a * plan.chips + t][...]


def first_factor_kernel(plan, at_ref, *refs):
    count = plan.chips * plan.cores
    f_ref, w_ref, a_ref, m_ref, d_ref, r_ref = refs[count:]
    na = f_ref.shape[0] // B
    place_parts(plan, at_ref, refs[:count], a_ref)
    for j in range(na):
        m_ref[: (j + 1) * B, j * B : (j + 1) * B] = a_ref[packed_start(j) : packed_start(j) + (j + 1) * B, :]

    def store(at, row, u, w):
        f_ref[pl.ds(at, B), :] = row
        f_ref[pl.ds(at, B), pl.ds(at, B)] = u
        w_ref[pl.ds(at, B), :] = w

    eliminate(na, m_ref, d_ref, r_ref, store)


def first_factor(at, plan, na, parts):
    vmem = pl.BlockSpec(memory_space=pltpu.VMEM)
    return pl.pallas_call(
        functools.partial(first_factor_kernel, plan),
        out_shape=(
            jax.ShapeDtypeStruct((na * B, na * B), jnp.float32),
            jax.ShapeDtypeStruct((na * B, B), jnp.float32),
        ),
        in_specs=[pl.BlockSpec(memory_space=pltpu.SMEM)] + [vmem] * len(parts),
        out_specs=(vmem,) * 2,
        scratch_shapes=[
            pltpu.VMEM((parts[0].shape[0] * len(parts), B), jnp.float32),
            pltpu.VMEM((na * B, na * B), jnp.float32),
            pltpu.VMEM((B, B), jnp.float32),
            pltpu.VMEM((B, na * B), jnp.float32),
        ],
        compiler_params=pltpu.CompilerParams(vmem_limit_bytes=16 << 20),
        name="chol_first",
    )(at, *parts)


def last_factor_kernel(plan, at_ref, f_ref, w_ref, *refs):
    count = plan.chips * plan.cores
    o_ref, a_ref, t_ref, m_ref, d_ref, r_ref = refs[count:]
    n, top = o_ref.shape[0] // B, f_ref.shape[0]
    na = top // B
    place_parts(plan, at_ref, refs[:count], a_ref)
    for j in range(na, n):
        start = packed_start(j) - packed_start(na)
        lanes = slice((j - na) * B, (j - na + 1) * B)
        t_ref[:, lanes] = a_ref[start : start + top, :]
        m_ref[: (j - na + 1) * B, lanes] = a_ref[start + top : start + (j + 1) * B, :]
    o_ref[:top, :top] = f_ref[...]
    o_ref[top:, :top] = jnp.zeros((n * B - top, top), jnp.float32)
    for k in range(na):
        rows = slice(k * B, (k + 1) * B)
        row = dot32(w_ref[rows, :], t_ref[rows, :])
        o_ref[rows, top:] = row
        if k < na - 1:
            t_ref[(k + 1) * B :, :] = t_ref[(k + 1) * B :, :] - dot32_t(f_ref[rows, (k + 1) * B :], row)
        m_ref[...] = m_ref[...] - dot32_t(row, row)

    def store(at, row, u, w):
        down = pl.multiple_of(top + at, B)
        o_ref[pl.ds(down, B), top:] = row
        o_ref[pl.ds(down, B), pl.ds(down, B)] = u

    eliminate(n - na, m_ref, d_ref, r_ref, store)


def last_factor(at, plan, n, f, w, parts):
    vmem = pl.BlockSpec(memory_space=pltpu.VMEM)
    top = f.shape[0]
    return pl.pallas_call(
        functools.partial(last_factor_kernel, plan),
        out_shape=jax.ShapeDtypeStruct((n, n), jnp.float32),
        in_specs=[pl.BlockSpec(memory_space=pltpu.SMEM)] + [vmem] * (2 + len(parts)),
        out_specs=vmem,
        scratch_shapes=[
            pltpu.VMEM((parts[0].shape[0] * len(parts), B), jnp.float32),
            pltpu.VMEM((top, n - top), jnp.float32),
            pltpu.VMEM((n - top, n - top), jnp.float32),
            pltpu.VMEM((B, B), jnp.float32),
            pltpu.VMEM((B, n - top), jnp.float32),
        ],
        compiler_params=pltpu.CompilerParams(vmem_limit_bytes=24 << 20),
        name="chol_last",
    )(at, f, w, *parts)


def swap(x, axis, s):
    return lax.ppermute(x, axis, [(i, i ^ s) for i in range(lax.axis_size(axis))])


def scatter(pieces, axis):
    return [pieces[0]] + [swap(p, axis, -q % len(pieces)) for q, p in enumerate(pieces) if q]


def spread_out(x, axis):
    return [x] + [swap(x, axis, s) for s in range(1, lax.axis_size(axis))]


def shards(embeddings, landmarks):
    lands, chips, cores = (lax.axis_size(a) for a in ("land", "chip", "core"))
    land, chip, core = (lax.axis_index(a) for a in ("land", "chip", "core"))
    at = jnp.stack([land, chip, core]).astype(jnp.int32)
    shard = landmarks.shape[0]
    n = shard * lands
    plan = Plan(lands, chips, cores, shard // (chips * cores) % 16 == 0, embeddings.shape[0] * lands * chips * cores)

    share = shard // (chips * cores)
    own = lax.dynamic_slice_in_dim(landmarks, (chip * cores + core) * share, share, 0)
    if plan.split:
        piece = own
    else:
        piece = lax.dynamic_slice_in_dim(landmarks, chip * (shard // chips), shard // chips, 0)
    z = jnp.concatenate(spread_out(piece, "land")[1:], 0)
    far = spread_out(z, "chip")
    x_mine, u = own_cross(landmarks, embeddings)
    if plan.split:
        far, x_mine, u = lax.optimization_barrier((far, x_mine, u))
        for a in range(1, cores):
            far = far + [swap(f, "core", a) for f in far[:chips]]

    na = n // B // 2
    keep, send = local_normal(at, plan, na, embeddings, landmarks, own, u, x_mine, far)
    rows = [r // cores for r in segments(plan, na, n // B)]
    parts = scatter(add_cut(at, 1, chips, rows, [keep, swap(send, "core", 1)]), "chip")
    rows = [r // chips for r in rows]
    parts = scatter(add_cut(at, 0, lands, rows, parts), "land")
    rows = [r // lands for r in rows]
    (whole,) = add_cut(at, 0, 1, rows, parts)
    first, last = place(at, 0, rows, spread_out(whole, "land"))
    first = spread_out(first, "chip")
    first, last = lax.optimization_barrier((first + [swap(p, "core", 1) for p in first], last))
    f, w = first_factor(at, plan, na, first)
    last, f, w = lax.optimization_barrier((spread_out(last, "chip"), f, w))
    last = last + [swap(p, "core", 1) for p in last]
    return last_factor(at, plan, n, f, w, last)


def solution(mesh):
    land, rows = mesh.axis_names
    cores = 2
    fine = Mesh(mesh.devices.reshape(mesh.shape[land], mesh.shape[rows] // cores, cores), ("land", "chip", "core"))
    in_specs = (P(("land", "chip", "core"), None), P("land", None))
    return jax.shard_map(shards, mesh=fine, in_specs=in_specs, out_specs=P(), check_vma=False)
```

```python
import functools
import math
import typing

import jax
import jax.numpy as jnp
from jax import lax
from jax.experimental import pallas as pl
from jax.experimental.pallas import tpu as pltpu
from jax.sharding import Mesh
from jax.sharding import PartitionSpec as P

LAYERS = 6
SCALE_SQ = 1.0 / 32.0
RIDGE = 0.1
EPS = 1e-06
B = 128
HALF = 64
CLIP = 1.0 - 2.0**-24

ARC = (0.9426497266634519, 0.04833294295062493, 0.004716300148249888, 0.004298816276929029)
KEEP = 1.0 / (1.0 + SCALE_SQ)
ARC = tuple(c * SCALE_SQ * KEEP / math.pi for c in ARC)
GROWTH = (1.0 + SCALE_SQ) ** LAYERS


def recursion(c):
    c = jnp.clip(c, -CLIP, CLIP)
    for _ in range(LAYERS):
        w = 1.0 - jnp.abs(c)
        t = (w * w) * lax.rsqrt(w)
        poly = ARC[3]
        for a in ARC[2::-1]:
            poly = poly * w + a
        c = jnp.maximum(c, KEEP * c) + t * poly
    return c


def nt(a, b):
    return lax.dot_general(a, b, (((1,), (1,)), ((), ())), preferred_element_type=jnp.float32)


def lane_tiles_of_squares(x):
    total = None
    for l in range(0, x.shape[1], B):
        wide = x[:, l : l + B].astype(jnp.float32)
        total = wide * wide if total is None else total + wide * wide
    return total


def squares_mean_column(x):
    total = jnp.sum(lane_tiles_of_squares(x), axis=1, keepdims=True)
    return jnp.broadcast_to(total * (1.0 / x.shape[1]) + EPS, (x.shape[0], B))


def squares_mean_row(x):
    total = lane_tiles_of_squares(x)
    rows = [jnp.sum(total[i : i + B].T, axis=0, keepdims=True) for i in range(0, x.shape[0], B)]
    row = jnp.concatenate(rows, axis=1) * (1.0 / x.shape[1]) + EPS
    return jnp.broadcast_to(row, (8, x.shape[0]))


def spread(column, lanes):
    return jnp.concatenate([column] * (lanes // B), axis=1)


CHUNK = 16


def fill_cross(marks_ref, emb_ref, u_ref, k_ref, vq_ref, x_ref, x_row):
    m, e = emb_ref.shape
    k_ref[...] = nt(marks_ref[...], emb_ref[...])
    vq_ref[...] = squares_mean_column(marks_ref[...])

    def part(i, _):
        r = pl.multiple_of(i * CHUNK, CHUNK)
        vq = vq_ref[pl.ds(r, CHUNK), :]
        v_inv = lax.rsqrt(vq)
        v_root = vq * v_inv
        up = jnp.concatenate([u_ref[:8, :]] * (CHUNK // 8), axis=0)
        ur = jnp.concatenate([u_ref[8:, :]] * (CHUNK // 8), axis=0)
        c = recursion(k_ref[pl.ds(r, CHUNK), :] * up * spread(v_inv * (1.0 / e), m))
        x_ref[pl.ds(x_row(r), CHUNK), :] = (c * ur * spread(v_root * GROWTH, m)).astype(jnp.bfloat16)
        return 0

    lax.fori_loop(0, marks_ref.shape[0] // CHUNK, part, 0)


def own_kernel(marks_ref, emb_ref, x_ref, u_ref, k_ref, vq_ref):
    uq = squares_mean_row(emb_ref[...])
    inv = lax.rsqrt(uq)
    u_ref[:8, :] = inv
    u_ref[8:, :] = uq * inv
    fill_cross(marks_ref, emb_ref, u_ref, k_ref, vq_ref, x_ref, lambda r: r)


def own_rest_kernel(marks_ref, emb_ref, u_ref, x_ref, k_ref, vq_ref):
    fill_cross(marks_ref, emb_ref, u_ref, k_ref, vq_ref, x_ref, lambda r: r)


def own_cross(landmarks, embeddings, u=None):
    m = embeddings.shape[0]
    rows = landmarks.shape[0]
    vmem = pl.BlockSpec(memory_space=pltpu.VMEM)
    x_shape = jax.ShapeDtypeStruct((rows, m), jnp.bfloat16)
    u_shape = jax.ShapeDtypeStruct((16, m), jnp.float32)
    given = () if u is None else (u,)
    return pl.pallas_call(
        own_rest_kernel if given else own_kernel,
        out_shape=x_shape if given else (x_shape, u_shape),
        in_specs=[vmem] * (2 + len(given)),
        out_specs=vmem if given else (vmem, vmem),
        scratch_shapes=[pltpu.VMEM((rows, m), jnp.float32), pltpu.VMEM((rows, B), jnp.float32)],
        compiler_params=pltpu.CompilerParams(vmem_limit_bytes=12 << 20),
        name="own_cross",
    )(landmarks, embeddings, *given)


class Plan(typing.NamedTuple):
    lands: int
    chips: int
    cores: int
    split: bool
    all_points: int


def gram_kernel(plan, na, at_ref, emb_ref, mine_ref, own_ref, u_ref, x_upper_ref, x_lower_ref, *refs):
    lands, chips, cores, split, all_points = plan
    count = chips * (cores if split else 1)
    far = refs[:count]
    keep_ref, send_ref, x_ref, ridge_ref, marks_ref, k_ref, vq_ref, out_ref = refs[count:]
    shard, e = mine_ref.shape
    n = shard * lands
    land, chip, core = at_ref[0], at_ref[1], at_ref[2]
    here = pl.multiple_of(land * shard, shard)
    x_ref[pl.ds(here, shard // 2), :] = x_upper_ref[...]
    x_ref[pl.ds(pl.multiple_of(here + shard // 2, CHUNK), shard // 2), :] = x_lower_ref[...]
    piece = far[0].shape[0] // (lands - 1)
    for a in range(cores if split else 1):
        for t in range(chips):
            slot = ((chip ^ t) * cores + (core ^ a)) if split else (chip ^ t)
            for s in range(1, lands):
                to = pl.multiple_of((s - 1) * shard + slot * piece, piece)
                marks_ref[pl.ds(to, piece), :] = far[a * chips + t][(s - 1) * piece : s * piece, :]

    def x_row(r):
        s = r // shard + 1
        return pl.multiple_of((land ^ s) * shard + r % shard, CHUNK)

    fill_cross(marks_ref, emb_ref, u_ref, k_ref, vq_ref, x_ref, x_row)

    share = own_ref.shape[0]
    oq = squares_mean_column(own_ref[...])
    o_inv = lax.rsqrt(oq)

    def ridge(marks, marks_q, to):
        k_own = nt(own_ref[...], marks)
        for l in range(0, shard, B):
            vq = marks_q[l : l + B].T[:8]
            v_inv = lax.rsqrt(vq)
            for i in range(share // 8):
                oi = o_inv[8 * i : 8 * i + 8]
                c = recursion(k_own[8 * i : 8 * i + 8, l : l + B] * v_inv * (oi * (1.0 / e)))
                root = oq[8 * i : 8 * i + 8] * oi
                ridge_ref[8 * i : 8 * i + 8, pl.ds(to + l, B)] = c * (vq * v_inv) * (root * (RIDGE * GROWTH))

    ridge(mine_ref[...], squares_mean_column(mine_ref[...]), here)
    for s in range(1, lands):
        rows = slice((s - 1) * shard, s * shard)
        ridge(marks_ref[rows, :], vq_ref[rows, :], pl.multiple_of((land ^ s) * shard, shard))

    position = land * shard + (chip * cores + core) * share
    row_block = position // B
    offset = position % B
    wide = 2 * B
    for w in range(n // wide):
        both = nt(x_ref[: (w + 1) * wide, :], x_ref[w * wide : (w + 1) * wide, :]) * (1.0 / all_points)
        for j in (2 * w, 2 * w + 1):
            start = column_start(plan, na, j)
            out_ref[start : start + (j + 1) * B, :] = both[: (j + 1) * B, (j % 2) * B : (j % 2 + 1) * B]
    for j in range(n // B):
        start = column_start(plan, na, j)

        @pl.when(row_block <= j)
        def _():
            at = pl.ds(pl.multiple_of(start + row_block * B + offset, share), share)
            out_ref[at, :] = out_ref[at, :] + ridge_ref[:, j * B : (j + 1) * B]

    done = base = 0
    for rows in segments(plan, na, n // B):
        half = rows // cores
        to = slice(done, done + half)
        keep_ref[to, :] = out_ref[pl.ds(pl.multiple_of(base + core * half, 8), half), :]
        send_ref[to, :] = out_ref[pl.ds(pl.multiple_of(base + (1 - core) * half, 8), half), :]
        done, base = done + half, base + rows


def packed_start(j):
    return j * (j + 1) // 2 * B


def segments(plan, na, nb):
    unit = 8 * plan.lands * plan.chips * plan.cores
    return [-(-rows // unit) * unit for rows in (packed_start(na), packed_start(nb) - packed_start(na))]


def column_start(plan, na, j):
    return packed_start(j) if j < na else packed_start(j) - packed_start(na) + segments(plan, na, j)[0]


def local_normal(at, plan, na, embeddings, landmarks, own, u, x_upper, x_lower, far):
    n, m = landmarks.shape[0] * plan.lands, embeddings.shape[0]
    away = n - landmarks.shape[0]
    rows = sum(segments(plan, na, n // B))
    half = jax.ShapeDtypeStruct((rows // plan.cores, B), jnp.float32)
    vmem = pl.BlockSpec(memory_space=pltpu.VMEM)
    return pl.pallas_call(
        functools.partial(gram_kernel, plan, na),
        out_shape=(half, half),
        in_specs=[pl.BlockSpec(memory_space=pltpu.SMEM)] + [vmem] * (6 + len(far)),
        out_specs=(vmem,) * 2,
        scratch_shapes=[
            pltpu.VMEM((n, m), jnp.bfloat16),
            pltpu.VMEM((own.shape[0], n), jnp.float32),
            pltpu.VMEM((away, landmarks.shape[1]), jnp.bfloat16),
            pltpu.VMEM((away, m), jnp.float32),
            pltpu.VMEM((away, B), jnp.float32),
            pltpu.VMEM((rows, B), jnp.float32),
        ],
        compiler_params=pltpu.CompilerParams(vmem_limit_bytes=24 << 20),
        name="gram",
    )(at, embeddings, landmarks, own, u, x_upper, x_lower, *far)


def add_cut_kernel(ways, axis, parts, at_ref, *refs):
    ins, outs = refs[: len(refs) - ways], refs[len(refs) - ways :]
    base = 0
    for rows in parts:
        h = rows // ways
        for q in range(ways):
            s = -q % ways
            at = pl.ds(pl.multiple_of(base + (at_ref[axis] ^ s) * h, 8), h) if ways > 1 else slice(base, base + h)
            total = ins[0][at, :]
            for r in ins[1:]:
                total = total + r[at, :]
            outs[q][base // ways : base // ways + h, :] = total
        base += rows


def add_cut(at, axis, ways, parts, ins):
    h = sum(parts) // ways
    vmem = pl.BlockSpec(memory_space=pltpu.VMEM)
    return pl.pallas_call(
        functools.partial(add_cut_kernel, ways, axis, parts),
        out_shape=tuple([jax.ShapeDtypeStruct((h, B), jnp.float32)] * ways),
        in_specs=[pl.BlockSpec(memory_space=pltpu.SMEM)] + [vmem] * len(ins),
        out_specs=tuple([vmem] * ways),
        compiler_params=pltpu.CompilerParams(vmem_limit_bytes=8 << 20),
        name="add_cut",
    )(at, *ins)


def place_kernel(axis, ways, parts, at_ref, *refs):
    ins, outs = refs[:ways], refs[ways:]
    base = 0
    for out, h in zip(outs, parts):
        for s in range(ways):
            out[pl.ds(pl.multiple_of((at_ref[axis] ^ s) * h, 8), h), :] = ins[s][base : base + h, :]
        base += h


def place(at, axis, parts, ins):
    vmem = pl.BlockSpec(memory_space=pltpu.VMEM)
    return pl.pallas_call(
        functools.partial(place_kernel, axis, len(ins), parts),
        out_shape=tuple(jax.ShapeDtypeStruct((h * len(ins), B), jnp.float32) for h in parts),
        in_specs=[pl.BlockSpec(memory_space=pltpu.SMEM)] + [vmem] * len(ins),
        out_specs=(vmem,) * len(parts),
        compiler_params=pltpu.CompilerParams(vmem_limit_bytes=8 << 20),
        name="place",
    )(at, *ins)


def thirds(x):
    h = x.astype(jnp.bfloat16)
    r = x - h.astype(jnp.float32)
    m = r.astype(jnp.bfloat16)
    return h, m, (r - m.astype(jnp.float32)).astype(jnp.bfloat16)

def left_terms(x, axis):
    h, m, l = thirds(x)
    return jnp.concatenate([h, h, h, m, m, l], axis)

def right_terms(x, axis):
    h, m, l = thirds(x)
    return jnp.concatenate([h, m, l, h, m, h], axis)

def dot32(a, b):
    return lax.dot_general(left_terms(a, 1), right_terms(b, 0), (((1,), (0,)), ((), ())), preferred_element_type=jnp.float32)

def dot32_t(a, b):
    return dot32(a.T, b)

def factor_block(d):
    row8 = lax.broadcasted_iota(jnp.int32, (8, B), 0)
    eye = (lax.broadcasted_iota(jnp.int32, (B, B), 0) == lax.broadcasted_iota(jnp.int32, (B, B), 1)).astype(jnp.float32)
    left = [d[i : i + 8] for i in range(0, B, 8)]
    right = [eye[i : i + 8] for i in range(0, B, 8)]
    zero = left[0] * 0.0
    half = HALF // 8

    def spread_columns(x, lane):
        columns = [jnp.broadcast_to(x[:, lane + i : lane + i + 1], (8, B)) for i in range(8)]
        return [columns[0] + zero] + columns[1:]

    def splat(x, r):
        return jnp.broadcast_to(x[r : r + 1], (8, B))

    for start in range(0, B // 8, half):
        end = start + half
        diag = spread_columns(left[start], 8 * start)
        for p in range(start, end):
            col = {r: spread_columns(left[r], 8 * p) for r in range(p + 1, end)}
            after = spread_columns(left[p + 1], 8 * p + 8) if p + 1 < end else None
            pivots = jnp.ones((8, B), jnp.float32)
            for j in range(8):
                pivot = splat(diag[j], j)
                pivots = jnp.where(row8 == j, pivot, pivots)
                inv = 1.0 / pivot
                coef = {i: splat(diag[j], i) for i in range(j + 1, 8)}
                for i in coef:
                    diag[i] = diag[i] - (diag[j] * coef[i]) * inv
                rl, rr = splat(left[p], j), splat(right[p], j)
                if j < 7:
                    c = jnp.where(row8 > j, diag[j] * inv, 0.0)
                    left[p] = left[p] - c * rl
                    right[p] = right[p] - c * rr
                for r in col:
                    c = col[r][j] * inv
                    if r == p + 1:
                        for i in range(8):
                            after[i] = after[i] - c * splat(col[r][j], i)
                    for i in coef:
                        col[r][i] = col[r][i] - c * coef[i]
                    left[r] = left[r] - c * rl
                    right[r] = right[r] - c * rr
            s = lax.rsqrt(pivots)
            left[p] = left[p] * s
            right[p] = right[p] * s
            diag = after
        if end < B // 8:
            ul = jnp.concatenate(left[start:end], 0)
            u = jnp.concatenate([ul, jnp.concatenate(right[start:end], 0)], 1)
            upd = dot32_t(ul, u)
            for r in range(end, B // 8):
                left[r] = left[r] - upd[8 * r : 8 * r + 8, :B]
                right[r] = right[r] - upd[8 * r : 8 * r + 8, B:]
    tri = lax.broadcasted_iota(jnp.int32, (B, B), 0) <= lax.broadcasted_iota(jnp.int32, (B, B), 1)
    return jnp.where(tri, jnp.concatenate(left, 0), 0.0), jnp.concatenate(right, 0)


def eliminate(nb, m_ref, d_ref, r_ref, store):
    lane_block = lax.broadcasted_iota(jnp.int32, (B, nb * B), 1) // B
    d_ref[...] = m_ref[:B, :B]
    r_ref[...] = jnp.zeros_like(r_ref)

    def step(k, _):
        u, w = factor_block(d_ref[...])
        prev = r_ref[...]
        m_ref[...] = m_ref[...] - dot32_t(prev, prev)
        row = dot32(w, m_ref[pl.ds(pl.multiple_of(k * B, B), B), :])
        row = jnp.where(lane_block > k, row, 0.0)
        r_ref[...] = row
        nxt = pl.multiple_of(jnp.minimum(k + 1, nb - 1) * B, B)
        rn = r_ref[:, pl.ds(nxt, B)]
        d_ref[...] = m_ref[pl.ds(nxt, B), pl.ds(nxt, B)] - dot32_t(rn, rn)
        store(pl.multiple_of(k * B, B), row, u, w)
        return 0

    lax.fori_loop(0, nb, step, 0)


def place_parts(plan, at_ref, parts, a_ref):
    h = parts[0].shape[0]
    for a in range(plan.cores):
        for t in range(plan.chips):
            slot = (at_ref[2] ^ a) * plan.chips + (at_ref[1] ^ t)
            a_ref[pl.ds(pl.multiple_of(slot * h, h), h), :] = parts[a * plan.chips + t][...]


def first_factor_kernel(plan, at_ref, *refs):
    count = plan.chips * plan.cores
    f_ref, w_ref, a_ref, m_ref, d_ref, r_ref = refs[count:]
    na = f_ref.shape[0] // B
    place_parts(plan, at_ref, refs[:count], a_ref)
    for j in range(na):
        m_ref[: (j + 1) * B, j * B : (j + 1) * B] = a_ref[packed_start(j) : packed_start(j) + (j + 1) * B, :]

    def store(at, row, u, w):
        f_ref[pl.ds(at, B), :] = row
        f_ref[pl.ds(at, B), pl.ds(at, B)] = u
        w_ref[pl.ds(at, B), :] = w

    eliminate(na, m_ref, d_ref, r_ref, store)


def first_factor(at, plan, na, parts):
    vmem = pl.BlockSpec(memory_space=pltpu.VMEM)
    return pl.pallas_call(
        functools.partial(first_factor_kernel, plan),
        out_shape=(
            jax.ShapeDtypeStruct((na * B, na * B), jnp.float32),
            jax.ShapeDtypeStruct((na * B, B), jnp.float32),
        ),
        in_specs=[pl.BlockSpec(memory_space=pltpu.SMEM)] + [vmem] * len(parts),
        out_specs=(vmem,) * 2,
        scratch_shapes=[
            pltpu.VMEM((parts[0].shape[0] * len(parts), B), jnp.float32),
            pltpu.VMEM((na * B, na * B), jnp.float32),
            pltpu.VMEM((B, B), jnp.float32),
            pltpu.VMEM((B, na * B), jnp.float32),
        ],
        compiler_params=pltpu.CompilerParams(vmem_limit_bytes=16 << 20),
        name="chol_first",
    )(at, *parts)


def last_factor_kernel(plan, at_ref, f_ref, w_ref, *refs):
    count = plan.chips * plan.cores
    o_ref, a_ref, t_ref, m_ref, d_ref, r_ref = refs[count:]
    n, top = o_ref.shape[0] // B, f_ref.shape[0]
    na = top // B
    place_parts(plan, at_ref, refs[:count], a_ref)
    for j in range(na, n):
        start = packed_start(j) - packed_start(na)
        lanes = slice((j - na) * B, (j - na + 1) * B)
        t_ref[:, lanes] = a_ref[start : start + top, :]
        m_ref[: (j - na + 1) * B, lanes] = a_ref[start + top : start + (j + 1) * B, :]
    o_ref[:top, :top] = f_ref[...]
    o_ref[top:, :top] = jnp.zeros((n * B - top, top), jnp.float32)
    for k in range(na):
        rows = slice(k * B, (k + 1) * B)
        row = dot32(w_ref[rows, :], t_ref[rows, :])
        o_ref[rows, top:] = row
        if k < na - 1:
            t_ref[(k + 1) * B :, :] = t_ref[(k + 1) * B :, :] - dot32_t(f_ref[rows, (k + 1) * B :], row)
        m_ref[...] = m_ref[...] - dot32_t(row, row)

    def store(at, row, u, w):
        down = pl.multiple_of(top + at, B)
        o_ref[pl.ds(down, B), top:] = row
        o_ref[pl.ds(down, B), pl.ds(down, B)] = u

    eliminate(n - na, m_ref, d_ref, r_ref, store)


def last_factor(at, plan, n, f, w, parts):
    vmem = pl.BlockSpec(memory_space=pltpu.VMEM)
    top = f.shape[0]
    return pl.pallas_call(
        functools.partial(last_factor_kernel, plan),
        out_shape=jax.ShapeDtypeStruct((n, n), jnp.float32),
        in_specs=[pl.BlockSpec(memory_space=pltpu.SMEM)] + [vmem] * (2 + len(parts)),
        out_specs=vmem,
        scratch_shapes=[
            pltpu.VMEM((parts[0].shape[0] * len(parts), B), jnp.float32),
            pltpu.VMEM((top, n - top), jnp.float32),
            pltpu.VMEM((n - top, n - top), jnp.float32),
            pltpu.VMEM((B, B), jnp.float32),
            pltpu.VMEM((B, n - top), jnp.float32),
        ],
        compiler_params=pltpu.CompilerParams(vmem_limit_bytes=24 << 20),
        name="chol_last",
    )(at, f, w, *parts)


def swap(x, axis, s):
    return lax.ppermute(x, axis, [(i, i ^ s) for i in range(lax.axis_size(axis))])


def scatter(pieces, axis):
    return [pieces[0]] + [swap(p, axis, -q % len(pieces)) for q, p in enumerate(pieces) if q]


def spread_out(x, axis):
    return [x] + [swap(x, axis, s) for s in range(1, lax.axis_size(axis))]


def shards(embeddings, landmarks):
    lands, chips, cores = (lax.axis_size(a) for a in ("land", "chip", "core"))
    land, chip, core = (lax.axis_index(a) for a in ("land", "chip", "core"))
    at = jnp.stack([land, chip, core]).astype(jnp.int32)
    shard = landmarks.shape[0]
    n = shard * lands
    plan = Plan(lands, chips, cores, shard // (chips * cores) % 16 == 0, embeddings.shape[0] * lands * chips * cores)

    share = shard // (chips * cores)
    own = lax.dynamic_slice_in_dim(landmarks, (chip * cores + core) * share, share, 0)
    if plan.split:
        piece = own
    else:
        piece = lax.dynamic_slice_in_dim(landmarks, chip * (shard // chips), shard // chips, 0)
    x_upper, u = own_cross(landmarks[: shard // 2], embeddings)
    z, x_upper, u = lax.optimization_barrier((spread_out(piece, "land")[1:], x_upper, u))
    far = spread_out(jnp.concatenate(z, 0), "chip")
    x_lower = own_cross(landmarks[shard // 2 :], embeddings, u)
    far, x_lower = lax.optimization_barrier((far, x_lower))
    if plan.split:
        for a in range(1, cores):
            far = far + [swap(f, "core", a) for f in far[:chips]]

    na = n // B // 2
    keep, send = local_normal(at, plan, na, embeddings, landmarks, own, u, x_upper, x_lower, far)
    rows = [r // cores for r in segments(plan, na, n // B)]
    parts = scatter(add_cut(at, 1, chips, rows, [keep, swap(send, "core", 1)]), "chip")
    rows = [r // chips for r in rows]
    parts = scatter(add_cut(at, 0, lands, rows, parts), "land")
    rows = [r // lands for r in rows]
    (whole,) = add_cut(at, 0, 1, rows, parts)
    first, last = place(at, 0, rows, spread_out(whole, "land"))
    first = spread_out(first, "chip")
    first, last = lax.optimization_barrier((first + [swap(p, "core", 1) for p in first], last))
    f, w = first_factor(at, plan, na, first)
    last, f, w = lax.optimization_barrier((spread_out(last, "chip"), f, w))
    last = last + [swap(p, "core", 1) for p in last]
    return last_factor(at, plan, n, f, w, last)


def solution(mesh):
    land, rows = mesh.axis_names
    cores = 2
    fine = Mesh(mesh.devices.reshape(mesh.shape[land], mesh.shape[rows] // cores, cores), ("land", "chip", "core"))
    in_specs = (P(("land", "chip", "core"), None), P("land", None))
    return jax.shard_map(shards, mesh=fine, in_specs=in_specs, out_specs=P(), check_vma=False)
```

```python
import functools
import math
import typing

import jax
import jax.numpy as jnp
from jax import lax
from jax.experimental import pallas as pl
from jax.experimental.pallas import tpu as pltpu
from jax.sharding import Mesh
from jax.sharding import PartitionSpec as P

LAYERS = 6
SCALE_SQ = 1.0 / 32.0
RIDGE = 0.1
EPS = 1e-06
B = 128
HALF = 64
CLIP = 1.0 - 2.0**-24

ARC = (0.9426497266634519, 0.04833294295062493, 0.004716300148249888, 0.004298816276929029)
KEEP = 1.0 / (1.0 + SCALE_SQ)
ARC = tuple(c * SCALE_SQ * KEEP / math.pi for c in ARC)
GROWTH = (1.0 + SCALE_SQ) ** LAYERS


def recursion(c):
    c = jnp.clip(c, -CLIP, CLIP)
    for _ in range(LAYERS):
        w = 1.0 - jnp.abs(c)
        t = (w * w) * lax.rsqrt(w)
        poly = ARC[3]
        for a in ARC[2::-1]:
            poly = poly * w + a
        c = jnp.maximum(c, KEEP * c) + t * poly
    return c


def nt(a, b):
    return lax.dot_general(a, b, (((1,), (1,)), ((), ())), preferred_element_type=jnp.float32)


def lane_tiles_of_squares(x):
    total = None
    for l in range(0, x.shape[1], B):
        wide = x[:, l : l + B].astype(jnp.float32)
        total = wide * wide if total is None else total + wide * wide
    return total


def squares_mean_column(x):
    total = jnp.sum(lane_tiles_of_squares(x), axis=1, keepdims=True)
    return jnp.broadcast_to(total * (1.0 / x.shape[1]) + EPS, (x.shape[0], B))


def squares_mean_row(x):
    total = lane_tiles_of_squares(x)
    rows = [jnp.sum(total[i : i + B].T, axis=0, keepdims=True) for i in range(0, x.shape[0], B)]
    row = jnp.concatenate(rows, axis=1) * (1.0 / x.shape[1]) + EPS
    return jnp.broadcast_to(row, (8, x.shape[0]))


def spread(column, lanes):
    return jnp.concatenate([column] * (lanes // B), axis=1)


CHUNK = 16


def fill_cross(marks_ref, emb_ref, u_ref, k_ref, vq_ref, x_ref, chunks, rows_of):
    m, e = emb_ref.shape
    rows = marks_ref.shape[0]
    k_ref[:rows, :] = nt(marks_ref[...], emb_ref[...])
    vq_ref[:rows, :] = squares_mean_column(marks_ref[...])

    def part(i, _):
        r, to = (pl.multiple_of(at, CHUNK) for at in rows_of(i))
        vq = vq_ref[pl.ds(r, CHUNK), :]
        v_inv = lax.rsqrt(vq)
        v_root = vq * v_inv
        up = jnp.concatenate([u_ref[:8, :]] * (CHUNK // 8), axis=0)
        ur = jnp.concatenate([u_ref[8:, :]] * (CHUNK // 8), axis=0)
        c = recursion(k_ref[pl.ds(r, CHUNK), :] * up * spread(v_inv * (1.0 / e), m))
        x_ref[pl.ds(to, CHUNK), :] = (c * ur * spread(v_root * GROWTH, m)).astype(jnp.bfloat16)
        return 0

    lax.fori_loop(0, chunks, part, 0)


def in_order(i):
    return i * CHUNK, i * CHUNK


def own_kernel(marks_ref, emb_ref, x_ref, u_ref, k_ref, vq_ref):
    uq = squares_mean_row(emb_ref[...])
    inv = lax.rsqrt(uq)
    u_ref[:8, :] = inv
    u_ref[8:, :] = uq * inv
    fill_cross(marks_ref, emb_ref, u_ref, k_ref, vq_ref, x_ref, x_ref.shape[0] // CHUNK, in_order)


def own_cross(landmarks, embeddings):
    m = embeddings.shape[0]
    rows = landmarks.shape[0]
    vmem = pl.BlockSpec(memory_space=pltpu.VMEM)
    return pl.pallas_call(
        own_kernel,
        out_shape=(jax.ShapeDtypeStruct((rows, m), jnp.bfloat16), jax.ShapeDtypeStruct((16, m), jnp.float32)),
        in_specs=[vmem] * 2,
        out_specs=(vmem, vmem),
        scratch_shapes=[pltpu.VMEM((rows, m), jnp.float32), pltpu.VMEM((rows, B), jnp.float32)],
        compiler_params=pltpu.CompilerParams(vmem_limit_bytes=12 << 20),
        name="own_cross",
    )(landmarks, embeddings)


def next_kernel(marks_ref, slices_ref, emb_ref, u_ref, x_ref, x_slices_ref, k_ref, vq_ref):
    for m_ref, to_ref in ((marks_ref, x_ref), (slices_ref, x_slices_ref)):
        fill_cross(m_ref, emb_ref, u_ref, k_ref, vq_ref, to_ref, to_ref.shape[0] // CHUNK, in_order)


def next_cross(landmarks, slices, embeddings, u):
    m = embeddings.shape[0]
    rows = max(landmarks.shape[0], slices.shape[0])
    vmem = pl.BlockSpec(memory_space=pltpu.VMEM)
    return pl.pallas_call(
        next_kernel,
        out_shape=tuple(jax.ShapeDtypeStruct((x.shape[0], m), jnp.bfloat16) for x in (landmarks, slices)),
        in_specs=[vmem] * 4,
        out_specs=(vmem, vmem),
        scratch_shapes=[pltpu.VMEM((rows, m), jnp.float32), pltpu.VMEM((rows, B), jnp.float32)],
        compiler_params=pltpu.CompilerParams(vmem_limit_bytes=12 << 20),
        name="next_cross",
    )(landmarks, slices, embeddings, u)


class Plan(typing.NamedTuple):
    lands: int
    chips: int
    cores: int
    split: bool
    all_points: int


def gram_kernel(plan, na, at_ref, emb_ref, mine_ref, own_ref, u_ref, x_upper_ref, x_lower_ref, x_slices_ref, *refs):
    lands, chips, cores, split, all_points = plan
    count = chips * (cores if split else 1)
    far = refs[:count]
    keep_ref, send_ref, x_ref, ridge_ref, marks_ref, k_ref, vq_ref, out_ref = refs[count:]
    shard, e = mine_ref.shape
    n = shard * lands
    land, chip, core = at_ref[0], at_ref[1], at_ref[2]
    here = pl.multiple_of(land * shard, shard)
    x_ref[pl.ds(here, shard // 2), :] = x_upper_ref[...]
    x_ref[pl.ds(pl.multiple_of(here + shard // 2, CHUNK), shard // 2), :] = x_lower_ref[...]
    piece = far[0].shape[0] // (lands - 1)
    for a in range(cores if split else 1):
        for t in range(chips):
            slot = ((chip ^ t) * cores + (core ^ a)) if split else (chip ^ t)
            for s in range(1, lands):
                to = pl.multiple_of((s - 1) * shard + slot * piece, piece)
                marks_ref[pl.ds(to, piece), :] = far[a * chips + t][(s - 1) * piece : s * piece, :]

    slots = shard // piece
    mine = chip * cores + core if split else chip
    for s in range(1, lands):
        to = pl.multiple_of((land ^ s) * shard + mine * piece, piece)
        x_ref[pl.ds(to, piece), :] = x_slices_ref[(s - 1) * piece : s * piece, :]
    steps = piece // CHUNK

    def rows_of(i):
        s, rest = i // ((slots - 1) * steps), i % ((slots - 1) * steps)
        at = (mine ^ (rest // steps + 1)) * piece + rest % steps * CHUNK
        return s * shard + at, (land ^ (s + 1)) * shard + at

    fill_cross(marks_ref, emb_ref, u_ref, k_ref, vq_ref, x_ref, (lands - 1) * (slots - 1) * steps, rows_of)

    share = own_ref.shape[0]
    oq = squares_mean_column(own_ref[...])
    o_inv = lax.rsqrt(oq)

    def ridge(marks, marks_q, to):
        k_own = nt(own_ref[...], marks)
        for l in range(0, shard, B):
            vq = marks_q[l : l + B].T[:8]
            v_inv = lax.rsqrt(vq)
            for i in range(share // 8):
                oi = o_inv[8 * i : 8 * i + 8]
                c = recursion(k_own[8 * i : 8 * i + 8, l : l + B] * v_inv * (oi * (1.0 / e)))
                root = oq[8 * i : 8 * i + 8] * oi
                ridge_ref[8 * i : 8 * i + 8, pl.ds(to + l, B)] = c * (vq * v_inv) * (root * (RIDGE * GROWTH))

    ridge(mine_ref[...], squares_mean_column(mine_ref[...]), here)
    for s in range(1, lands):
        rows = slice((s - 1) * shard, s * shard)
        ridge(marks_ref[rows, :], vq_ref[rows, :], pl.multiple_of((land ^ s) * shard, shard))

    position = land * shard + (chip * cores + core) * share
    row_block = position // B
    offset = position % B
    wide = 2 * B
    for w in range(n // wide):
        both = nt(x_ref[: (w + 1) * wide, :], x_ref[w * wide : (w + 1) * wide, :]) * (1.0 / all_points)
        for j in (2 * w, 2 * w + 1):
            start = column_start(plan, na, j)
            out_ref[start : start + (j + 1) * B, :] = both[: (j + 1) * B, (j % 2) * B : (j % 2 + 1) * B]
    for j in range(n // B):
        start = column_start(plan, na, j)

        @pl.when(row_block <= j)
        def _():
            at = pl.ds(pl.multiple_of(start + row_block * B + offset, share), share)
            out_ref[at, :] = out_ref[at, :] + ridge_ref[:, j * B : (j + 1) * B]

    done = base = 0
    for rows in segments(plan, na, n // B):
        half = rows // cores
        to = slice(done, done + half)
        keep_ref[to, :] = out_ref[pl.ds(pl.multiple_of(base + core * half, 8), half), :]
        send_ref[to, :] = out_ref[pl.ds(pl.multiple_of(base + (1 - core) * half, 8), half), :]
        done, base = done + half, base + rows


def packed_start(j):
    return j * (j + 1) // 2 * B


def segments(plan, na, nb):
    unit = 8 * plan.lands * plan.chips * plan.cores
    return [-(-rows // unit) * unit for rows in (packed_start(na), packed_start(nb) - packed_start(na))]


def column_start(plan, na, j):
    return packed_start(j) if j < na else packed_start(j) - packed_start(na) + segments(plan, na, j)[0]


def local_normal(at, plan, na, embeddings, landmarks, own, u, x_upper, x_lower, x_slices, far):
    n, m = landmarks.shape[0] * plan.lands, embeddings.shape[0]
    away = n - landmarks.shape[0]
    rows = sum(segments(plan, na, n // B))
    half = jax.ShapeDtypeStruct((rows // plan.cores, B), jnp.float32)
    vmem = pl.BlockSpec(memory_space=pltpu.VMEM)
    return pl.pallas_call(
        functools.partial(gram_kernel, plan, na),
        out_shape=(half, half),
        in_specs=[pl.BlockSpec(memory_space=pltpu.SMEM)] + [vmem] * (7 + len(far)),
        out_specs=(vmem,) * 2,
        scratch_shapes=[
            pltpu.VMEM((n, m), jnp.bfloat16),
            pltpu.VMEM((own.shape[0], n), jnp.float32),
            pltpu.VMEM((away, landmarks.shape[1]), jnp.bfloat16),
            pltpu.VMEM((away, m), jnp.float32),
            pltpu.VMEM((away, B), jnp.float32),
            pltpu.VMEM((rows, B), jnp.float32),
        ],
        compiler_params=pltpu.CompilerParams(vmem_limit_bytes=24 << 20),
        name="gram",
    )(at, embeddings, landmarks, own, u, x_upper, x_lower, x_slices, *far)


def add_cut_kernel(ways, axis, parts, at_ref, *refs):
    ins, outs = refs[: len(refs) - ways], refs[len(refs) - ways :]
    base = 0
    for rows in parts:
        h = rows // ways
        for q in range(ways):
            s = -q % ways
            at = pl.ds(pl.multiple_of(base + (at_ref[axis] ^ s) * h, 8), h) if ways > 1 else slice(base, base + h)
            total = ins[0][at, :]
            for r in ins[1:]:
                total = total + r[at, :]
            outs[q][base // ways : base // ways + h, :] = total
        base += rows


def add_cut(at, axis, ways, parts, ins):
    h = sum(parts) // ways
    vmem = pl.BlockSpec(memory_space=pltpu.VMEM)
    return pl.pallas_call(
        functools.partial(add_cut_kernel, ways, axis, parts),
        out_shape=tuple([jax.ShapeDtypeStruct((h, B), jnp.float32)] * ways),
        in_specs=[pl.BlockSpec(memory_space=pltpu.SMEM)] + [vmem] * len(ins),
        out_specs=tuple([vmem] * ways),
        compiler_params=pltpu.CompilerParams(vmem_limit_bytes=8 << 20),
        name="add_cut",
    )(at, *ins)


def place_kernel(axis, ways, parts, at_ref, *refs):
    ins, outs = refs[:ways], refs[ways:]
    base = 0
    for out, h in zip(outs, parts):
        for s in range(ways):
            out[pl.ds(pl.multiple_of((at_ref[axis] ^ s) * h, 8), h), :] = ins[s][base : base + h, :]
        base += h


def place(at, axis, parts, ins):
    vmem = pl.BlockSpec(memory_space=pltpu.VMEM)
    return pl.pallas_call(
        functools.partial(place_kernel, axis, len(ins), parts),
        out_shape=tuple(jax.ShapeDtypeStruct((h * len(ins), B), jnp.float32) for h in parts),
        in_specs=[pl.BlockSpec(memory_space=pltpu.SMEM)] + [vmem] * len(ins),
        out_specs=(vmem,) * len(parts),
        compiler_params=pltpu.CompilerParams(vmem_limit_bytes=8 << 20),
        name="place",
    )(at, *ins)


def thirds(x):
    h = x.astype(jnp.bfloat16)
    r = x - h.astype(jnp.float32)
    m = r.astype(jnp.bfloat16)
    return h, m, (r - m.astype(jnp.float32)).astype(jnp.bfloat16)

def left_terms(x, axis):
    h, m, l = thirds(x)
    return jnp.concatenate([h, h, h, m, m, l], axis)

def right_terms(x, axis):
    h, m, l = thirds(x)
    return jnp.concatenate([h, m, l, h, m, h], axis)

def dot32(a, b):
    return lax.dot_general(left_terms(a, 1), right_terms(b, 0), (((1,), (0,)), ((), ())), preferred_element_type=jnp.float32)

def dot32_t(a, b):
    return dot32(a.T, b)

def factor_block(d):
    row8 = lax.broadcasted_iota(jnp.int32, (8, B), 0)
    eye = (lax.broadcasted_iota(jnp.int32, (B, B), 0) == lax.broadcasted_iota(jnp.int32, (B, B), 1)).astype(jnp.float32)
    left = [d[i : i + 8] for i in range(0, B, 8)]
    right = [eye[i : i + 8] for i in range(0, B, 8)]
    zero = left[0] * 0.0
    half = HALF // 8

    def spread_columns(x, lane):
        columns = [jnp.broadcast_to(x[:, lane + i : lane + i + 1], (8, B)) for i in range(8)]
        return [columns[0] + zero] + columns[1:]

    def splat(x, r):
        return jnp.broadcast_to(x[r : r + 1], (8, B))

    for start in range(0, B // 8, half):
        end = start + half
        diag = spread_columns(left[start], 8 * start)
        for p in range(start, end):
            col = {r: spread_columns(left[r], 8 * p) for r in range(p + 1, end)}
            after = spread_columns(left[p + 1], 8 * p + 8) if p + 1 < end else None
            pivots = jnp.ones((8, B), jnp.float32)
            for j in range(8):
                pivot = splat(diag[j], j)
                pivots = jnp.where(row8 == j, pivot, pivots)
                inv = 1.0 / pivot
                coef = {i: splat(diag[j], i) for i in range(j + 1, 8)}
                for i in coef:
                    diag[i] = diag[i] - (diag[j] * coef[i]) * inv
                rl, rr = splat(left[p], j), splat(right[p], j)
                if j < 7:
                    c = jnp.where(row8 > j, diag[j] * inv, 0.0)
                    left[p] = left[p] - c * rl
                    right[p] = right[p] - c * rr
                for r in col:
                    c = col[r][j] * inv
                    if r == p + 1:
                        for i in range(8):
                            after[i] = after[i] - c * splat(col[r][j], i)
                    for i in coef:
                        col[r][i] = col[r][i] - c * coef[i]
                    left[r] = left[r] - c * rl
                    right[r] = right[r] - c * rr
            s = lax.rsqrt(pivots)
            left[p] = left[p] * s
            right[p] = right[p] * s
            diag = after
        if end < B // 8:
            ul = jnp.concatenate(left[start:end], 0)
            u = jnp.concatenate([ul, jnp.concatenate(right[start:end], 0)], 1)
            upd = dot32_t(ul, u)
            for r in range(end, B // 8):
                left[r] = left[r] - upd[8 * r : 8 * r + 8, :B]
                right[r] = right[r] - upd[8 * r : 8 * r + 8, B:]
    tri = lax.broadcasted_iota(jnp.int32, (B, B), 0) <= lax.broadcasted_iota(jnp.int32, (B, B), 1)
    return jnp.where(tri, jnp.concatenate(left, 0), 0.0), jnp.concatenate(right, 0)


def eliminate(nb, m_ref, d_ref, r_ref, store):
    lane_block = lax.broadcasted_iota(jnp.int32, (B, nb * B), 1) // B
    d_ref[...] = m_ref[:B, :B]
    r_ref[...] = jnp.zeros_like(r_ref)

    def step(k, _):
        u, w = factor_block(d_ref[...])
        prev = r_ref[...]
        m_ref[...] = m_ref[...] - dot32_t(prev, prev)
        row = dot32(w, m_ref[pl.ds(pl.multiple_of(k * B, B), B), :])
        row = jnp.where(lane_block > k, row, 0.0)
        r_ref[...] = row
        nxt = pl.multiple_of(jnp.minimum(k + 1, nb - 1) * B, B)
        rn = r_ref[:, pl.ds(nxt, B)]
        d_ref[...] = m_ref[pl.ds(nxt, B), pl.ds(nxt, B)] - dot32_t(rn, rn)
        store(k, row, u, w)
        return 0

    lax.fori_loop(0, nb, step, 0)


def place_parts(plan, at_ref, parts, a_ref):
    h = parts[0].shape[0]
    for a in range(plan.cores):
        for t in range(plan.chips):
            slot = (at_ref[2] ^ a) * plan.chips + (at_ref[1] ^ t)
            a_ref[pl.ds(pl.multiple_of(slot * h, h), h), :] = parts[a * plan.chips + t][...]


def first_factor_kernel(plan, at_ref, *refs):
    count = plan.chips * plan.cores
    f_ref, w_ref, a_ref, m_ref, d_ref, r_ref = refs[count:]
    na = f_ref.shape[0] // B
    place_parts(plan, at_ref, refs[:count], a_ref)
    for j in range(na):
        m_ref[: (j + 1) * B, j * B : (j + 1) * B] = a_ref[packed_start(j) : packed_start(j) + (j + 1) * B, :]

    def store(k, row, u, w):
        at = pl.multiple_of(k * B, B)
        f_ref[pl.ds(at, B), :] = row
        f_ref[pl.ds(at, B), pl.ds(at, B)] = u
        w_ref[pl.ds(at, B), :] = w

    eliminate(na, m_ref, d_ref, r_ref, store)


def first_factor(at, plan, na, parts):
    vmem = pl.BlockSpec(memory_space=pltpu.VMEM)
    return pl.pallas_call(
        functools.partial(first_factor_kernel, plan),
        out_shape=(
            jax.ShapeDtypeStruct((na * B, na * B), jnp.float32),
            jax.ShapeDtypeStruct((na * B, B), jnp.float32),
        ),
        in_specs=[pl.BlockSpec(memory_space=pltpu.SMEM)] + [vmem] * len(parts),
        out_specs=(vmem,) * 2,
        scratch_shapes=[
            pltpu.VMEM((parts[0].shape[0] * len(parts), B), jnp.float32),
            pltpu.VMEM((na * B, na * B), jnp.float32),
            pltpu.VMEM((B, B), jnp.float32),
            pltpu.VMEM((B, na * B), jnp.float32),
        ],
        compiler_params=pltpu.CompilerParams(vmem_limit_bytes=16 << 20),
        name="chol_first",
    )(at, *parts)


def last_factor_kernel(plan, at_ref, f_ref, w_ref, *refs):
    count = plan.chips * plan.cores
    out_ref, o_ref, a_ref, t_ref, m_ref, d_ref, r_ref, sem = refs[count:]
    n, top = o_ref.shape[0] // B, f_ref.shape[0]
    na = top // B
    place_parts(plan, at_ref, refs[:count], a_ref)
    for j in range(na, n):
        start = packed_start(j) - packed_start(na)
        lanes = slice((j - na) * B, (j - na + 1) * B)
        t_ref[:, lanes] = a_ref[start : start + top, :]
        m_ref[: (j - na + 1) * B, lanes] = a_ref[start + top : start + (j + 1) * B, :]
    o_ref[:top, :top] = f_ref[...]
    o_ref[top:, :top] = jnp.zeros((n * B - top, top), jnp.float32)
    for k in range(na):
        rows = slice(k * B, (k + 1) * B)
        row = dot32(w_ref[rows, :], t_ref[rows, :])
        o_ref[rows, top:] = row
        if k < na - 1:
            t_ref[(k + 1) * B :, :] = t_ref[(k + 1) * B :, :] - dot32_t(f_ref[rows, (k + 1) * B :], row)
        m_ref[...] = m_ref[...] - dot32_t(row, row)

    head = pltpu.make_async_copy(o_ref.at[pl.ds(0, top), :], out_ref.at[pl.ds(0, top), :], sem.at[n - na])
    head.start()

    def block_row(k):
        rows = pl.ds(pl.multiple_of(top + k * B, B), B)
        return pltpu.make_async_copy(o_ref.at[rows, :], out_ref.at[rows, :], sem.at[k])

    def store(k, row, u, w):
        down = pl.multiple_of(top + k * B, B)
        o_ref[pl.ds(down, B), top:] = row
        o_ref[pl.ds(down, B), pl.ds(down, B)] = u
        block_row(k).start()

    eliminate(n - na, m_ref, d_ref, r_ref, store)
    for k in range(n - na):
        block_row(k).wait()
    head.wait()


def last_factor(at, plan, n, f, w, parts):
    vmem = pl.BlockSpec(memory_space=pltpu.VMEM)
    top = f.shape[0]
    return pl.pallas_call(
        functools.partial(last_factor_kernel, plan),
        out_shape=jax.ShapeDtypeStruct((n, n), jnp.float32),
        in_specs=[pl.BlockSpec(memory_space=pltpu.SMEM)] + [vmem] * (2 + len(parts)),
        out_specs=pl.BlockSpec(memory_space=pl.ANY),
        scratch_shapes=[
            pltpu.VMEM((n, n), jnp.float32),
            pltpu.VMEM((parts[0].shape[0] * len(parts), B), jnp.float32),
            pltpu.VMEM((top, n - top), jnp.float32),
            pltpu.VMEM((n - top, n - top), jnp.float32),
            pltpu.VMEM((B, B), jnp.float32),
            pltpu.VMEM((B, n - top), jnp.float32),
            pltpu.SemaphoreType.DMA(((n - top) // B + 1,)),
        ],
        compiler_params=pltpu.CompilerParams(vmem_limit_bytes=24 << 20),
        name="chol_last",
    )(at, f, w, *parts)


def swap(x, axis, s):
    return lax.ppermute(x, axis, [(i, i ^ s) for i in range(lax.axis_size(axis))])


def scatter(pieces, axis):
    return [pieces[0]] + [swap(p, axis, -q % len(pieces)) for q, p in enumerate(pieces) if q]


def spread_out(x, axis):
    return [x] + [swap(x, axis, s) for s in range(1, lax.axis_size(axis))]


def shards(embeddings, landmarks):
    lands, chips, cores = (lax.axis_size(a) for a in ("land", "chip", "core"))
    land, chip, core = (lax.axis_index(a) for a in ("land", "chip", "core"))
    at = jnp.stack([land, chip, core]).astype(jnp.int32)
    shard = landmarks.shape[0]
    n = shard * lands
    plan = Plan(lands, chips, cores, shard // (chips * cores) % 16 == 0, embeddings.shape[0] * lands * chips * cores)

    share = shard // (chips * cores)
    own = lax.dynamic_slice_in_dim(landmarks, (chip * cores + core) * share, share, 0)
    if plan.split:
        piece = own
    else:
        piece = lax.dynamic_slice_in_dim(landmarks, chip * (shard // chips), shard // chips, 0)
    x_upper, u = own_cross(landmarks[: shard // 2], embeddings)
    z, x_upper, u = lax.optimization_barrier((spread_out(piece, "land")[1:], x_upper, u))
    slices = jnp.concatenate(z, 0)
    far = spread_out(slices, "chip")
    x_lower, x_slices = next_cross(landmarks[shard // 2 :], slices, embeddings, u)
    far, x_lower, x_slices = lax.optimization_barrier((far, x_lower, x_slices))
    if plan.split:
        for a in range(1, cores):
            far = far + [swap(f, "core", a) for f in far[:chips]]

    na = n // B // 2
    keep, send = local_normal(at, plan, na, embeddings, landmarks, own, u, x_upper, x_lower, x_slices, far)
    rows = [r // cores for r in segments(plan, na, n // B)]
    parts = scatter(add_cut(at, 1, chips, rows, [keep, swap(send, "core", 1)]), "chip")
    rows = [r // chips for r in rows]
    parts = scatter(add_cut(at, 0, lands, rows, parts), "land")
    rows = [r // lands for r in rows]
    (whole,) = add_cut(at, 0, 1, rows, parts)
    first, last = place(at, 0, rows, spread_out(whole, "land"))
    first = spread_out(first, "chip")
    first, last = lax.optimization_barrier((first + [swap(p, "core", 1) for p in first], last))
    f, w = first_factor(at, plan, na, first)
    last, f, w = lax.optimization_barrier((spread_out(last, "chip"), f, w))
    last = last + [swap(p, "core", 1) for p in last]
    return last_factor(at, plan, n, f, w, last)


def solution(mesh):
    land, rows = mesh.axis_names
    cores = 2
    fine = Mesh(mesh.devices.reshape(mesh.shape[land], mesh.shape[rows] // cores, cores), ("land", "chip", "core"))
    in_specs = (P(("land", "chip", "core"), None), P("land", None))
    return jax.shard_map(shards, mesh=fine, in_specs=in_specs, out_specs=P(), check_vma=False)
```

```python
import functools
import math
import typing

import jax
import jax.numpy as jnp
from jax import lax
from jax.experimental import pallas as pl
from jax.experimental.pallas import tpu as pltpu
from jax.sharding import Mesh
from jax.sharding import PartitionSpec as P

LAYERS = 6
SCALE_SQ = 1.0 / 32.0
RIDGE = 0.1
EPS = 1e-06
B = 128
HALF = 64
CLIP = 1.0 - 2.0**-24

ARC = (0.9426497266634519, 0.04833294295062493, 0.004716300148249888, 0.004298816276929029)
KEEP = 1.0 / (1.0 + SCALE_SQ)
ARC = tuple(c * SCALE_SQ * KEEP / math.pi for c in ARC)
GROWTH = (1.0 + SCALE_SQ) ** LAYERS


def recursion(c):
    c = jnp.clip(c, -CLIP, CLIP)
    for _ in range(LAYERS):
        w = 1.0 - jnp.abs(c)
        t = (w * w) * lax.rsqrt(w)
        poly = ARC[3]
        for a in ARC[2::-1]:
            poly = poly * w + a
        c = jnp.maximum(c, KEEP * c) + t * poly
    return c


def nt(a, b):
    return lax.dot_general(a, b, (((1,), (1,)), ((), ())), preferred_element_type=jnp.float32)


def lane_tiles_of_squares(x):
    total = None
    for l in range(0, x.shape[1], B):
        wide = x[:, l : l + B].astype(jnp.float32)
        total = wide * wide if total is None else total + wide * wide
    return total


def squares_mean_column(x):
    total = jnp.sum(lane_tiles_of_squares(x), axis=1, keepdims=True)
    return jnp.broadcast_to(total * (1.0 / x.shape[1]) + EPS, (x.shape[0], B))


def squares_mean_row(x):
    total = lane_tiles_of_squares(x)
    rows = [jnp.sum(total[i : i + B].T, axis=0, keepdims=True) for i in range(0, x.shape[0], B)]
    row = jnp.concatenate(rows, axis=1) * (1.0 / x.shape[1]) + EPS
    return jnp.broadcast_to(row, (8, x.shape[0]))


def spread(column, lanes):
    return jnp.concatenate([column] * (lanes // B), axis=1)


CHUNK = 16


def fill_cross(marks_ref, emb_ref, u_ref, k_ref, vq_ref, x_ref, chunks, rows_of):
    m, e = emb_ref.shape
    rows = marks_ref.shape[0]
    k_ref[:rows, :] = nt(marks_ref[...], emb_ref[...])
    vq_ref[:rows, :] = squares_mean_column(marks_ref[...])

    def part(i, _):
        r, to = (pl.multiple_of(at, CHUNK) for at in rows_of(i))
        vq = vq_ref[pl.ds(r, CHUNK), :]
        v_inv = lax.rsqrt(vq)
        v_root = vq * v_inv
        up = jnp.concatenate([u_ref[:8, :]] * (CHUNK // 8), axis=0)
        ur = jnp.concatenate([u_ref[8:, :]] * (CHUNK // 8), axis=0)
        c = recursion(k_ref[pl.ds(r, CHUNK), :] * up * spread(v_inv * (1.0 / e), m))
        x_ref[pl.ds(to, CHUNK), :] = (c * ur * spread(v_root * GROWTH, m)).astype(jnp.bfloat16)
        return 0

    lax.fori_loop(0, chunks, part, 0)


def in_order(i):
    return i * CHUNK, i * CHUNK


def own_kernel(marks_ref, emb_ref, x_ref, u_ref, k_ref, vq_ref):
    uq = squares_mean_row(emb_ref[...])
    inv = lax.rsqrt(uq)
    u_ref[:8, :] = inv
    u_ref[8:, :] = uq * inv
    fill_cross(marks_ref, emb_ref, u_ref, k_ref, vq_ref, x_ref, x_ref.shape[0] // CHUNK, in_order)


def own_cross(landmarks, embeddings):
    m = embeddings.shape[0]
    rows = landmarks.shape[0]
    vmem = pl.BlockSpec(memory_space=pltpu.VMEM)
    return pl.pallas_call(
        own_kernel,
        out_shape=(jax.ShapeDtypeStruct((rows, m), jnp.bfloat16), jax.ShapeDtypeStruct((16, m), jnp.float32)),
        in_specs=[vmem] * 2,
        out_specs=(vmem, vmem),
        scratch_shapes=[pltpu.VMEM((rows, m), jnp.float32), pltpu.VMEM((rows, B), jnp.float32)],
        compiler_params=pltpu.CompilerParams(vmem_limit_bytes=12 << 20),
        name="own_cross",
    )(landmarks, embeddings)


def next_kernel(marks_ref, slices_ref, emb_ref, u_ref, x_ref, x_slices_ref, k_ref, vq_ref):
    for m_ref, to_ref in ((marks_ref, x_ref), (slices_ref, x_slices_ref)):
        fill_cross(m_ref, emb_ref, u_ref, k_ref, vq_ref, to_ref, to_ref.shape[0] // CHUNK, in_order)


def next_cross(landmarks, slices, embeddings, u):
    m = embeddings.shape[0]
    rows = max(landmarks.shape[0], slices.shape[0])
    vmem = pl.BlockSpec(memory_space=pltpu.VMEM)
    return pl.pallas_call(
        next_kernel,
        out_shape=tuple(jax.ShapeDtypeStruct((x.shape[0], m), jnp.bfloat16) for x in (landmarks, slices)),
        in_specs=[vmem] * 4,
        out_specs=(vmem, vmem),
        scratch_shapes=[pltpu.VMEM((rows, m), jnp.float32), pltpu.VMEM((rows, B), jnp.float32)],
        compiler_params=pltpu.CompilerParams(vmem_limit_bytes=12 << 20),
        name="next_cross",
    )(landmarks, slices, embeddings, u)


class Plan(typing.NamedTuple):
    lands: int
    chips: int
    cores: int
    split: bool
    all_points: int


def gram_kernel(plan, na, at_ref, emb_ref, mine_ref, own_ref, u_ref, x_upper_ref, x_lower_ref, x_slices_ref, *refs):
    lands, chips, cores, split, all_points = plan
    count = chips * (cores if split else 1)
    far = refs[:count]
    keep_ref, send_ref, x_ref, ridge_ref, marks_ref, k_ref, vq_ref, out_ref = refs[count:]
    shard, e = mine_ref.shape
    n = shard * lands
    land, chip, core = at_ref[0], at_ref[1], at_ref[2]
    here = pl.multiple_of(land * shard, shard)
    x_ref[pl.ds(here, shard // 2), :] = x_upper_ref[...]
    x_ref[pl.ds(pl.multiple_of(here + shard // 2, CHUNK), shard // 2), :] = x_lower_ref[...]
    piece = far[0].shape[0] // (lands - 1)
    for a in range(cores if split else 1):
        for t in range(chips):
            slot = ((chip ^ t) * cores + (core ^ a)) if split else (chip ^ t)
            for s in range(1, lands):
                to = pl.multiple_of((s - 1) * shard + slot * piece, piece)
                marks_ref[pl.ds(to, piece), :] = far[a * chips + t][(s - 1) * piece : s * piece, :]

    slots = shard // piece
    mine = chip * cores + core if split else chip
    for s in range(1, lands):
        to = pl.multiple_of((land ^ s) * shard + mine * piece, piece)
        x_ref[pl.ds(to, piece), :] = x_slices_ref[(s - 1) * piece : s * piece, :]
    steps = piece // CHUNK

    def rows_of(i):
        s, rest = i // ((slots - 1) * steps), i % ((slots - 1) * steps)
        at = (mine ^ (rest // steps + 1)) * piece + rest % steps * CHUNK
        return s * shard + at, (land ^ (s + 1)) * shard + at

    fill_cross(marks_ref, emb_ref, u_ref, k_ref, vq_ref, x_ref, (lands - 1) * (slots - 1) * steps, rows_of)

    share = own_ref.shape[0]
    oq = squares_mean_column(own_ref[...])
    o_inv = lax.rsqrt(oq)

    def ridge(marks, marks_q, to):
        k_own = nt(own_ref[...], marks)
        for l in range(0, shard, B):
            vq = marks_q[l : l + B].T[:8]
            v_inv = lax.rsqrt(vq)
            for i in range(share // 8):
                oi = o_inv[8 * i : 8 * i + 8]
                c = recursion(k_own[8 * i : 8 * i + 8, l : l + B] * v_inv * (oi * (1.0 / e)))
                root = oq[8 * i : 8 * i + 8] * oi
                ridge_ref[8 * i : 8 * i + 8, pl.ds(to + l, B)] = c * (vq * v_inv) * (root * (RIDGE * GROWTH))

    ridge(mine_ref[...], squares_mean_column(mine_ref[...]), here)
    for s in range(1, lands):
        rows = slice((s - 1) * shard, s * shard)
        ridge(marks_ref[rows, :], vq_ref[rows, :], pl.multiple_of((land ^ s) * shard, shard))

    position = land * shard + (chip * cores + core) * share
    row_block = position // B
    offset = position % B
    wide = 2 * B
    for w in range(n // wide):
        both = nt(x_ref[: (w + 1) * wide, :], x_ref[w * wide : (w + 1) * wide, :]) * (1.0 / all_points)
        for j in (2 * w, 2 * w + 1):
            start = column_start(plan, na, j)
            out_ref[start : start + (j + 1) * B, :] = both[: (j + 1) * B, (j % 2) * B : (j % 2 + 1) * B]
    for j in range(n // B):
        start = column_start(plan, na, j)

        @pl.when(row_block <= j)
        def _():
            at = pl.ds(pl.multiple_of(start + row_block * B + offset, share), share)
            out_ref[at, :] = out_ref[at, :] + ridge_ref[:, j * B : (j + 1) * B]

    done = base = 0
    for rows in segments(plan, na, n // B):
        half = rows // cores
        to = slice(done, done + half)
        keep_ref[to, :] = out_ref[pl.ds(pl.multiple_of(base + core * half, 8), half), :]
        send_ref[to, :] = out_ref[pl.ds(pl.multiple_of(base + (1 - core) * half, 8), half), :]
        done, base = done + half, base + rows


def packed_start(j):
    return j * (j + 1) // 2 * B


def segments(plan, na, nb):
    unit = 8 * plan.lands * plan.chips * plan.cores
    return [-(-rows // unit) * unit for rows in (packed_start(na), packed_start(nb) - packed_start(na))]


def column_start(plan, na, j):
    return packed_start(j) if j < na else packed_start(j) - packed_start(na) + segments(plan, na, j)[0]


def local_normal(at, plan, na, embeddings, landmarks, own, u, x_upper, x_lower, x_slices, far):
    n, m = landmarks.shape[0] * plan.lands, embeddings.shape[0]
    away = n - landmarks.shape[0]
    rows = sum(segments(plan, na, n // B))
    half = jax.ShapeDtypeStruct((rows // plan.cores, B), jnp.float32)
    vmem = pl.BlockSpec(memory_space=pltpu.VMEM)
    return pl.pallas_call(
        functools.partial(gram_kernel, plan, na),
        out_shape=(half, half),
        in_specs=[pl.BlockSpec(memory_space=pltpu.SMEM)] + [vmem] * (7 + len(far)),
        out_specs=(vmem,) * 2,
        scratch_shapes=[
            pltpu.VMEM((n, m), jnp.bfloat16),
            pltpu.VMEM((own.shape[0], n), jnp.float32),
            pltpu.VMEM((away, landmarks.shape[1]), jnp.bfloat16),
            pltpu.VMEM((away, m), jnp.float32),
            pltpu.VMEM((away, B), jnp.float32),
            pltpu.VMEM((rows, B), jnp.float32),
        ],
        compiler_params=pltpu.CompilerParams(vmem_limit_bytes=24 << 20),
        name="gram",
    )(at, embeddings, landmarks, own, u, x_upper, x_lower, x_slices, *far)


def add_cut_kernel(ways, axis, parts, at_ref, *refs):
    ins, outs = refs[: len(refs) - ways], refs[len(refs) - ways :]
    base = 0
    for rows in parts:
        h = rows // ways
        for q in range(ways):
            s = -q % ways
            at = pl.ds(pl.multiple_of(base + (at_ref[axis] ^ s) * h, 8), h) if ways > 1 else slice(base, base + h)
            total = ins[0][at, :]
            for r in ins[1:]:
                total = total + r[at, :]
            outs[q][base // ways : base // ways + h, :] = total
        base += rows


def add_cut(at, axis, ways, parts, ins):
    h = sum(parts) // ways
    vmem = pl.BlockSpec(memory_space=pltpu.VMEM)
    return pl.pallas_call(
        functools.partial(add_cut_kernel, ways, axis, parts),
        out_shape=tuple([jax.ShapeDtypeStruct((h, B), jnp.float32)] * ways),
        in_specs=[pl.BlockSpec(memory_space=pltpu.SMEM)] + [vmem] * len(ins),
        out_specs=tuple([vmem] * ways),
        compiler_params=pltpu.CompilerParams(vmem_limit_bytes=8 << 20),
        name="add_cut",
    )(at, *ins)


def place_kernel(axis, ways, parts, at_ref, *refs):
    ins, outs = refs[:ways], refs[ways:]
    base = 0
    for out, h in zip(outs, parts):
        for s in range(ways):
            out[pl.ds(pl.multiple_of((at_ref[axis] ^ s) * h, 8), h), :] = ins[s][base : base + h, :]
        base += h


def place(at, axis, parts, ins):
    vmem = pl.BlockSpec(memory_space=pltpu.VMEM)
    return pl.pallas_call(
        functools.partial(place_kernel, axis, len(ins), parts),
        out_shape=tuple(jax.ShapeDtypeStruct((h * len(ins), B), jnp.float32) for h in parts),
        in_specs=[pl.BlockSpec(memory_space=pltpu.SMEM)] + [vmem] * len(ins),
        out_specs=(vmem,) * len(parts),
        compiler_params=pltpu.CompilerParams(vmem_limit_bytes=8 << 20),
        name="place",
    )(at, *ins)


def thirds(x):
    h = x.astype(jnp.bfloat16)
    r = x - h.astype(jnp.float32)
    m = r.astype(jnp.bfloat16)
    return h, m, (r - m.astype(jnp.float32)).astype(jnp.bfloat16)

def left_terms(x, axis):
    h, m, l = thirds(x)
    return jnp.concatenate([h, h, h, m, m, l], axis)

def right_terms(x, axis):
    h, m, l = thirds(x)
    return jnp.concatenate([h, m, l, h, m, h], axis)

def dot32(a, b):
    return lax.dot_general(left_terms(a, 1), right_terms(b, 0), (((1,), (0,)), ((), ())), preferred_element_type=jnp.float32)

def dot32_t(a, b):
    return dot32(a.T, b)

def factor_block(d):
    row8 = lax.broadcasted_iota(jnp.int32, (8, B), 0)
    lane8 = lax.broadcasted_iota(jnp.int32, (8, B), 1)
    rows = [d[i : i + 8] for i in range(0, B, 8)]
    factor, inverse = [None] * (B // 8), [None] * (B // 8)
    zero = rows[0] * 0.0
    half = HALF // 8

    def spread_columns(x, lane):
        columns = [jnp.broadcast_to(x[:, lane + i : lane + i + 1], (8, B)) for i in range(8)]
        return [columns[0] + zero] + columns[1:]

    def splat(x, r):
        return jnp.broadcast_to(x[r : r + 1], (8, B))

    for start in range(0, B // 8, half):
        end = start + half
        diag = spread_columns(rows[start], 8 * start)
        for p in range(start, end):
            col = {r: spread_columns(rows[r], 8 * p) for r in range(p + 1, end)}
            after = spread_columns(rows[p + 1], 8 * p + 8) if p + 1 < end else None
            panel = (lane8 >= 8 * p) & (lane8 < 8 * p + 8)
            unit = jnp.where(lane8 == row8 + 8 * p, 1.0, 0.0)
            for r in col:
                rows[r] = jnp.where(panel, 0.0, rows[r])
            pivots = jnp.ones((8, B), jnp.float32)
            for j in range(8):
                pivot = splat(diag[j], j)
                pivots = jnp.where(row8 == j, pivot, pivots)
                inv = 1.0 / pivot
                coef = {i: splat(diag[j], i) for i in range(j + 1, 8)}
                row, unit_row = splat(rows[p], j), splat(unit, j)
                both = jnp.where(panel, unit_row, row)
                if j < 7:
                    c = jnp.where(row8 > j, diag[j] * inv, 0.0)
                    rows[p] = rows[p] - c * row
                    unit = unit - c * unit_row
                for i in coef:
                    diag[i] = diag[i] - (diag[j] * coef[i]) * inv
                for r in col:
                    c = col[r][j] * inv
                    if r == p + 1:
                        for i in range(8):
                            after[i] = after[i] - c * splat(col[r][j], i)
                    for i in coef:
                        col[r][i] = col[r][i] - c * coef[i]
                    rows[r] = rows[r] - c * both
            s = lax.rsqrt(pivots)
            factor[p] = rows[p] * s
            inverse[p] = jnp.where(panel, unit * s, jnp.where(lane8 < 8 * p, factor[p], 0.0))
            diag = after
        if end < B // 8:
            u = jnp.concatenate(factor[start:end], 0)
            w = jnp.concatenate(inverse[start:end], 0)
            lanes = lax.broadcasted_iota(jnp.int32, w.shape, 1)
            upd = lax.dot_general(
                left_terms(u, 0),
                right_terms(jnp.where(lanes < 8 * end, w, u), 0),
                (((0,), (0,)), ((), ())),
                preferred_element_type=jnp.float32,
            )
            for r in range(end, B // 8):
                rows[r] = jnp.where(lane8 < 8 * end, 0.0, rows[r]) - upd[8 * r : 8 * r + 8]
    tri = lax.broadcasted_iota(jnp.int32, (B, B), 0) <= lax.broadcasted_iota(jnp.int32, (B, B), 1)
    return jnp.where(tri, jnp.concatenate(factor, 0), 0.0), jnp.concatenate(inverse, 0)


def product(a_terms, b_terms):
    return lax.dot_general(a_terms, b_terms, (((1,), (0,)), ((), ())), preferred_element_type=jnp.float32)


def update_upper(m_ref, row, first):
    turned, terms = left_terms(row.T, 1), right_terms(row, 0)
    for i in range(row.shape[1] // B):
        at = (first + i) * B
        m_ref[at : at + B, at:] = m_ref[at : at + B, at:] - product(turned[i * B : (i + 1) * B], terms[:, i * B :])


def eliminate(nb, m_ref, store):
    for k in range(nb):
        at, on = k * B, (k + 1) * B
        u, w = factor_block(m_ref[at:on, at:on])
        row = dot32(w, m_ref[at:on, on:]) if k < nb - 1 else None
        store(k, u, w, row)
        if row is not None:
            update_upper(m_ref, row, k + 1)


def place_parts(plan, at_ref, parts, a_ref):
    h = parts[0].shape[0]
    for a in range(plan.cores):
        for t in range(plan.chips):
            slot = (at_ref[2] ^ a) * plan.chips + (at_ref[1] ^ t)
            a_ref[pl.ds(pl.multiple_of(slot * h, h), h), :] = parts[a * plan.chips + t][...]


def first_factor_kernel(plan, at_ref, *refs):
    count = plan.chips * plan.cores
    f_ref, w_ref, a_ref, m_ref = refs[count:]
    na = f_ref.shape[0] // B
    place_parts(plan, at_ref, refs[:count], a_ref)
    for j in range(na):
        m_ref[: (j + 1) * B, j * B : (j + 1) * B] = a_ref[packed_start(j) : packed_start(j) + (j + 1) * B, :]

    f_ref[...] = jnp.zeros_like(f_ref)

    def store(k, u, w, row):
        at, on = k * B, (k + 1) * B
        f_ref[at:on, at:on] = u
        w_ref[at:on, :] = w
        if row is not None:
            f_ref[at:on, on:] = row

    eliminate(na, m_ref, store)


def first_factor(at, plan, na, parts):
    vmem = pl.BlockSpec(memory_space=pltpu.VMEM)
    return pl.pallas_call(
        functools.partial(first_factor_kernel, plan),
        out_shape=(
            jax.ShapeDtypeStruct((na * B, na * B), jnp.float32),
            jax.ShapeDtypeStruct((na * B, B), jnp.float32),
        ),
        in_specs=[pl.BlockSpec(memory_space=pltpu.SMEM)] + [vmem] * len(parts),
        out_specs=(vmem,) * 2,
        scratch_shapes=[
            pltpu.VMEM((parts[0].shape[0] * len(parts), B), jnp.float32),
            pltpu.VMEM((na * B, na * B), jnp.float32),
        ],
        compiler_params=pltpu.CompilerParams(vmem_limit_bytes=16 << 20),
        name="chol_first",
    )(at, *parts)


def last_factor_kernel(plan, at_ref, f_ref, w_ref, *refs):
    count = plan.chips * plan.cores
    out_ref, o_ref, a_ref, t_ref, m_ref, sem = refs[count:]
    n, top = o_ref.shape[0] // B, f_ref.shape[0]
    na = top // B
    place_parts(plan, at_ref, refs[:count], a_ref)
    for j in range(na, n):
        start = packed_start(j) - packed_start(na)
        lanes = slice((j - na) * B, (j - na + 1) * B)
        t_ref[:, lanes] = a_ref[start : start + top, :]
        m_ref[: (j - na + 1) * B, lanes] = a_ref[start + top : start + (j + 1) * B, :]
    o_ref[:top, :top] = f_ref[...]
    o_ref[top:, :] = jnp.zeros((n * B - top, n * B), jnp.float32)
    for k in range(na):
        rows = slice(k * B, (k + 1) * B)
        row = dot32(w_ref[rows, :], t_ref[rows, :])
        o_ref[rows, top:] = row
        if k < na - 1:
            t_ref[(k + 1) * B :, :] = t_ref[(k + 1) * B :, :] - dot32_t(f_ref[rows, (k + 1) * B :], row)
        update_upper(m_ref, row, 0)

    head = pltpu.make_async_copy(o_ref.at[pl.ds(0, top), :], out_ref.at[pl.ds(0, top), :], sem.at[n - na])
    head.start()

    copies = [head]

    def store(k, u, w, row):
        at, on = top + k * B, top + (k + 1) * B
        o_ref[at:on, at:on] = u
        if row is not None:
            o_ref[at:on, on:] = row
        copies.append(pltpu.make_async_copy(o_ref.at[pl.ds(at, B), :], out_ref.at[pl.ds(at, B), :], sem.at[k]))
        copies[-1].start()

    eliminate(n - na, m_ref, store)
    for copy in copies:
        copy.wait()


def last_factor(at, plan, n, f, w, parts):
    vmem = pl.BlockSpec(memory_space=pltpu.VMEM)
    top = f.shape[0]
    return pl.pallas_call(
        functools.partial(last_factor_kernel, plan),
        out_shape=jax.ShapeDtypeStruct((n, n), jnp.float32),
        in_specs=[pl.BlockSpec(memory_space=pltpu.SMEM)] + [vmem] * (2 + len(parts)),
        out_specs=pl.BlockSpec(memory_space=pl.ANY),
        scratch_shapes=[
            pltpu.VMEM((n, n), jnp.float32),
            pltpu.VMEM((parts[0].shape[0] * len(parts), B), jnp.float32),
            pltpu.VMEM((top, n - top), jnp.float32),
            pltpu.VMEM((n - top, n - top), jnp.float32),
            pltpu.SemaphoreType.DMA(((n - top) // B + 1,)),
        ],
        compiler_params=pltpu.CompilerParams(vmem_limit_bytes=24 << 20),
        name="chol_last",
    )(at, f, w, *parts)


def swap(x, axis, s):
    return lax.ppermute(x, axis, [(i, i ^ s) for i in range(lax.axis_size(axis))])


def scatter(pieces, axis):
    return [pieces[0]] + [swap(p, axis, -q % len(pieces)) for q, p in enumerate(pieces) if q]


def spread_out(x, axis):
    return [x] + [swap(x, axis, s) for s in range(1, lax.axis_size(axis))]


def shards(embeddings, landmarks):
    lands, chips, cores = (lax.axis_size(a) for a in ("land", "chip", "core"))
    land, chip, core = (lax.axis_index(a) for a in ("land", "chip", "core"))
    at = jnp.stack([land, chip, core]).astype(jnp.int32)
    shard = landmarks.shape[0]
    n = shard * lands
    plan = Plan(lands, chips, cores, shard // (chips * cores) % 16 == 0, embeddings.shape[0] * lands * chips * cores)

    share = shard // (chips * cores)
    own = lax.dynamic_slice_in_dim(landmarks, (chip * cores + core) * share, share, 0)
    if plan.split:
        piece = own
    else:
        piece = lax.dynamic_slice_in_dim(landmarks, chip * (shard // chips), shard // chips, 0)
    x_upper, u = own_cross(landmarks[: shard // 2], embeddings)
    z, x_upper, u = lax.optimization_barrier((spread_out(piece, "land")[1:], x_upper, u))
    slices = jnp.concatenate(z, 0)
    far = spread_out(slices, "chip")
    x_lower, x_slices = next_cross(landmarks[shard // 2 :], slices, embeddings, u)
    far, x_lower, x_slices = lax.optimization_barrier((far, x_lower, x_slices))
    if plan.split:
        for a in range(1, cores):
            far = far + [swap(f, "core", a) for f in far[:chips]]

    na = n // B // 2
    keep, send = local_normal(at, plan, na, embeddings, landmarks, own, u, x_upper, x_lower, x_slices, far)
    rows = [r // cores for r in segments(plan, na, n // B)]
    parts = scatter(add_cut(at, 1, chips, rows, [keep, swap(send, "core", 1)]), "chip")
    rows = [r // chips for r in rows]
    parts = scatter(add_cut(at, 0, lands, rows, parts), "land")
    rows = [r // lands for r in rows]
    (whole,) = add_cut(at, 0, 1, rows, parts)
    first, last = place(at, 0, rows, spread_out(whole, "land"))
    first = spread_out(first, "chip")
    first, last = lax.optimization_barrier((first + [swap(p, "core", 1) for p in first], last))
    f, w = first_factor(at, plan, na, first)
    last, f, w = lax.optimization_barrier((spread_out(last, "chip"), f, w))
    last = last + [swap(p, "core", 1) for p in last]
    return last_factor(at, plan, n, f, w, last)


def solution(mesh):
    land, rows = mesh.axis_names
    cores = 2
    fine = Mesh(mesh.devices.reshape(mesh.shape[land], mesh.shape[rows] // cores, cores), ("land", "chip", "core"))
    in_specs = (P(("land", "chip", "core"), None), P("land", None))
    return jax.shard_map(shards, mesh=fine, in_specs=in_specs, out_specs=P(), check_vma=False)
```

```python
import functools
import math
import typing

import jax
import jax.numpy as jnp
from jax import lax
from jax.experimental import pallas as pl
from jax.experimental.pallas import tpu as pltpu
from jax.sharding import Mesh
from jax.sharding import PartitionSpec as P

LAYERS = 6
SCALE_SQ = 1.0 / 32.0
RIDGE = 0.1
EPS = 1e-06
B = 128
HALF = 64
CLIP = 1.0 - 2.0**-24

ARC = (0.9426497266634519, 0.04833294295062493, 0.004716300148249888, 0.004298816276929029)
KEEP = 1.0 / (1.0 + SCALE_SQ)
ARC = tuple(c * SCALE_SQ * KEEP / math.pi for c in ARC)
GROWTH = (1.0 + SCALE_SQ) ** LAYERS


def recursion(c):
    c = jnp.clip(c, -CLIP, CLIP)
    for _ in range(LAYERS):
        w = 1.0 - jnp.abs(c)
        t = (w * w) * lax.rsqrt(w)
        poly = ARC[3]
        for a in ARC[2::-1]:
            poly = poly * w + a
        c = jnp.maximum(c, KEEP * c) + t * poly
    return c


def nt(a, b):
    return lax.dot_general(a, b, (((1,), (1,)), ((), ())), preferred_element_type=jnp.float32)


def lane_tiles_of_squares(x):
    total = None
    for l in range(0, x.shape[1], B):
        wide = x[:, l : l + B].astype(jnp.float32)
        total = wide * wide if total is None else total + wide * wide
    return total


def squares_mean_column(x):
    total = jnp.sum(lane_tiles_of_squares(x), axis=1, keepdims=True)
    return jnp.broadcast_to(total * (1.0 / x.shape[1]) + EPS, (x.shape[0], B))


def squares_mean_row(x):
    total = lane_tiles_of_squares(x)
    rows = [jnp.sum(total[i : i + B].T, axis=0, keepdims=True) for i in range(0, x.shape[0], B)]
    row = jnp.concatenate(rows, axis=1) * (1.0 / x.shape[1]) + EPS
    return jnp.broadcast_to(row, (8, x.shape[0]))


def spread(column, lanes):
    return jnp.concatenate([column] * (lanes // B), axis=1)


CHUNK = 16
LANES = 512


def fill_cross(marks_ref, emb_ref, u_ref, k_ref, vq_ref, x_ref, chunks, rows_of):
    m, e = emb_ref.shape
    rows = marks_ref.shape[0]
    k_ref[:rows, :] = nt(marks_ref[...], emb_ref[...])
    vq_ref[:rows, :] = squares_mean_column(marks_ref[...])

    together = max(d for d in range(1, 9) if chunks % d == 0)

    def part(i, _):
        for q in range(together):
            r, to = (pl.multiple_of(at, CHUNK) for at in rows_of(i * together + q))
            vq = vq_ref[pl.ds(r, CHUNK), :]
            v_inv = lax.rsqrt(vq)
            v_in, v_out = v_inv * (1.0 / e), vq * v_inv * GROWTH
            for l in range(0, m, LANES):
                lanes = slice(l, l + LANES)
                up = jnp.concatenate([u_ref[:8, lanes]] * (CHUNK // 8), axis=0)
                ur = jnp.concatenate([u_ref[8:, lanes]] * (CHUNK // 8), axis=0)
                c = recursion(k_ref[pl.ds(r, CHUNK), lanes] * up * spread(v_in, LANES))
                x_ref[pl.ds(to, CHUNK), lanes] = (c * ur * spread(v_out, LANES)).astype(jnp.bfloat16)
        return 0

    lax.fori_loop(0, chunks // together, part, 0)


def in_order(i):
    return i * CHUNK, i * CHUNK


def own_kernel(marks_ref, emb_ref, x_ref, u_ref, k_ref, vq_ref):
    uq = squares_mean_row(emb_ref[...])
    inv = lax.rsqrt(uq)
    u_ref[:8, :] = inv
    u_ref[8:, :] = uq * inv
    fill_cross(marks_ref, emb_ref, u_ref, k_ref, vq_ref, x_ref, x_ref.shape[0] // CHUNK, in_order)


def own_cross(landmarks, embeddings):
    m = embeddings.shape[0]
    rows = landmarks.shape[0]
    vmem = pl.BlockSpec(memory_space=pltpu.VMEM)
    return pl.pallas_call(
        own_kernel,
        out_shape=(jax.ShapeDtypeStruct((rows, m), jnp.bfloat16), jax.ShapeDtypeStruct((16, m), jnp.float32)),
        in_specs=[vmem] * 2,
        out_specs=(vmem, vmem),
        scratch_shapes=[pltpu.VMEM((rows, m), jnp.float32), pltpu.VMEM((rows, B), jnp.float32)],
        compiler_params=pltpu.CompilerParams(vmem_limit_bytes=12 << 20),
        name="own_cross",
    )(landmarks, embeddings)


def next_kernel(marks_ref, slices_ref, emb_ref, u_ref, x_ref, x_slices_ref, k_ref, vq_ref):
    for m_ref, to_ref in ((marks_ref, x_ref), (slices_ref, x_slices_ref)):
        fill_cross(m_ref, emb_ref, u_ref, k_ref, vq_ref, to_ref, to_ref.shape[0] // CHUNK, in_order)


def next_cross(landmarks, slices, embeddings, u):
    m = embeddings.shape[0]
    rows = max(landmarks.shape[0], slices.shape[0])
    vmem = pl.BlockSpec(memory_space=pltpu.VMEM)
    return pl.pallas_call(
        next_kernel,
        out_shape=tuple(jax.ShapeDtypeStruct((x.shape[0], m), jnp.bfloat16) for x in (landmarks, slices)),
        in_specs=[vmem] * 4,
        out_specs=(vmem, vmem),
        scratch_shapes=[pltpu.VMEM((rows, m), jnp.float32), pltpu.VMEM((rows, B), jnp.float32)],
        compiler_params=pltpu.CompilerParams(vmem_limit_bytes=12 << 20),
        name="next_cross",
    )(landmarks, slices, embeddings, u)


class Plan(typing.NamedTuple):
    lands: int
    chips: int
    cores: int
    split: bool
    all_points: int


def gram_kernel(plan, na, at_ref, emb_ref, mine_ref, own_ref, u_ref, x_upper_ref, x_lower_ref, x_slices_ref, *refs):
    lands, chips, cores, split, all_points = plan
    count = chips * (cores if split else 1)
    far = refs[:count]
    keep_ref, send_ref, x_ref, ridge_ref, marks_ref, k_ref, vq_ref, out_ref = refs[count:]
    shard, e = mine_ref.shape
    n = shard * lands
    land, chip, core = at_ref[0], at_ref[1], at_ref[2]
    here = pl.multiple_of(land * shard, shard)
    x_ref[pl.ds(here, shard // 2), :] = x_upper_ref[...]
    x_ref[pl.ds(pl.multiple_of(here + shard // 2, CHUNK), shard // 2), :] = x_lower_ref[...]
    piece = far[0].shape[0] // (lands - 1)
    for a in range(cores if split else 1):
        for t in range(chips):
            slot = ((chip ^ t) * cores + (core ^ a)) if split else (chip ^ t)
            for s in range(1, lands):
                to = pl.multiple_of((s - 1) * shard + slot * piece, piece)
                marks_ref[pl.ds(to, piece), :] = far[a * chips + t][(s - 1) * piece : s * piece, :]

    slots = shard // piece
    mine = chip * cores + core if split else chip
    for s in range(1, lands):
        to = pl.multiple_of((land ^ s) * shard + mine * piece, piece)
        x_ref[pl.ds(to, piece), :] = x_slices_ref[(s - 1) * piece : s * piece, :]
    steps = piece // CHUNK

    def rows_of(i):
        s, rest = i // ((slots - 1) * steps), i % ((slots - 1) * steps)
        at = (mine ^ (rest // steps + 1)) * piece + rest % steps * CHUNK
        return s * shard + at, (land ^ (s + 1)) * shard + at

    fill_cross(marks_ref, emb_ref, u_ref, k_ref, vq_ref, x_ref, (lands - 1) * (slots - 1) * steps, rows_of)

    share = own_ref.shape[0]
    oq = squares_mean_column(own_ref[...])
    o_inv = lax.rsqrt(oq)

    def ridge(marks, marks_q, to):
        k_own = nt(own_ref[...], marks)
        for l in range(0, shard, B):
            vq = marks_q[l : l + B].T[:8]
            v_inv = lax.rsqrt(vq)
            for i in range(share // 8):
                oi = o_inv[8 * i : 8 * i + 8]
                c = recursion(k_own[8 * i : 8 * i + 8, l : l + B] * v_inv * (oi * (1.0 / e)))
                root = oq[8 * i : 8 * i + 8] * oi
                ridge_ref[8 * i : 8 * i + 8, pl.ds(to + l, B)] = c * (vq * v_inv) * (root * (RIDGE * GROWTH))

    ridge(mine_ref[...], squares_mean_column(mine_ref[...]), here)
    for s in range(1, lands):
        rows = slice((s - 1) * shard, s * shard)
        ridge(marks_ref[rows, :], vq_ref[rows, :], pl.multiple_of((land ^ s) * shard, shard))

    position = land * shard + (chip * cores + core) * share
    row_block = position // B
    offset = position % B
    wide = 2 * B
    for w in range(n // wide):
        both = nt(x_ref[: (w + 1) * wide, :], x_ref[w * wide : (w + 1) * wide, :]) * (1.0 / all_points)
        for j in (2 * w, 2 * w + 1):
            start = column_start(plan, na, j)
            out_ref[start : start + (j + 1) * B, :] = both[: (j + 1) * B, (j % 2) * B : (j % 2 + 1) * B]
    for j in range(n // B):
        start = column_start(plan, na, j)

        @pl.when(row_block <= j)
        def _():
            at = pl.ds(pl.multiple_of(start + row_block * B + offset, share), share)
            out_ref[at, :] = out_ref[at, :] + ridge_ref[:, j * B : (j + 1) * B]

    done = base = 0
    for rows in segments(plan, na, n // B):
        half = rows // cores
        to = slice(done, done + half)
        keep_ref[to, :] = out_ref[pl.ds(pl.multiple_of(base + core * half, 8), half), :]
        send_ref[to, :] = out_ref[pl.ds(pl.multiple_of(base + (1 - core) * half, 8), half), :]
        done, base = done + half, base + rows


def packed_start(j):
    return j * (j + 1) // 2 * B


def segments(plan, na, nb):
    unit = 8 * plan.lands * plan.chips * plan.cores
    return [-(-rows // unit) * unit for rows in (packed_start(na), packed_start(nb) - packed_start(na))]


def column_start(plan, na, j):
    return packed_start(j) if j < na else packed_start(j) - packed_start(na) + segments(plan, na, j)[0]


def local_normal(at, plan, na, embeddings, landmarks, own, u, x_upper, x_lower, x_slices, far):
    n, m = landmarks.shape[0] * plan.lands, embeddings.shape[0]
    away = n - landmarks.shape[0]
    rows = sum(segments(plan, na, n // B))
    half = jax.ShapeDtypeStruct((rows // plan.cores, B), jnp.float32)
    vmem = pl.BlockSpec(memory_space=pltpu.VMEM)
    return pl.pallas_call(
        functools.partial(gram_kernel, plan, na),
        out_shape=(half, half),
        in_specs=[pl.BlockSpec(memory_space=pltpu.SMEM)] + [vmem] * (7 + len(far)),
        out_specs=(vmem,) * 2,
        scratch_shapes=[
            pltpu.VMEM((n, m), jnp.bfloat16),
            pltpu.VMEM((own.shape[0], n), jnp.float32),
            pltpu.VMEM((away, landmarks.shape[1]), jnp.bfloat16),
            pltpu.VMEM((away, m), jnp.float32),
            pltpu.VMEM((away, B), jnp.float32),
            pltpu.VMEM((rows, B), jnp.float32),
        ],
        compiler_params=pltpu.CompilerParams(vmem_limit_bytes=24 << 20),
        name="gram",
    )(at, embeddings, landmarks, own, u, x_upper, x_lower, x_slices, *far)


def add_cut_kernel(ways, axis, parts, at_ref, *refs):
    ins, outs = refs[: len(refs) - ways], refs[len(refs) - ways :]
    base = 0
    for rows in parts:
        h = rows // ways
        for q in range(ways):
            s = -q % ways
            at = pl.ds(pl.multiple_of(base + (at_ref[axis] ^ s) * h, 8), h) if ways > 1 else slice(base, base + h)
            total = ins[0][at, :]
            for r in ins[1:]:
                total = total + r[at, :]
            outs[q][base // ways : base // ways + h, :] = total
        base += rows


def add_cut(at, axis, ways, parts, ins):
    h = sum(parts) // ways
    vmem = pl.BlockSpec(memory_space=pltpu.VMEM)
    return pl.pallas_call(
        functools.partial(add_cut_kernel, ways, axis, parts),
        out_shape=tuple([jax.ShapeDtypeStruct((h, B), jnp.float32)] * ways),
        in_specs=[pl.BlockSpec(memory_space=pltpu.SMEM)] + [vmem] * len(ins),
        out_specs=tuple([vmem] * ways),
        compiler_params=pltpu.CompilerParams(vmem_limit_bytes=8 << 20),
        name="add_cut",
    )(at, *ins)


def place_kernel(axis, ways, parts, at_ref, *refs):
    ins, outs = refs[:ways], refs[ways:]
    base = 0
    for out, h in zip(outs, parts):
        for s in range(ways):
            out[pl.ds(pl.multiple_of((at_ref[axis] ^ s) * h, 8), h), :] = ins[s][base : base + h, :]
        base += h


def place(at, axis, parts, ins):
    vmem = pl.BlockSpec(memory_space=pltpu.VMEM)
    return pl.pallas_call(
        functools.partial(place_kernel, axis, len(ins), parts),
        out_shape=tuple(jax.ShapeDtypeStruct((h * len(ins), B), jnp.float32) for h in parts),
        in_specs=[pl.BlockSpec(memory_space=pltpu.SMEM)] + [vmem] * len(ins),
        out_specs=(vmem,) * len(parts),
        compiler_params=pltpu.CompilerParams(vmem_limit_bytes=8 << 20),
        name="place",
    )(at, *ins)


def thirds(x):
    h = x.astype(jnp.bfloat16)
    r = x - h.astype(jnp.float32)
    m = r.astype(jnp.bfloat16)
    return h, m, (r - m.astype(jnp.float32)).astype(jnp.bfloat16)

def left_terms(x, axis):
    h, m, l = thirds(x)
    return jnp.concatenate([h, h, h, m, m, l], axis)

def right_terms(x, axis):
    h, m, l = thirds(x)
    return jnp.concatenate([h, m, l, h, m, h], axis)

def dot32(a, b):
    return lax.dot_general(left_terms(a, 1), right_terms(b, 0), (((1,), (0,)), ((), ())), preferred_element_type=jnp.float32)

def dot32_t(a, b):
    return dot32(a.T, b)

def factor_block(d):
    row8 = lax.broadcasted_iota(jnp.int32, (8, B), 0)
    lane8 = lax.broadcasted_iota(jnp.int32, (8, B), 1)
    rows = [d[i : i + 8] for i in range(0, B, 8)]
    factor, inverse = [None] * (B // 8), [None] * (B // 8)
    zero = rows[0] * 0.0
    half = HALF // 8

    def spread_columns(x, lane):
        columns = [jnp.broadcast_to(x[:, lane + i : lane + i + 1], (8, B)) for i in range(8)]
        return [columns[0] + zero] + columns[1:]

    def splat(x, r):
        return jnp.broadcast_to(x[r : r + 1], (8, B))

    for start in range(0, B // 8, half):
        end = start + half
        diag = spread_columns(rows[start], 8 * start)
        for p in range(start, end):
            col = {r: spread_columns(rows[r], 8 * p) for r in range(p + 1, end)}
            after = spread_columns(rows[p + 1], 8 * p + 8) if p + 1 < end else None
            panel = (lane8 >= 8 * p) & (lane8 < 8 * p + 8)
            unit = jnp.where(lane8 == row8 + 8 * p, 1.0, 0.0)
            for r in col:
                rows[r] = jnp.where(panel, 0.0, rows[r])
            pivots = jnp.ones((8, B), jnp.float32)
            for j in range(8):
                pivot = splat(diag[j], j)
                pivots = jnp.where(row8 == j, pivot, pivots)
                inv = 1.0 / pivot
                coef = {i: splat(diag[j], i) for i in range(j + 1, 8)}
                row, unit_row = splat(rows[p], j), splat(unit, j)
                both = jnp.where(panel, unit_row, row)
                if j < 7:
                    c = jnp.where(row8 > j, diag[j] * inv, 0.0)
                    rows[p] = rows[p] - c * row
                    unit = unit - c * unit_row
                for i in coef:
                    diag[i] = diag[i] - (diag[j] * coef[i]) * inv
                for r in col:
                    c = col[r][j] * inv
                    if r == p + 1:
                        for i in range(8):
                            after[i] = after[i] - c * splat(col[r][j], i)
                    for i in coef:
                        col[r][i] = col[r][i] - c * coef[i]
                    rows[r] = rows[r] - c * both
            s = lax.rsqrt(pivots)
            factor[p] = rows[p] * s
            inverse[p] = jnp.where(panel, unit * s, jnp.where(lane8 < 8 * p, factor[p], 0.0))
            diag = after
        if end < B // 8:
            u = jnp.concatenate(factor[start:end], 0)
            w = jnp.concatenate(inverse[start:end], 0)
            lanes = lax.broadcasted_iota(jnp.int32, w.shape, 1)
            upd = lax.dot_general(
                left_terms(u, 0),
                right_terms(jnp.where(lanes < 8 * end, w, u), 0),
                (((0,), (0,)), ((), ())),
                preferred_element_type=jnp.float32,
            )
            for r in range(end, B // 8):
                rows[r] = jnp.where(lane8 < 8 * end, 0.0, rows[r]) - upd[8 * r : 8 * r + 8]
    tri = lax.broadcasted_iota(jnp.int32, (B, B), 0) <= lax.broadcasted_iota(jnp.int32, (B, B), 1)
    return jnp.where(tri, jnp.concatenate(factor, 0), 0.0), jnp.concatenate(inverse, 0)


def product(a_terms, b_terms):
    return lax.dot_general(a_terms, b_terms, (((1,), (0,)), ((), ())), preferred_element_type=jnp.float32)


def update_upper(m_ref, row, first):
    turned, terms = left_terms(row.T, 1), right_terms(row, 0)
    for i in range(row.shape[1] // B):
        at = (first + i) * B
        m_ref[at : at + B, at:] = m_ref[at : at + B, at:] - product(turned[i * B : (i + 1) * B], terms[:, i * B :])


def eliminate(nb, m_ref, store):
    for k in range(nb):
        at, on = k * B, (k + 1) * B
        u, w = factor_block(m_ref[at:on, at:on])
        row = dot32(w, m_ref[at:on, on:]) if k < nb - 1 else None
        store(k, u, w, row)
        if row is not None:
            update_upper(m_ref, row, k + 1)


def place_parts(plan, at_ref, parts, a_ref):
    h = parts[0].shape[0]
    for a in range(plan.cores):
        for t in range(plan.chips):
            slot = (at_ref[2] ^ a) * plan.chips + (at_ref[1] ^ t)
            a_ref[pl.ds(pl.multiple_of(slot * h, h), h), :] = parts[a * plan.chips + t][...]


def first_factor_kernel(plan, at_ref, *refs):
    count = plan.chips * plan.cores
    f_ref, w_ref, a_ref, m_ref = refs[count:]
    na = f_ref.shape[0] // B
    place_parts(plan, at_ref, refs[:count], a_ref)
    for j in range(na):
        m_ref[: (j + 1) * B, j * B : (j + 1) * B] = a_ref[packed_start(j) : packed_start(j) + (j + 1) * B, :]

    f_ref[...] = jnp.zeros_like(f_ref)

    def store(k, u, w, row):
        at, on = k * B, (k + 1) * B
        f_ref[at:on, at:on] = u
        w_ref[at:on, :] = w
        if row is not None:
            f_ref[at:on, on:] = row

    eliminate(na, m_ref, store)


def first_factor(at, plan, na, parts):
    vmem = pl.BlockSpec(memory_space=pltpu.VMEM)
    return pl.pallas_call(
        functools.partial(first_factor_kernel, plan),
        out_shape=(
            jax.ShapeDtypeStruct((na * B, na * B), jnp.float32),
            jax.ShapeDtypeStruct((na * B, B), jnp.float32),
        ),
        in_specs=[pl.BlockSpec(memory_space=pltpu.SMEM)] + [vmem] * len(parts),
        out_specs=(vmem,) * 2,
        scratch_shapes=[
            pltpu.VMEM((parts[0].shape[0] * len(parts), B), jnp.float32),
            pltpu.VMEM((na * B, na * B), jnp.float32),
        ],
        compiler_params=pltpu.CompilerParams(vmem_limit_bytes=16 << 20),
        name="chol_first",
    )(at, *parts)


def last_factor_kernel(plan, at_ref, f_ref, w_ref, *refs):
    count = plan.chips * plan.cores
    out_ref, o_ref, a_ref, t_ref, m_ref, sem = refs[count:]
    n, top = o_ref.shape[0] // B, f_ref.shape[0]
    na = top // B
    place_parts(plan, at_ref, refs[:count], a_ref)
    for j in range(na, n):
        start = packed_start(j) - packed_start(na)
        lanes = slice((j - na) * B, (j - na + 1) * B)
        t_ref[:, lanes] = a_ref[start : start + top, :]
        m_ref[: (j - na + 1) * B, lanes] = a_ref[start + top : start + (j + 1) * B, :]
    o_ref[:top, :top] = f_ref[...]
    o_ref[top:, :] = jnp.zeros((n * B - top, n * B), jnp.float32)
    for k in range(na):
        rows = slice(k * B, (k + 1) * B)
        row = dot32(w_ref[rows, :], t_ref[rows, :])
        o_ref[rows, top:] = row
        if k < na - 1:
            t_ref[(k + 1) * B :, :] = t_ref[(k + 1) * B :, :] - dot32_t(f_ref[rows, (k + 1) * B :], row)
        update_upper(m_ref, row, 0)

    head = pltpu.make_async_copy(o_ref.at[pl.ds(0, top), :], out_ref.at[pl.ds(0, top), :], sem.at[n - na])
    head.start()

    copies = [head]

    def store(k, u, w, row):
        at, on = top + k * B, top + (k + 1) * B
        o_ref[at:on, at:on] = u
        if row is not None:
            o_ref[at:on, on:] = row
        copies.append(pltpu.make_async_copy(o_ref.at[pl.ds(at, B), :], out_ref.at[pl.ds(at, B), :], sem.at[k]))
        copies[-1].start()

    eliminate(n - na, m_ref, store)
    for copy in copies:
        copy.wait()


def last_factor(at, plan, n, f, w, parts):
    vmem = pl.BlockSpec(memory_space=pltpu.VMEM)
    top = f.shape[0]
    return pl.pallas_call(
        functools.partial(last_factor_kernel, plan),
        out_shape=jax.ShapeDtypeStruct((n, n), jnp.float32),
        in_specs=[pl.BlockSpec(memory_space=pltpu.SMEM)] + [vmem] * (2 + len(parts)),
        out_specs=pl.BlockSpec(memory_space=pl.ANY),
        scratch_shapes=[
            pltpu.VMEM((n, n), jnp.float32),
            pltpu.VMEM((parts[0].shape[0] * len(parts), B), jnp.float32),
            pltpu.VMEM((top, n - top), jnp.float32),
            pltpu.VMEM((n - top, n - top), jnp.float32),
            pltpu.SemaphoreType.DMA(((n - top) // B + 1,)),
        ],
        compiler_params=pltpu.CompilerParams(vmem_limit_bytes=24 << 20),
        name="chol_last",
    )(at, f, w, *parts)


def swap(x, axis, s):
    return lax.ppermute(x, axis, [(i, i ^ s) for i in range(lax.axis_size(axis))])


def scatter(pieces, axis):
    return [pieces[0]] + [swap(p, axis, -q % len(pieces)) for q, p in enumerate(pieces) if q]


def spread_out(x, axis):
    return [x] + [swap(x, axis, s) for s in range(1, lax.axis_size(axis))]


def shards(embeddings, landmarks):
    lands, chips, cores = (lax.axis_size(a) for a in ("land", "chip", "core"))
    land, chip, core = (lax.axis_index(a) for a in ("land", "chip", "core"))
    at = jnp.stack([land, chip, core]).astype(jnp.int32)
    shard = landmarks.shape[0]
    n = shard * lands
    plan = Plan(lands, chips, cores, shard // (chips * cores) % 16 == 0, embeddings.shape[0] * lands * chips * cores)

    share = shard // (chips * cores)
    own = lax.dynamic_slice_in_dim(landmarks, (chip * cores + core) * share, share, 0)
    if plan.split:
        piece = own
    else:
        piece = lax.dynamic_slice_in_dim(landmarks, chip * (shard // chips), shard // chips, 0)
    x_upper, u = own_cross(landmarks[: shard // 2], embeddings)
    z, x_upper, u = lax.optimization_barrier((spread_out(piece, "land")[1:], x_upper, u))
    slices = jnp.concatenate(z, 0)
    far = spread_out(slices, "chip")
    x_lower, x_slices = next_cross(landmarks[shard // 2 :], slices, embeddings, u)
    far, x_lower, x_slices = lax.optimization_barrier((far, x_lower, x_slices))
    if plan.split:
        for a in range(1, cores):
            far = far + [swap(f, "core", a) for f in far[:chips]]

    na = n // B // 2
    keep, send = local_normal(at, plan, na, embeddings, landmarks, own, u, x_upper, x_lower, x_slices, far)
    rows = [r // cores for r in segments(plan, na, n // B)]
    parts = scatter(add_cut(at, 1, chips, rows, [keep, swap(send, "core", 1)]), "chip")
    rows = [r // chips for r in rows]
    parts = scatter(add_cut(at, 0, lands, rows, parts), "land")
    rows = [r // lands for r in rows]
    (whole,) = add_cut(at, 0, 1, rows, parts)
    first, last = place(at, 0, rows, spread_out(whole, "land"))
    first = spread_out(first, "chip")
    first, last = lax.optimization_barrier((first + [swap(p, "core", 1) for p in first], last))
    f, w = first_factor(at, plan, na, first)
    last, f, w = lax.optimization_barrier((spread_out(last, "chip"), f, w))
    last = last + [swap(p, "core", 1) for p in last]
    return last_factor(at, plan, n, f, w, last)


def solution(mesh):
    land, rows = mesh.axis_names
    cores = 2
    fine = Mesh(mesh.devices.reshape(mesh.shape[land], mesh.shape[rows] // cores, cores), ("land", "chip", "core"))
    in_specs = (P(("land", "chip", "core"), None), P("land", None))
    return jax.shard_map(shards, mesh=fine, in_specs=in_specs, out_specs=P(), check_vma=False)
```

```python
import functools
import math
import typing

import jax
import jax.numpy as jnp
from jax import lax
from jax.experimental import pallas as pl
from jax.experimental.pallas import tpu as pltpu
from jax.sharding import Mesh
from jax.sharding import PartitionSpec as P

LAYERS = 6
SCALE_SQ = 1.0 / 32.0
RIDGE = 0.1
EPS = 1e-06
B = 128
HALF = 64
CLIP = 1.0 - 2.0**-24

ARC = (0.9426497266634519, 0.04833294295062493, 0.004716300148249888, 0.004298816276929029)
KEEP = 1.0 / (1.0 + SCALE_SQ)
ARC = tuple(c * SCALE_SQ * KEEP / math.pi for c in ARC)
GROWTH = (1.0 + SCALE_SQ) ** LAYERS


def recursion(c):
    c = jnp.clip(c, -CLIP, CLIP)
    for _ in range(LAYERS):
        w = 1.0 - jnp.abs(c)
        t = (w * w) * lax.rsqrt(w)
        poly = ARC[3]
        for a in ARC[2::-1]:
            poly = poly * w + a
        c = jnp.maximum(c, KEEP * c) + t * poly
    return c


def nt(a, b):
    return lax.dot_general(a, b, (((1,), (1,)), ((), ())), preferred_element_type=jnp.float32)


def lane_tiles_of_squares(x):
    total = None
    for l in range(0, x.shape[1], B):
        wide = x[:, l : l + B].astype(jnp.float32)
        total = wide * wide if total is None else total + wide * wide
    return total


def squares_mean_column(x):
    total = jnp.sum(lane_tiles_of_squares(x), axis=1, keepdims=True)
    return jnp.broadcast_to(total * (1.0 / x.shape[1]) + EPS, (x.shape[0], B))


def squares_mean_row(x):
    total = lane_tiles_of_squares(x)
    rows = [jnp.sum(total[i : i + B].T, axis=0, keepdims=True) for i in range(0, x.shape[0], B)]
    row = jnp.concatenate(rows, axis=1) * (1.0 / x.shape[1]) + EPS
    return jnp.broadcast_to(row, (8, x.shape[0]))


def spread(column, lanes):
    return jnp.concatenate([column] * (lanes // B), axis=1)


CHUNK = 16
LANES = 512


def fill_chunk(k_ref, r, vq, u_ref, x_ref, to, e):
    v_inv = lax.rsqrt(vq)
    v_in, v_out = v_inv * (1.0 / e), vq * v_inv * GROWTH
    for l in range(0, k_ref.shape[1], LANES):
        lanes = slice(l, l + LANES)
        up = jnp.concatenate([u_ref[:8, lanes]] * (CHUNK // 8), axis=0)
        ur = jnp.concatenate([u_ref[8:, lanes]] * (CHUNK // 8), axis=0)
        c = recursion(k_ref[pl.ds(r, CHUNK), lanes] * up * spread(v_in, LANES))
        x_ref[pl.ds(to, CHUNK), lanes] = (c * ur * spread(v_out, LANES)).astype(jnp.bfloat16)


def loop_chunks(chunks, most, chunk, beside=None):
    together = max(d for d in range(1, most + 1) if chunks % d == 0)

    def part(i, _):
        for q in range(together):
            chunk(i * together + q)
        if beside is not None:
            beside(i, chunks // together)
        return 0

    lax.fori_loop(0, chunks // together, part, 0)


def fill_cross(marks_ref, emb_ref, u_ref, k_ref, vq_ref, x_ref, most):
    rows, e = marks_ref.shape
    k_ref[:rows, :] = nt(marks_ref[...], emb_ref[...])
    vq_ref[:rows, :] = squares_mean_column(marks_ref[...])

    def chunk(i):
        r = pl.multiple_of(i * CHUNK, CHUNK)
        fill_chunk(k_ref, r, vq_ref[pl.ds(r, CHUNK), :], u_ref, x_ref, r, e)

    loop_chunks(rows // CHUNK, most, chunk)


def fill_shards(marks_ref, emb_ref, u_ref, k_refs, vq_ref, x_ref, chunks, rows_of):
    m, e = emb_ref.shape
    shard = marks_ref.shape[0] // len(k_refs)
    vq_ref[...] = squares_mean_column(marks_ref[...])
    k_refs[0][...] = nt(marks_ref[:shard, :], emb_ref[...])
    for s, k_ref in enumerate(k_refs):

        def chunk(i):
            r, to = (pl.multiple_of(at, CHUNK) for at in rows_of(s, i))
            fill_chunk(k_ref, r, vq_ref[pl.ds(s * shard + r, CHUNK), :], u_ref, x_ref, to, e)

        def beside(step, steps):
            span = m // steps
            at = pl.ds(pl.multiple_of(step * span, B), span)
            k_refs[s + 1][:, at] = nt(marks_ref[(s + 1) * shard : (s + 2) * shard, :], emb_ref[at, :])

        steps = chunks // max(d for d in range(1, 8) if chunks % d == 0)
        if s + 1 < len(k_refs) and m % (steps * B):
            k_refs[s + 1][...] = nt(marks_ref[(s + 1) * shard : (s + 2) * shard, :], emb_ref[...])
            loop_chunks(chunks, 7, chunk)
        else:
            loop_chunks(chunks, 7, chunk, beside if s + 1 < len(k_refs) else None)


def own_kernel(marks_ref, emb_ref, x_ref, u_ref, k_ref, vq_ref):
    uq = squares_mean_row(emb_ref[...])
    inv = lax.rsqrt(uq)
    u_ref[:8, :] = inv
    u_ref[8:, :] = uq * inv
    fill_cross(marks_ref, emb_ref, u_ref, k_ref, vq_ref, x_ref, 8)


def own_cross(landmarks, embeddings):
    m = embeddings.shape[0]
    rows = landmarks.shape[0]
    vmem = pl.BlockSpec(memory_space=pltpu.VMEM)
    return pl.pallas_call(
        own_kernel,
        out_shape=(jax.ShapeDtypeStruct((rows, m), jnp.bfloat16), jax.ShapeDtypeStruct((16, m), jnp.float32)),
        in_specs=[vmem] * 2,
        out_specs=(vmem, vmem),
        scratch_shapes=[pltpu.VMEM((rows, m), jnp.float32), pltpu.VMEM((rows, B), jnp.float32)],
        compiler_params=pltpu.CompilerParams(vmem_limit_bytes=12 << 20),
        name="own_cross",
    )(landmarks, embeddings)


def next_kernel(marks_ref, slices_ref, emb_ref, u_ref, x_ref, x_slices_ref, k_ref, vq_ref):
    for m_ref, to_ref in ((marks_ref, x_ref), (slices_ref, x_slices_ref)):
        fill_cross(m_ref, emb_ref, u_ref, k_ref, vq_ref, to_ref, 2)


def next_cross(landmarks, slices, embeddings, u):
    m = embeddings.shape[0]
    rows = max(landmarks.shape[0], slices.shape[0])
    vmem = pl.BlockSpec(memory_space=pltpu.VMEM)
    return pl.pallas_call(
        next_kernel,
        out_shape=tuple(jax.ShapeDtypeStruct((x.shape[0], m), jnp.bfloat16) for x in (landmarks, slices)),
        in_specs=[vmem] * 4,
        out_specs=(vmem, vmem),
        scratch_shapes=[pltpu.VMEM((rows, m), jnp.float32), pltpu.VMEM((rows, B), jnp.float32)],
        compiler_params=pltpu.CompilerParams(vmem_limit_bytes=12 << 20),
        name="next_cross",
    )(landmarks, slices, embeddings, u)


class Plan(typing.NamedTuple):
    lands: int
    chips: int
    cores: int
    split: bool
    all_points: int


def gram_kernel(plan, na, at_ref, emb_ref, mine_ref, own_ref, u_ref, x_upper_ref, x_lower_ref, x_slices_ref, *refs):
    lands, chips, cores, split, all_points = plan
    count = chips * (cores if split else 1)
    far = refs[:count]
    keep_ref, send_ref, x_ref, ridge_ref, marks_ref, vq_ref, out_ref, *k_refs = refs[count:]
    shard, e = mine_ref.shape
    n = shard * lands
    land, chip, core = at_ref[0], at_ref[1], at_ref[2]
    here = pl.multiple_of(land * shard, shard)
    x_ref[pl.ds(here, shard // 2), :] = x_upper_ref[...]
    x_ref[pl.ds(pl.multiple_of(here + shard // 2, CHUNK), shard // 2), :] = x_lower_ref[...]
    piece = far[0].shape[0] // (lands - 1)
    for a in range(cores if split else 1):
        for t in range(chips):
            slot = ((chip ^ t) * cores + (core ^ a)) if split else (chip ^ t)
            for s in range(1, lands):
                to = pl.multiple_of((s - 1) * shard + slot * piece, piece)
                marks_ref[pl.ds(to, piece), :] = far[a * chips + t][(s - 1) * piece : s * piece, :]

    slots = shard // piece
    mine = chip * cores + core if split else chip
    for s in range(1, lands):
        to = pl.multiple_of((land ^ s) * shard + mine * piece, piece)
        x_ref[pl.ds(to, piece), :] = x_slices_ref[(s - 1) * piece : s * piece, :]
    steps = piece // CHUNK

    def rows_of(s, i):
        at = (mine ^ (i // steps + 1)) * piece + i % steps * CHUNK
        return at, (land ^ (s + 1)) * shard + at

    fill_shards(marks_ref, emb_ref, u_ref, k_refs, vq_ref, x_ref, (slots - 1) * steps, rows_of)

    share = own_ref.shape[0]
    oq = squares_mean_column(own_ref[...])
    o_inv = lax.rsqrt(oq)

    def ridge(marks, marks_q, to):
        k_own = nt(own_ref[...], marks)
        for l in range(0, shard, B):
            vq = marks_q[l : l + B].T[:8]
            v_inv = lax.rsqrt(vq)
            for i in range(share // 8):
                oi = o_inv[8 * i : 8 * i + 8]
                c = recursion(k_own[8 * i : 8 * i + 8, l : l + B] * v_inv * (oi * (1.0 / e)))
                root = oq[8 * i : 8 * i + 8] * oi
                ridge_ref[8 * i : 8 * i + 8, pl.ds(to + l, B)] = c * (vq * v_inv) * (root * (RIDGE * GROWTH))

    ridge(mine_ref[...], squares_mean_column(mine_ref[...]), here)
    for s in range(1, lands):
        rows = slice((s - 1) * shard, s * shard)
        ridge(marks_ref[rows, :], vq_ref[rows, :], pl.multiple_of((land ^ s) * shard, shard))

    position = land * shard + (chip * cores + core) * share
    row_block = position // B
    offset = position % B
    wide = 2 * B
    for w in range(n // wide):
        both = nt(x_ref[: (w + 1) * wide, :], x_ref[w * wide : (w + 1) * wide, :]) * (1.0 / all_points)
        for j in (2 * w, 2 * w + 1):
            start = column_start(plan, na, j)
            out_ref[start : start + (j + 1) * B, :] = both[: (j + 1) * B, (j % 2) * B : (j % 2 + 1) * B]
    for j in range(n // B):
        start = column_start(plan, na, j)

        @pl.when(row_block <= j)
        def _():
            at = pl.ds(pl.multiple_of(start + row_block * B + offset, share), share)
            out_ref[at, :] = out_ref[at, :] + ridge_ref[:, j * B : (j + 1) * B]

    done = base = 0
    for rows in segments(plan, na, n // B):
        half = rows // cores
        to = slice(done, done + half)
        keep_ref[to, :] = out_ref[pl.ds(pl.multiple_of(base + core * half, 8), half), :]
        send_ref[to, :] = out_ref[pl.ds(pl.multiple_of(base + (1 - core) * half, 8), half), :]
        done, base = done + half, base + rows


def packed_start(j):
    return j * (j + 1) // 2 * B


def segments(plan, na, nb):
    unit = 8 * plan.lands * plan.chips * plan.cores
    return [-(-rows // unit) * unit for rows in (packed_start(na), packed_start(nb) - packed_start(na))]


def column_start(plan, na, j):
    return packed_start(j) if j < na else packed_start(j) - packed_start(na) + segments(plan, na, j)[0]


def local_normal(at, plan, na, embeddings, landmarks, own, u, x_upper, x_lower, x_slices, far):
    n, m = landmarks.shape[0] * plan.lands, embeddings.shape[0]
    away = n - landmarks.shape[0]
    rows = sum(segments(plan, na, n // B))
    half = jax.ShapeDtypeStruct((rows // plan.cores, B), jnp.float32)
    vmem = pl.BlockSpec(memory_space=pltpu.VMEM)
    return pl.pallas_call(
        functools.partial(gram_kernel, plan, na),
        out_shape=(half, half),
        in_specs=[pl.BlockSpec(memory_space=pltpu.SMEM)] + [vmem] * (7 + len(far)),
        out_specs=(vmem,) * 2,
        scratch_shapes=[
            pltpu.VMEM((n, m), jnp.bfloat16),
            pltpu.VMEM((own.shape[0], n), jnp.float32),
            pltpu.VMEM((away, landmarks.shape[1]), jnp.bfloat16),
            pltpu.VMEM((away, B), jnp.float32),
            pltpu.VMEM((rows, B), jnp.float32),
        ]
        + [pltpu.VMEM((landmarks.shape[0], m), jnp.float32)] * (plan.lands - 1),
        compiler_params=pltpu.CompilerParams(vmem_limit_bytes=24 << 20),
        name="gram",
    )(at, embeddings, landmarks, own, u, x_upper, x_lower, x_slices, *far)


def add_cut_kernel(ways, axis, parts, at_ref, *refs):
    ins, outs = refs[: len(refs) - ways], refs[len(refs) - ways :]
    base = 0
    for rows in parts:
        h = rows // ways
        for q in range(ways):
            s = -q % ways
            at = pl.ds(pl.multiple_of(base + (at_ref[axis] ^ s) * h, 8), h) if ways > 1 else slice(base, base + h)
            total = ins[0][at, :]
            for r in ins[1:]:
                total = total + r[at, :]
            outs[q][base // ways : base // ways + h, :] = total
        base += rows


def add_cut(at, axis, ways, parts, ins):
    h = sum(parts) // ways
    vmem = pl.BlockSpec(memory_space=pltpu.VMEM)
    return pl.pallas_call(
        functools.partial(add_cut_kernel, ways, axis, parts),
        out_shape=tuple([jax.ShapeDtypeStruct((h, B), jnp.float32)] * ways),
        in_specs=[pl.BlockSpec(memory_space=pltpu.SMEM)] + [vmem] * len(ins),
        out_specs=tuple([vmem] * ways),
        compiler_params=pltpu.CompilerParams(vmem_limit_bytes=8 << 20),
        name="add_cut",
    )(at, *ins)


def place_kernel(axis, ways, parts, at_ref, *refs):
    ins, outs = refs[:ways], refs[ways:]
    base = 0
    for out, h in zip(outs, parts):
        for s in range(ways):
            out[pl.ds(pl.multiple_of((at_ref[axis] ^ s) * h, 8), h), :] = ins[s][base : base + h, :]
        base += h


def place(at, axis, parts, ins):
    vmem = pl.BlockSpec(memory_space=pltpu.VMEM)
    return pl.pallas_call(
        functools.partial(place_kernel, axis, len(ins), parts),
        out_shape=tuple(jax.ShapeDtypeStruct((h * len(ins), B), jnp.float32) for h in parts),
        in_specs=[pl.BlockSpec(memory_space=pltpu.SMEM)] + [vmem] * len(ins),
        out_specs=(vmem,) * len(parts),
        compiler_params=pltpu.CompilerParams(vmem_limit_bytes=8 << 20),
        name="place",
    )(at, *ins)


def thirds(x):
    h = x.astype(jnp.bfloat16)
    r = x - h.astype(jnp.float32)
    m = r.astype(jnp.bfloat16)
    return h, m, (r - m.astype(jnp.float32)).astype(jnp.bfloat16)

def left_terms(x, axis):
    h, m, l = thirds(x)
    return jnp.concatenate([h, h, h, m, m, l], axis)

def right_terms(x, axis):
    h, m, l = thirds(x)
    return jnp.concatenate([h, m, l, h, m, h], axis)

def dot32(a, b):
    return lax.dot_general(left_terms(a, 1), right_terms(b, 0), (((1,), (0,)), ((), ())), preferred_element_type=jnp.float32)

def dot32_t(a, b):
    return dot32(a.T, b)

def factor_block(d):
    row8 = lax.broadcasted_iota(jnp.int32, (8, B), 0)
    lane8 = lax.broadcasted_iota(jnp.int32, (8, B), 1)
    rows = [d[i : i + 8] for i in range(0, B, 8)]
    factor, inverse = [None] * (B // 8), [None] * (B // 8)
    zero = rows[0] * 0.0
    half = HALF // 8

    def spread_columns(x, lane):
        columns = [jnp.broadcast_to(x[:, lane + i : lane + i + 1], (8, B)) for i in range(8)]
        return [columns[0] + zero] + columns[1:]

    def splat(x, r):
        return jnp.broadcast_to(x[r : r + 1], (8, B))

    for start in range(0, B // 8, half):
        end = start + half
        diag = spread_columns(rows[start], 8 * start)
        for p in range(start, end):
            col = {r: spread_columns(rows[r], 8 * p) for r in range(p + 1, end)}
            after = spread_columns(rows[p + 1], 8 * p + 8) if p + 1 < end else None
            panel = (lane8 >= 8 * p) & (lane8 < 8 * p + 8)
            unit = jnp.where(lane8 == row8 + 8 * p, 1.0, 0.0)
            for r in col:
                rows[r] = jnp.where(panel, 0.0, rows[r])
            pivots = jnp.ones((8, B), jnp.float32)
            for j in range(8):
                pivot = splat(diag[j], j)
                pivots = jnp.where(row8 == j, pivot, pivots)
                inv = 1.0 / pivot
                coef = {i: splat(diag[j], i) for i in range(j + 1, 8)}
                row, unit_row = splat(rows[p], j), splat(unit, j)
                both = jnp.where(panel, unit_row, row)
                if j < 7:
                    c = jnp.where(row8 > j, diag[j] * inv, 0.0)
                    rows[p] = rows[p] - c * row
                    unit = unit - c * unit_row
                for i in coef:
                    diag[i] = diag[i] - (diag[j] * coef[i]) * inv
                for r in col:
                    c = col[r][j] * inv
                    if r == p + 1:
                        for i in range(8):
                            after[i] = after[i] - c * splat(col[r][j], i)
                    for i in coef:
                        col[r][i] = col[r][i] - c * coef[i]
                    rows[r] = rows[r] - c * both
            s = lax.rsqrt(pivots)
            factor[p] = rows[p] * s
            inverse[p] = jnp.where(panel, unit * s, jnp.where(lane8 < 8 * p, factor[p], 0.0))
            diag = after
        if end < B // 8:
            u = jnp.concatenate(factor[start:end], 0)
            w = jnp.concatenate(inverse[start:end], 0)
            lanes = lax.broadcasted_iota(jnp.int32, w.shape, 1)
            upd = lax.dot_general(
                left_terms(u, 0),
                right_terms(jnp.where(lanes < 8 * end, w, u), 0),
                (((0,), (0,)), ((), ())),
                preferred_element_type=jnp.float32,
            )
            for r in range(end, B // 8):
                rows[r] = jnp.where(lane8 < 8 * end, 0.0, rows[r]) - upd[8 * r : 8 * r + 8]
    tri = lax.broadcasted_iota(jnp.int32, (B, B), 0) <= lax.broadcasted_iota(jnp.int32, (B, B), 1)
    return jnp.where(tri, jnp.concatenate(factor, 0), 0.0), jnp.concatenate(inverse, 0)


def product(a_terms, b_terms):
    return lax.dot_general(a_terms, b_terms, (((1,), (0,)), ((), ())), preferred_element_type=jnp.float32)


def update_upper(m_ref, row, first):
    turned, terms = left_terms(row.T, 1), right_terms(row, 0)
    for i in range(row.shape[1] // B):
        at = (first + i) * B
        m_ref[at : at + B, at:] = m_ref[at : at + B, at:] - product(turned[i * B : (i + 1) * B], terms[:, i * B :])


def eliminate(nb, m_ref, store):
    for k in range(nb):
        at, on = k * B, (k + 1) * B
        u, w = factor_block(m_ref[at:on, at:on])
        row = dot32(w, m_ref[at:on, on:]) if k < nb - 1 else None
        store(k, u, w, row)
        if row is not None:
            update_upper(m_ref, row, k + 1)


def place_parts(plan, at_ref, parts, a_ref):
    h = parts[0].shape[0]
    for a in range(plan.cores):
        for t in range(plan.chips):
            slot = (at_ref[2] ^ a) * plan.chips + (at_ref[1] ^ t)
            a_ref[pl.ds(pl.multiple_of(slot * h, h), h), :] = parts[a * plan.chips + t][...]


def first_factor_kernel(plan, at_ref, *refs):
    count = plan.chips * plan.cores
    f_ref, w_ref, a_ref, m_ref = refs[count:]
    na = f_ref.shape[0] // B
    place_parts(plan, at_ref, refs[:count], a_ref)
    for j in range(na):
        m_ref[: (j + 1) * B, j * B : (j + 1) * B] = a_ref[packed_start(j) : packed_start(j) + (j + 1) * B, :]

    f_ref[...] = jnp.zeros_like(f_ref)

    def store(k, u, w, row):
        at, on = k * B, (k + 1) * B
        f_ref[at:on, at:on] = u
        w_ref[at:on, :] = w
        if row is not None:
            f_ref[at:on, on:] = row

    eliminate(na, m_ref, store)


def first_factor(at, plan, na, parts):
    vmem = pl.BlockSpec(memory_space=pltpu.VMEM)
    return pl.pallas_call(
        functools.partial(first_factor_kernel, plan),
        out_shape=(
            jax.ShapeDtypeStruct((na * B, na * B), jnp.float32),
            jax.ShapeDtypeStruct((na * B, B), jnp.float32),
        ),
        in_specs=[pl.BlockSpec(memory_space=pltpu.SMEM)] + [vmem] * len(parts),
        out_specs=(vmem,) * 2,
        scratch_shapes=[
            pltpu.VMEM((parts[0].shape[0] * len(parts), B), jnp.float32),
            pltpu.VMEM((na * B, na * B), jnp.float32),
        ],
        compiler_params=pltpu.CompilerParams(vmem_limit_bytes=16 << 20),
        name="chol_first",
    )(at, *parts)


def last_factor_kernel(plan, at_ref, f_ref, w_ref, *refs):
    count = plan.chips * plan.cores
    out_ref, o_ref, a_ref, t_ref, m_ref, sem = refs[count:]
    n, top = o_ref.shape[0] // B, f_ref.shape[0]
    na = top // B
    place_parts(plan, at_ref, refs[:count], a_ref)
    for j in range(na, n):
        start = packed_start(j) - packed_start(na)
        lanes = slice((j - na) * B, (j - na + 1) * B)
        t_ref[:, lanes] = a_ref[start : start + top, :]
        m_ref[: (j - na + 1) * B, lanes] = a_ref[start + top : start + (j + 1) * B, :]
    o_ref[:top, :top] = f_ref[...]
    o_ref[top:, :] = jnp.zeros((n * B - top, n * B), jnp.float32)
    for k in range(na):
        rows = slice(k * B, (k + 1) * B)
        row = dot32(w_ref[rows, :], t_ref[rows, :])
        o_ref[rows, top:] = row
        if k < na - 1:
            t_ref[(k + 1) * B :, :] = t_ref[(k + 1) * B :, :] - dot32_t(f_ref[rows, (k + 1) * B :], row)
        update_upper(m_ref, row, 0)

    head = pltpu.make_async_copy(o_ref.at[pl.ds(0, top), :], out_ref.at[pl.ds(0, top), :], sem.at[n - na])
    head.start()

    copies = [head]

    def store(k, u, w, row):
        at, on = top + k * B, top + (k + 1) * B
        o_ref[at:on, at:on] = u
        if row is not None:
            o_ref[at:on, on:] = row
        copies.append(pltpu.make_async_copy(o_ref.at[pl.ds(at, B), :], out_ref.at[pl.ds(at, B), :], sem.at[k]))
        copies[-1].start()

    eliminate(n - na, m_ref, store)
    for copy in copies:
        copy.wait()


def last_factor(at, plan, n, f, w, parts):
    vmem = pl.BlockSpec(memory_space=pltpu.VMEM)
    top = f.shape[0]
    return pl.pallas_call(
        functools.partial(last_factor_kernel, plan),
        out_shape=jax.ShapeDtypeStruct((n, n), jnp.float32),
        in_specs=[pl.BlockSpec(memory_space=pltpu.SMEM)] + [vmem] * (2 + len(parts)),
        out_specs=pl.BlockSpec(memory_space=pl.ANY),
        scratch_shapes=[
            pltpu.VMEM((n, n), jnp.float32),
            pltpu.VMEM((parts[0].shape[0] * len(parts), B), jnp.float32),
            pltpu.VMEM((top, n - top), jnp.float32),
            pltpu.VMEM((n - top, n - top), jnp.float32),
            pltpu.SemaphoreType.DMA(((n - top) // B + 1,)),
        ],
        compiler_params=pltpu.CompilerParams(vmem_limit_bytes=24 << 20),
        name="chol_last",
    )(at, f, w, *parts)


def swap(x, axis, s):
    return lax.ppermute(x, axis, [(i, i ^ s) for i in range(lax.axis_size(axis))])


def scatter(pieces, axis):
    return [pieces[0]] + [swap(p, axis, -q % len(pieces)) for q, p in enumerate(pieces) if q]


def spread_out(x, axis):
    return [x] + [swap(x, axis, s) for s in range(1, lax.axis_size(axis))]


def shards(embeddings, landmarks):
    lands, chips, cores = (lax.axis_size(a) for a in ("land", "chip", "core"))
    land, chip, core = (lax.axis_index(a) for a in ("land", "chip", "core"))
    at = jnp.stack([land, chip, core]).astype(jnp.int32)
    shard = landmarks.shape[0]
    n = shard * lands
    plan = Plan(lands, chips, cores, shard // (chips * cores) % 16 == 0, embeddings.shape[0] * lands * chips * cores)

    share = shard // (chips * cores)
    own = lax.dynamic_slice_in_dim(landmarks, (chip * cores + core) * share, share, 0)
    if plan.split:
        piece = own
    else:
        piece = lax.dynamic_slice_in_dim(landmarks, chip * (shard // chips), shard // chips, 0)
    x_upper, u = own_cross(landmarks[: shard // 2], embeddings)
    z, x_upper, u = lax.optimization_barrier((spread_out(piece, "land")[1:], x_upper, u))
    slices = jnp.concatenate(z, 0)
    far = spread_out(slices, "chip")
    x_lower, x_slices = next_cross(landmarks[shard // 2 :], slices, embeddings, u)
    far, x_lower, x_slices = lax.optimization_barrier((far, x_lower, x_slices))
    if plan.split:
        for a in range(1, cores):
            far = far + [swap(f, "core", a) for f in far[:chips]]

    na = n // B // 2
    keep, send = local_normal(at, plan, na, embeddings, landmarks, own, u, x_upper, x_lower, x_slices, far)
    rows = [r // cores for r in segments(plan, na, n // B)]
    parts = scatter(add_cut(at, 1, chips, rows, [keep, swap(send, "core", 1)]), "chip")
    rows = [r // chips for r in rows]
    parts = scatter(add_cut(at, 0, lands, rows, parts), "land")
    rows = [r // lands for r in rows]
    (whole,) = add_cut(at, 0, 1, rows, parts)
    first, last = place(at, 0, rows, spread_out(whole, "land"))
    first = spread_out(first, "chip")
    first, last = lax.optimization_barrier((first + [swap(p, "core", 1) for p in first], last))
    f, w = first_factor(at, plan, na, first)
    last, f, w = lax.optimization_barrier((spread_out(last, "chip"), f, w))
    last = last + [swap(p, "core", 1) for p in last]
    return last_factor(at, plan, n, f, w, last)


def solution(mesh):
    land, rows = mesh.axis_names
    cores = 2
    fine = Mesh(mesh.devices.reshape(mesh.shape[land], mesh.shape[rows] // cores, cores), ("land", "chip", "core"))
    in_specs = (P(("land", "chip", "core"), None), P("land", None))
    return jax.shard_map(shards, mesh=fine, in_specs=in_specs, out_specs=P(), check_vma=False)
```

```python
import functools
import math
import typing

import jax
import jax.numpy as jnp
from jax import lax
from jax.experimental import pallas as pl
from jax.experimental.pallas import tpu as pltpu
from jax.sharding import Mesh
from jax.sharding import PartitionSpec as P

LAYERS = 6
SCALE_SQ = 1.0 / 32.0
RIDGE = 0.1
EPS = 1e-06
B = 128
HALF = 64
CLIP = 1.0 - 2.0**-24

ARC = (0.9426497266634519, 0.04833294295062493, 0.004716300148249888, 0.004298816276929029)
KEEP = 1.0 / (1.0 + SCALE_SQ)
ARC = tuple(c * SCALE_SQ * KEEP / math.pi for c in ARC)
GROWTH = (1.0 + SCALE_SQ) ** LAYERS


def recursion(c):
    c = jnp.clip(c, -CLIP, CLIP)
    for _ in range(LAYERS):
        w = 1.0 - jnp.abs(c)
        t = (w * w) * lax.rsqrt(w)
        poly = ARC[3]
        for a in ARC[2::-1]:
            poly = poly * w + a
        c = jnp.maximum(c, KEEP * c) + t * poly
    return c


def nt(a, b):
    return lax.dot_general(a, b, (((1,), (1,)), ((), ())), preferred_element_type=jnp.float32)


def lane_tiles_of_squares(x):
    total = None
    for l in range(0, x.shape[1], B):
        wide = x[:, l : l + B].astype(jnp.float32)
        total = wide * wide if total is None else total + wide * wide
    return total


def squares_mean_column(x):
    total = jnp.sum(lane_tiles_of_squares(x), axis=1, keepdims=True)
    return jnp.broadcast_to(total * (1.0 / x.shape[1]) + EPS, (x.shape[0], B))


def squares_mean_row(x):
    total = lane_tiles_of_squares(x)
    rows = [jnp.sum(total[i : i + B].T, axis=0, keepdims=True) for i in range(0, x.shape[0], B)]
    row = jnp.concatenate(rows, axis=1) * (1.0 / x.shape[1]) + EPS
    return jnp.broadcast_to(row, (8, x.shape[0]))


def spread(column, lanes):
    return jnp.concatenate([column] * (lanes // B), axis=1)


CHUNK = 16
LANES = 512


def fill_chunk(k_ref, r, vq, u_ref, x_ref, to, e):
    v_inv = lax.rsqrt(vq)
    v_in, v_out = v_inv * (1.0 / e), vq * v_inv * GROWTH
    for l in range(0, k_ref.shape[1], LANES):
        lanes = slice(l, l + LANES)
        up = jnp.concatenate([u_ref[:8, lanes]] * (CHUNK // 8), axis=0)
        ur = jnp.concatenate([u_ref[8:, lanes]] * (CHUNK // 8), axis=0)
        c = recursion(k_ref[pl.ds(r, CHUNK), lanes] * up * spread(v_in, LANES))
        x_ref[pl.ds(to, CHUNK), lanes] = (c * ur * spread(v_out, LANES)).astype(jnp.bfloat16)


def loop_chunks(chunks, most, chunk, beside=None):
    together = max(d for d in range(1, most + 1) if chunks % d == 0)

    def part(i, _):
        for q in range(together):
            chunk(i * together + q)
        if beside is not None:
            beside(i, chunks // together)
        return 0

    lax.fori_loop(0, chunks // together, part, 0)


def fill_cross(marks_ref, emb_ref, u_ref, k_ref, vq_ref, x_ref, most):
    rows, e = marks_ref.shape
    k_ref[:rows, :] = nt(marks_ref[...], emb_ref[...])
    vq_ref[:rows, :] = squares_mean_column(marks_ref[...])

    def chunk(i):
        r = pl.multiple_of(i * CHUNK, CHUNK)
        fill_chunk(k_ref, r, vq_ref[pl.ds(r, CHUNK), :], u_ref, x_ref, r, e)

    loop_chunks(rows // CHUNK, most, chunk)


def fill_shards(marks_ref, emb_ref, u_ref, k_refs, vq_ref, x_ref, chunks, rows_of):
    m, e = emb_ref.shape
    shard = marks_ref.shape[0] // len(k_refs)
    vq_ref[...] = squares_mean_column(marks_ref[...])
    k_refs[0][...] = nt(marks_ref[:shard, :], emb_ref[...])
    for s, k_ref in enumerate(k_refs):

        def chunk(i):
            r, to = (pl.multiple_of(at, CHUNK) for at in rows_of(s, i))
            fill_chunk(k_ref, r, vq_ref[pl.ds(s * shard + r, CHUNK), :], u_ref, x_ref, to, e)

        def beside(step, steps):
            span = m // steps
            at = pl.ds(pl.multiple_of(step * span, B), span)
            k_refs[s + 1][:, at] = nt(marks_ref[(s + 1) * shard : (s + 2) * shard, :], emb_ref[at, :])

        steps = chunks // max(d for d in range(1, 8) if chunks % d == 0)
        if s + 1 < len(k_refs) and m % (steps * B):
            k_refs[s + 1][...] = nt(marks_ref[(s + 1) * shard : (s + 2) * shard, :], emb_ref[...])
            loop_chunks(chunks, 7, chunk)
        else:
            loop_chunks(chunks, 7, chunk, beside if s + 1 < len(k_refs) else None)


def own_kernel(marks_ref, emb_ref, x_ref, u_ref, k_ref, vq_ref):
    uq = squares_mean_row(emb_ref[...])
    inv = lax.rsqrt(uq)
    u_ref[:8, :] = inv
    u_ref[8:, :] = uq * inv
    fill_cross(marks_ref, emb_ref, u_ref, k_ref, vq_ref, x_ref, 8)


def own_cross(landmarks, embeddings):
    m = embeddings.shape[0]
    rows = landmarks.shape[0]
    vmem = pl.BlockSpec(memory_space=pltpu.VMEM)
    return pl.pallas_call(
        own_kernel,
        out_shape=(jax.ShapeDtypeStruct((rows, m), jnp.bfloat16), jax.ShapeDtypeStruct((16, m), jnp.float32)),
        in_specs=[vmem] * 2,
        out_specs=(vmem, vmem),
        scratch_shapes=[pltpu.VMEM((rows, m), jnp.float32), pltpu.VMEM((rows, B), jnp.float32)],
        compiler_params=pltpu.CompilerParams(vmem_limit_bytes=12 << 20),
        name="own_cross",
    )(landmarks, embeddings)


def next_kernel(marks_ref, slices_ref, emb_ref, u_ref, x_ref, x_slices_ref, k_ref, vq_ref):
    for m_ref, to_ref in ((marks_ref, x_ref), (slices_ref, x_slices_ref)):
        fill_cross(m_ref, emb_ref, u_ref, k_ref, vq_ref, to_ref, 2)


def next_cross(landmarks, slices, embeddings, u):
    m = embeddings.shape[0]
    rows = max(landmarks.shape[0], slices.shape[0])
    vmem = pl.BlockSpec(memory_space=pltpu.VMEM)
    return pl.pallas_call(
        next_kernel,
        out_shape=tuple(jax.ShapeDtypeStruct((x.shape[0], m), jnp.bfloat16) for x in (landmarks, slices)),
        in_specs=[vmem] * 4,
        out_specs=(vmem, vmem),
        scratch_shapes=[pltpu.VMEM((rows, m), jnp.float32), pltpu.VMEM((rows, B), jnp.float32)],
        compiler_params=pltpu.CompilerParams(vmem_limit_bytes=12 << 20),
        name="next_cross",
    )(landmarks, slices, embeddings, u)


class Plan(typing.NamedTuple):
    lands: int
    chips: int
    cores: int
    split: bool
    all_points: int


def gram_kernel(plan, na, at_ref, emb_ref, mine_ref, own_ref, u_ref, x_upper_ref, x_lower_ref, x_slices_ref, *refs):
    lands, chips, cores, split, all_points = plan
    count = chips * (cores if split else 1)
    far = refs[:count]
    keep_ref, send_ref, x_ref, ridge_ref, marks_ref, vq_ref, out_ref, *k_refs = refs[count:]
    shard, e = mine_ref.shape
    n = shard * lands
    land, chip, core = at_ref[0], at_ref[1], at_ref[2]
    here = pl.multiple_of(land * shard, shard)
    x_ref[pl.ds(here, shard // 2), :] = x_upper_ref[...]
    x_ref[pl.ds(pl.multiple_of(here + shard // 2, CHUNK), shard // 2), :] = x_lower_ref[...]
    piece = far[0].shape[0] // (lands - 1)
    for a in range(cores if split else 1):
        for t in range(chips):
            slot = ((chip ^ t) * cores + (core ^ a)) if split else (chip ^ t)
            for s in range(1, lands):
                to = pl.multiple_of((s - 1) * shard + slot * piece, piece)
                marks_ref[pl.ds(to, piece), :] = far[a * chips + t][(s - 1) * piece : s * piece, :]

    slots = shard // piece
    mine = chip * cores + core if split else chip
    for s in range(1, lands):
        to = pl.multiple_of((land ^ s) * shard + mine * piece, piece)
        x_ref[pl.ds(to, piece), :] = x_slices_ref[(s - 1) * piece : s * piece, :]
    steps = piece // CHUNK

    def rows_of(s, i):
        at = (mine ^ (i // steps + 1)) * piece + i % steps * CHUNK
        return at, (land ^ (s + 1)) * shard + at

    fill_shards(marks_ref, emb_ref, u_ref, k_refs, vq_ref, x_ref, (slots - 1) * steps, rows_of)

    share = own_ref.shape[0]
    oq = squares_mean_column(own_ref[...])
    o_inv = lax.rsqrt(oq)

    def ridge(marks, marks_q, to):
        k_own = nt(own_ref[...], marks)
        for l in range(0, shard, B):
            vq = marks_q[l : l + B].T[:8]
            v_inv = lax.rsqrt(vq)
            for i in range(share // 8):
                oi = o_inv[8 * i : 8 * i + 8]
                c = recursion(k_own[8 * i : 8 * i + 8, l : l + B] * v_inv * (oi * (1.0 / e)))
                root = oq[8 * i : 8 * i + 8] * oi
                ridge_ref[8 * i : 8 * i + 8, pl.ds(to + l, B)] = c * (vq * v_inv) * (root * (RIDGE * GROWTH))

    ridge(mine_ref[...], squares_mean_column(mine_ref[...]), here)
    for s in range(1, lands):
        rows = slice((s - 1) * shard, s * shard)
        ridge(marks_ref[rows, :], vq_ref[rows, :], pl.multiple_of((land ^ s) * shard, shard))

    position = land * shard + (chip * cores + core) * share
    row_block = position // B
    offset = position % B
    wide = 2 * B
    for w in range(n // wide):
        both = nt(x_ref[: (w + 1) * wide, :], x_ref[w * wide : (w + 1) * wide, :]) * (1.0 / all_points)
        for j in (2 * w, 2 * w + 1):
            start = column_start(plan, na, j)
            out_ref[start : start + (j + 1) * B, :] = both[: (j + 1) * B, (j % 2) * B : (j % 2 + 1) * B]
    for j in range(n // B):
        start = column_start(plan, na, j)

        @pl.when(row_block <= j)
        def _():
            at = pl.ds(pl.multiple_of(start + row_block * B + offset, share), share)
            out_ref[at, :] = out_ref[at, :] + ridge_ref[:, j * B : (j + 1) * B]

    done = base = 0
    for rows in segments(plan, na, n // B):
        half = rows // cores
        to = slice(done, done + half)
        keep_ref[to, :] = out_ref[pl.ds(pl.multiple_of(base + core * half, 8), half), :]
        send_ref[to, :] = out_ref[pl.ds(pl.multiple_of(base + (1 - core) * half, 8), half), :]
        done, base = done + half, base + rows


def packed_start(j):
    return j * (j + 1) // 2 * B


def segments(plan, na, nb):
    unit = 8 * plan.lands * plan.chips * plan.cores
    return [-(-rows // unit) * unit for rows in (packed_start(na), packed_start(nb) - packed_start(na))]


def column_start(plan, na, j):
    return packed_start(j) if j < na else packed_start(j) - packed_start(na) + segments(plan, na, j)[0]


def local_normal(at, plan, na, embeddings, landmarks, own, u, x_upper, x_lower, x_slices, far):
    n, m = landmarks.shape[0] * plan.lands, embeddings.shape[0]
    away = n - landmarks.shape[0]
    rows = sum(segments(plan, na, n // B))
    half = jax.ShapeDtypeStruct((rows // plan.cores, B), jnp.float32)
    vmem = pl.BlockSpec(memory_space=pltpu.VMEM)
    return pl.pallas_call(
        functools.partial(gram_kernel, plan, na),
        out_shape=(half, half),
        in_specs=[pl.BlockSpec(memory_space=pltpu.SMEM)] + [vmem] * (7 + len(far)),
        out_specs=(vmem,) * 2,
        scratch_shapes=[
            pltpu.VMEM((n, m), jnp.bfloat16),
            pltpu.VMEM((own.shape[0], n), jnp.float32),
            pltpu.VMEM((away, landmarks.shape[1]), jnp.bfloat16),
            pltpu.VMEM((away, B), jnp.float32),
            pltpu.VMEM((rows, B), jnp.float32),
        ]
        + [pltpu.VMEM((landmarks.shape[0], m), jnp.float32)] * (plan.lands - 1),
        compiler_params=pltpu.CompilerParams(vmem_limit_bytes=24 << 20),
        name="gram",
    )(at, embeddings, landmarks, own, u, x_upper, x_lower, x_slices, *far)


def add_cut_kernel(ways, axis, parts, at_ref, *refs):
    ins, outs = refs[: len(refs) - ways], refs[len(refs) - ways :]
    base = 0
    for rows in parts:
        h = rows // ways
        for q in range(ways):
            s = -q % ways
            at = pl.ds(pl.multiple_of(base + (at_ref[axis] ^ s) * h, 8), h) if ways > 1 else slice(base, base + h)
            total = ins[0][at, :]
            for r in ins[1:]:
                total = total + r[at, :]
            outs[q][base // ways : base // ways + h, :] = total
        base += rows


def add_cut(at, axis, ways, parts, ins):
    h = sum(parts) // ways
    vmem = pl.BlockSpec(memory_space=pltpu.VMEM)
    return pl.pallas_call(
        functools.partial(add_cut_kernel, ways, axis, parts),
        out_shape=tuple([jax.ShapeDtypeStruct((h, B), jnp.float32)] * ways),
        in_specs=[pl.BlockSpec(memory_space=pltpu.SMEM)] + [vmem] * len(ins),
        out_specs=tuple([vmem] * ways),
        compiler_params=pltpu.CompilerParams(vmem_limit_bytes=8 << 20),
        name="add_cut",
    )(at, *ins)


def place_kernel(axis, ways, parts, at_ref, *refs):
    ins, outs = refs[:ways], refs[ways:]
    base = 0
    for out, h in zip(outs, parts):
        for s in range(ways):
            out[pl.ds(pl.multiple_of((at_ref[axis] ^ s) * h, 8), h), :] = ins[s][base : base + h, :]
        base += h


def place(at, axis, parts, ins):
    vmem = pl.BlockSpec(memory_space=pltpu.VMEM)
    return pl.pallas_call(
        functools.partial(place_kernel, axis, len(ins), parts),
        out_shape=tuple(jax.ShapeDtypeStruct((h * len(ins), B), jnp.float32) for h in parts),
        in_specs=[pl.BlockSpec(memory_space=pltpu.SMEM)] + [vmem] * len(ins),
        out_specs=(vmem,) * len(parts),
        compiler_params=pltpu.CompilerParams(vmem_limit_bytes=8 << 20),
        name="place",
    )(at, *ins)


def thirds(x):
    h = x.astype(jnp.bfloat16)
    r = x - h.astype(jnp.float32)
    m = r.astype(jnp.bfloat16)
    return h, m, (r - m.astype(jnp.float32)).astype(jnp.bfloat16)

def left_terms(x, axis):
    h, m, l = thirds(x)
    return jnp.concatenate([h, h, h, m, m, l], axis)

def right_terms(x, axis):
    h, m, l = thirds(x)
    return jnp.concatenate([h, m, l, h, m, h], axis)

def dot32(a, b):
    return lax.dot_general(left_terms(a, 1), right_terms(b, 0), (((1,), (0,)), ((), ())), preferred_element_type=jnp.float32)

def dot32_t(a, b):
    return dot32(a.T, b)

def factor_block(d):
    row8 = lax.broadcasted_iota(jnp.int32, (8, B), 0)
    lane8 = lax.broadcasted_iota(jnp.int32, (8, B), 1)
    rows = [d[i : i + 8] for i in range(0, B, 8)]
    factor, inverse = [None] * (B // 8), [None] * (B // 8)
    zero = rows[0] * 0.0
    half = HALF // 8

    def spread_columns(x, lane):
        columns = [jnp.broadcast_to(x[:, lane + i : lane + i + 1], (8, B)) for i in range(8)]
        return [columns[0] + zero] + columns[1:]

    def splat(x, r):
        return jnp.broadcast_to(x[r : r + 1], (8, B))

    for start in range(0, B // 8, half):
        end = start + half
        diag = spread_columns(rows[start], 8 * start)
        for p in range(start, end):
            col = {r: spread_columns(rows[r], 8 * p) for r in range(p + 1, end)}
            after = spread_columns(rows[p + 1], 8 * p + 8) if p + 1 < end else None
            panel = (lane8 >= 8 * p) & (lane8 < 8 * p + 8)
            unit = jnp.where(lane8 == row8 + 8 * p, 1.0, 0.0)
            for r in col:
                rows[r] = jnp.where(panel, 0.0, rows[r])
            pivots = jnp.ones((8, B), jnp.float32)
            for j in range(8):
                pivot = splat(diag[j], j)
                pivots = jnp.where(row8 == j, pivot, pivots)
                inv = 1.0 / pivot
                coef = {i: splat(diag[j], i) for i in range(j + 1, 8)}
                row, unit_row = splat(rows[p], j), splat(unit, j)
                both = jnp.where(panel, unit_row, row)
                if j < 7:
                    c = jnp.where(row8 > j, diag[j] * inv, 0.0)
                    rows[p] = rows[p] - c * row
                    unit = unit - c * unit_row
                for i in coef:
                    diag[i] = diag[i] - (diag[j] * coef[i]) * inv
                for r in col:
                    c = col[r][j] * inv
                    if r == p + 1:
                        for i in range(8):
                            after[i] = after[i] - c * splat(col[r][j], i)
                    for i in coef:
                        col[r][i] = col[r][i] - c * coef[i]
                    rows[r] = rows[r] - c * both
            s = lax.rsqrt(pivots)
            factor[p] = rows[p] * s
            inverse[p] = jnp.where(panel, unit * s, jnp.where(lane8 < 8 * p, factor[p], 0.0))
            diag = after
        if end < B // 8:
            u = jnp.concatenate(factor[start:end], 0)
            w = jnp.concatenate(inverse[start:end], 0)
            lanes = lax.broadcasted_iota(jnp.int32, w.shape, 1)
            upd = lax.dot_general(
                left_terms(u, 0),
                right_terms(jnp.where(lanes < 8 * end, w, u), 0),
                (((0,), (0,)), ((), ())),
                preferred_element_type=jnp.float32,
            )
            for r in range(end, B // 8):
                rows[r] = jnp.where(lane8 < 8 * end, 0.0, rows[r]) - upd[8 * r : 8 * r + 8]
    tri = lax.broadcasted_iota(jnp.int32, (B, B), 0) <= lax.broadcasted_iota(jnp.int32, (B, B), 1)
    return jnp.where(tri, jnp.concatenate(factor, 0), 0.0), jnp.concatenate(inverse, 0)


def product(a_terms, b_terms):
    return lax.dot_general(a_terms, b_terms, (((1,), (0,)), ((), ())), preferred_element_type=jnp.float32)


def update_upper(m_ref, row, first):
    turned, terms = left_terms(row.T, 1), right_terms(row, 0)
    for i in range(row.shape[1] // B):
        at = (first + i) * B
        m_ref[at : at + B, at:] = m_ref[at : at + B, at:] - product(turned[i * B : (i + 1) * B], terms[:, i * B :])


def eliminate(nb, m_ref, store):
    for k in range(nb):
        at, on = k * B, (k + 1) * B
        u, w = factor_block(m_ref[at:on, at:on])
        row = dot32(w, m_ref[at:on, on:]) if k < nb - 1 else None
        store(k, u, w, row)
        if row is not None:
            update_upper(m_ref, row, k + 1)


def place_parts(plan, at_ref, parts, a_ref):
    h = parts[0].shape[0]
    for a in range(plan.cores):
        for t in range(plan.chips):
            slot = (at_ref[2] ^ a) * plan.chips + (at_ref[1] ^ t)
            a_ref[pl.ds(pl.multiple_of(slot * h, h), h), :] = parts[a * plan.chips + t][...]


def first_factor_kernel(plan, at_ref, *refs):
    count = plan.chips * plan.cores
    f_ref, w_ref, a_ref, m_ref = refs[count:]
    na = f_ref.shape[0] // B
    place_parts(plan, at_ref, refs[:count], a_ref)
    for j in range(na):
        m_ref[: (j + 1) * B, j * B : (j + 1) * B] = a_ref[packed_start(j) : packed_start(j) + (j + 1) * B, :]

    f_ref[...] = jnp.zeros_like(f_ref)

    def store(k, u, w, row):
        at, on = k * B, (k + 1) * B
        f_ref[at:on, at:on] = u
        w_ref[at:on, :] = w
        if row is not None:
            f_ref[at:on, on:] = row

    eliminate(na, m_ref, store)


def first_factor(at, plan, na, parts):
    vmem = pl.BlockSpec(memory_space=pltpu.VMEM)
    return pl.pallas_call(
        functools.partial(first_factor_kernel, plan),
        out_shape=(
            jax.ShapeDtypeStruct((na * B, na * B), jnp.float32),
            jax.ShapeDtypeStruct((na * B, B), jnp.float32),
        ),
        in_specs=[pl.BlockSpec(memory_space=pltpu.SMEM)] + [vmem] * len(parts),
        out_specs=(vmem,) * 2,
        scratch_shapes=[
            pltpu.VMEM((parts[0].shape[0] * len(parts), B), jnp.float32),
            pltpu.VMEM((na * B, na * B), jnp.float32),
        ],
        compiler_params=pltpu.CompilerParams(vmem_limit_bytes=16 << 20),
        name="chol_first",
    )(at, *parts)


def last_factor_kernel(plan, at_ref, f_ref, w_ref, *refs):
    count = plan.chips * plan.cores
    out_ref, o_ref, a_ref, t_ref, m_ref, sem = refs[count:]
    n, top = o_ref.shape[0] // B, f_ref.shape[0]
    na = top // B
    place_parts(plan, at_ref, refs[:count], a_ref)
    for j in range(na, n):
        start = packed_start(j) - packed_start(na)
        lanes = slice((j - na) * B, (j - na + 1) * B)
        t_ref[:, lanes] = a_ref[start : start + top, :]
        m_ref[: (j - na + 1) * B, lanes] = a_ref[start + top : start + (j + 1) * B, :]
    o_ref[:top, :top] = f_ref[...]
    o_ref[top:, :] = jnp.zeros((n * B - top, n * B), jnp.float32)
    for k in range(na):
        rows = slice(k * B, (k + 1) * B)
        row = dot32(w_ref[rows, :], t_ref[rows, :])
        o_ref[rows, top:] = row
        if k < na - 1:
            t_ref[(k + 1) * B :, :] = t_ref[(k + 1) * B :, :] - dot32_t(f_ref[rows, (k + 1) * B :], row)
        update_upper(m_ref, row, 0)

    head = pltpu.make_async_copy(o_ref.at[pl.ds(0, top), :], out_ref.at[pl.ds(0, top), :], sem.at[n - na])
    head.start()

    copies = [head]

    def store(k, u, w, row):
        at, on = top + k * B, top + (k + 1) * B
        o_ref[at:on, at:on] = u
        if row is not None:
            o_ref[at:on, on:] = row
        copies.append(pltpu.make_async_copy(o_ref.at[pl.ds(at, B), :], out_ref.at[pl.ds(at, B), :], sem.at[k]))
        copies[-1].start()

    eliminate(n - na, m_ref, store)
    for copy in copies:
        copy.wait()


def last_factor(at, plan, n, f, w, parts):
    vmem = pl.BlockSpec(memory_space=pltpu.VMEM)
    top = f.shape[0]
    return pl.pallas_call(
        functools.partial(last_factor_kernel, plan),
        out_shape=jax.ShapeDtypeStruct((n, n), jnp.float32),
        in_specs=[pl.BlockSpec(memory_space=pltpu.SMEM)] + [vmem] * (2 + len(parts)),
        out_specs=pl.BlockSpec(memory_space=pl.ANY),
        scratch_shapes=[
            pltpu.VMEM((n, n), jnp.float32),
            pltpu.VMEM((parts[0].shape[0] * len(parts), B), jnp.float32),
            pltpu.VMEM((top, n - top), jnp.float32),
            pltpu.VMEM((n - top, n - top), jnp.float32),
            pltpu.SemaphoreType.DMA(((n - top) // B + 1,)),
        ],
        compiler_params=pltpu.CompilerParams(vmem_limit_bytes=24 << 20),
        name="chol_last",
    )(at, f, w, *parts)


def swap(x, axis, s):
    return lax.ppermute(x, axis, [(i, i ^ s) for i in range(lax.axis_size(axis))])


def scatter(pieces, axis):
    return [pieces[0]] + [swap(p, axis, -q % len(pieces)) for q, p in enumerate(pieces) if q]


def spread_out(x, axis):
    return [x] + [swap(x, axis, s) for s in range(1, lax.axis_size(axis))]


def shards(embeddings, landmarks):
    lands, chips, cores = (lax.axis_size(a) for a in ("land", "chip", "core"))
    land, chip, core = (lax.axis_index(a) for a in ("land", "chip", "core"))
    at = jnp.stack([land, chip, core]).astype(jnp.int32)
    shard = landmarks.shape[0]
    n = shard * lands
    plan = Plan(lands, chips, cores, shard // (chips * cores) % 16 == 0, embeddings.shape[0] * lands * chips * cores)

    share = shard // (chips * cores)
    own = lax.dynamic_slice_in_dim(landmarks, (chip * cores + core) * share, share, 0)
    if plan.split:
        piece = own
    else:
        piece = lax.dynamic_slice_in_dim(landmarks, chip * (shard // chips), shard // chips, 0)
    x_upper, u = own_cross(landmarks[: shard // 2], embeddings)
    z, x_upper, u = lax.optimization_barrier((spread_out(piece, "land")[1:], x_upper, u))
    slices = jnp.concatenate(z, 0)
    far = spread_out(slices, "chip")
    x_lower, x_slices = next_cross(landmarks[shard // 2 :], slices, embeddings, u)
    far, x_lower, x_slices = lax.optimization_barrier((far, x_lower, x_slices))
    if plan.split:
        for a in range(1, cores):
            far = far + [swap(f, "core", a) for f in far[:chips]]

    na = max(1, n // B * 3 // 8)
    keep, send = local_normal(at, plan, na, embeddings, landmarks, own, u, x_upper, x_lower, x_slices, far)
    rows = [r // cores for r in segments(plan, na, n // B)]
    parts = scatter(add_cut(at, 1, chips, rows, [keep, swap(send, "core", 1)]), "chip")
    rows = [r // chips for r in rows]
    parts = scatter(add_cut(at, 0, lands, rows, parts), "land")
    rows = [r // lands for r in rows]
    (whole,) = add_cut(at, 0, 1, rows, parts)
    first, last = place(at, 0, rows, spread_out(whole, "land"))
    first = spread_out(first, "chip")
    first, last = lax.optimization_barrier((first + [swap(p, "core", 1) for p in first], last))
    f, w = first_factor(at, plan, na, first)
    last, f, w = lax.optimization_barrier((spread_out(last, "chip"), f, w))
    last = last + [swap(p, "core", 1) for p in last]
    return last_factor(at, plan, n, f, w, last)


def solution(mesh):
    land, rows = mesh.axis_names
    cores = 2
    fine = Mesh(mesh.devices.reshape(mesh.shape[land], mesh.shape[rows] // cores, cores), ("land", "chip", "core"))
    in_specs = (P(("land", "chip", "core"), None), P("land", None))
    return jax.shard_map(shards, mesh=fine, in_specs=in_specs, out_specs=P(), check_vma=False)
```
